128 devices in a mesh: gx: 4 (over z), gy: 8 (over y_lo, x), gz: 4 (over y_hi, core).
Axes of the slice: x: 4, y: 4 (y_hi: 2, y_lo: 2; y = y_hi * 2 + y_lo), z: 4, core: 2. Of those that a mesh axis runs over, the one named last changes fastest.
Arguments:
- images: float32 [2, 64, 256, 512], P(None, 'gx', 'gy', 'gz'), may hold values from -6 to 6
- velocity: float32 [2, 3, 8, 32, 64], P(None, None, 'gx', None, 'gz'), may hold values from -2 to 2
Outputs:
- new_velocity: float32 [2, 3, 8, 32, 64], P(None, None, 'gx', None, 'gz')
- velocity_field: bfloat16 [2, 3, 64, 256, 512], P(None, None, 'gx', 'gy', 'gz')
The draws below stay inside these ranges and needn't reach their ends.
All inputs are finite; a program needn't handle non-finite values.
Results may differ from the reference program's by a relative error of at most 0.001.
Values sent between devices are 32-bit elements; how exact they have to be, the bound alone decides.
No kernel may reach another device: no remote copies, remote signals or barrier semaphores. Data moves between devices by JAX's collectives and lax.ppermute only.
A program may use at most 64 MiB of HBM per device.

```python
import jax
import jax.numpy as jnp
from jax import lax

NX = 64
NY = 256
NZ = 512
LX = 8
LY = 32
LZ = 64


def block_scale(own_key, dims, shards, low, high):
    def one(position, parts):
        draws = jax.random.uniform(jax.random.fold_in(jax.random.fold_in(own_key, 6), position), (parts,), jnp.float32, low / len(shards), high / len(shards))
        return jnp.repeat(jnp.exp(draws), dims[position] // parts).reshape((-1,) + (1,) * (len(dims) - position - 1))

    factor_of = one(*shards[0])
    for cut in shards[1:]:
        factor_of = factor_of * one(*cut)
    return factor_of


def scatter_about(rng, shape, width, bound, shards=(), held_as=jnp.bfloat16):
    drawn = jax.random.normal(rng, shape, jnp.float32) * width
    if len(shards) > 0:
        drawn = block_scale(rng, shape, shards, -0.22, 0.18) * drawn
    return jnp.clip(drawn, min=-bound, max=bound).astype(held_as)


def setup_inputs(seed: int = 0) -> dict:
    key_of = jax.random.split(jax.random.key(seed), 3)
    images = scatter_about(key_of[0], (2, NX, NY, NZ), 1.0, 6.0, ((1, 4), (2, 8), (3, 4)), jnp.float32)
    velocity = scatter_about(key_of[1], (2, 3, LX, LY, LZ), 0.3, 2.0, ((2, 4), (4, 4)), jnp.float32)
    return {"images": images, "velocity": velocity}


epsilon_value = 1e-5
step_size = 0.5


def spline_weight(offset):
    magnitude = jnp.abs(offset)
    interior = 2.0 / 3.0 - magnitude * magnitude + 0.5 * magnitude * magnitude * magnitude
    outside = jnp.maximum(2.0 - magnitude, 0.0)
    outside = outside * outside * outside / 6.0
    return jnp.where(magnitude < 1.0, interior, outside)


def spline_table(voxels, points, first_point):
    positions = jnp.arange(voxels, dtype=jnp.float32)[:, None]
    centres = 8.0 * (jnp.arange(points, dtype=jnp.float32)[None, :] + first_point) + 3.5
    return spline_weight((positions - centres) / 8.0)


def window_sum(values, which_axis, keep_count):
    running = lax.slice_in_dim(values, 0, keep_count, axis=which_axis)
    for offset in range(1, 9):
        running = running + lax.slice_in_dim(values, offset, offset + keep_count, axis=which_axis)
    return running


def gradient(volume, count_x, count_y, count_z):
    along_x = volume[5:5 + count_x, 4:4 + count_y, 4:4 + count_z] - volume[3:3 + count_x, 4:4 + count_y, 4:4 + count_z]
    along_y = volume[4:4 + count_x, 5:5 + count_y, 4:4 + count_z] - volume[4:4 + count_x, 3:3 + count_y, 4:4 + count_z]
    along_z = volume[4:4 + count_x, 4:4 + count_y, 5:5 + count_z] - volume[4:4 + count_x, 4:4 + count_y, 3:3 + count_z]
    return 0.5 * jnp.stack([along_x, along_y, along_z])


def local_forces(padded):
    count_x = padded.shape[1] - 8
    count_y = padded.shape[2] - 8
    count_z = padded.shape[3] - 8
    fixed_side = padded[0]
    moving_side = padded[1]
    products = jnp.stack([fixed_side, moving_side, fixed_side * fixed_side, moving_side * moving_side, fixed_side * moving_side])
    window_sums = window_sum(window_sum(window_sum(products, 1, count_x), 2, count_y), 3, count_z)
    averages = window_sums / 729.0
    mean_fixed = averages[0]
    mean_moving = averages[1]
    var_fixed = averages[2] - mean_fixed * mean_fixed + epsilon_value
    var_moving = averages[3] - mean_moving * mean_moving + epsilon_value
    covariance = averages[4] - mean_fixed * mean_moving
    centre_fixed = fixed_side[4:4 + count_x, 4:4 + count_y, 4:4 + count_z] - mean_fixed
    centre_moving = moving_side[4:4 + count_x, 4:4 + count_y, 4:4 + count_z] - mean_moving
    factor = 2.0 * covariance / (var_fixed * var_moving)
    pull_fixed = factor * (centre_moving - covariance / var_fixed * centre_fixed)
    pull_moving = factor * (centre_fixed - covariance / var_moving * centre_moving)
    return jnp.stack([pull_fixed[None] * gradient(fixed_side, count_x, count_y, count_z),
                      pull_moving[None] * gradient(moving_side, count_x, count_y, count_z)])


def reference(images, velocity):
    highest = lax.Precision.HIGHEST
    padded = jnp.pad(images, ((0, 0), (4, 4), (4, 4), (4, 4)))
    table_x = spline_table(NX, LX, 0.0)
    table_y = spline_table(NY, LY, 0.0)
    table_z = spline_table(NZ, LZ, 0.0)
    slab_count = NX // 8
    slab_ids = jnp.arange(slab_count, dtype=jnp.int32)

    def project_slab(slab_index):
        slab_rows = lax.dynamic_slice_in_dim(padded, slab_index * 8, 16, 1)
        pushes = local_forces(slab_rows)
        along_z = jnp.einsum('hcxyz,zk->hcxyk', pushes, table_z, precision=highest)
        return jnp.einsum('hcxyk,yj->hcxjk', along_z, table_y, precision=highest)

    partial_value = lax.map(project_slab, slab_ids)
    partial_value = jnp.moveaxis(partial_value, 0, 2).reshape(2, 3, NX, LY, LZ)
    descent = jnp.einsum('hcxjk,xi->hcijk', partial_value, table_x, precision=highest)
    new_velocity = velocity + step_size * descent

    def evaluate_slab(slab_index):
        table_rows = lax.dynamic_slice_in_dim(table_x, slab_index * 8, 8, 0)
        along_x = jnp.einsum('hcijk,xi->hcxjk', new_velocity, table_rows, precision=highest)
        along_y = jnp.einsum('hcxjk,yj->hcxyk', along_x, table_y, precision=highest)
        return jnp.einsum('hcxyk,zk->hcxyz', along_y, table_z, precision=highest).astype(jnp.bfloat16)

    field_slabs = lax.map(evaluate_slab, slab_ids)
    velocity_field = jnp.moveaxis(field_slabs, 0, 2).reshape(2, 3, NX, NY, NZ)
    return new_velocity, velocity_field
```

```python
import functools

import jax
import jax.numpy as jnp
import numpy as np
from jax import lax
from jax.experimental import pallas as pl
from jax.experimental.pallas import tpu as pltpu
from jax.sharding import PartitionSpec as P

epsilon_value = 1e-05
step_size = 0.5
f32 = jnp.float32
bf16 = jnp.bfloat16


def spline(t):
    m = np.abs(t)
    inside = 2.0 / 3.0 - m * m + 0.5 * m * m * m
    out = np.maximum(2.0 - m, 0.0)
    return np.where(m < 1.0, inside, out * out * out / 6.0)


def split_two(w):
    hi = w.astype(np.float32).astype(jnp.bfloat16)
    lo = (w - hi.astype(np.float64)).astype(np.float32).astype(jnp.bfloat16)
    return hi, lo


def seam_table(size, points, fold_from):
    idx = np.arange(size)
    pos = np.where(idx >= fold_from, idx - size, idx) if fold_from else idx - 4
    pts = np.arange(points) - 2
    w = spline((pos[None, :] - 8.0 * pts[:, None] - 3.5) / 8.0)
    same = (pos[None, :] < 0) == (pts[:, None] < 0)
    return w, w * same


def projection_tables(nx, ny, nz):
    bx, by, bz = nx // 8, ny // 8, nz // 8
    return bx, by, bz


def pack_kernel(img_ref, out_ref):
    lane = lax.broadcasted_iota(jnp.int32, (32, 128), 1)
    for h in range(2):
        acc = jnp.zeros((32, 128), f32)
        for t in range(16):
            moved = pltpu.roll(img_ref[h, t], (8 * t + 8) % 128, 1)
            acc = jnp.where((lane >= 8 * t) & (lane < 8 * t + 8), moved, acc)
        out_ref[h] = acc


def split3(v):
    hi = v.astype(bf16)
    r = v - hi.astype(f32)
    mid = r.astype(bf16)
    lo = (r - mid.astype(f32)).astype(bf16)
    return hi, mid, lo


def split2(v):
    hi = v.astype(bf16)
    return hi, (v - hi.astype(f32)).astype(bf16)


def dot(a, b):
    return jnp.dot(a, b, preferred_element_type=f32)


def up_by(v, n, row):
    size = v.shape[0]
    return jnp.where(row < size - n, pltpu.roll(v, size - n, 0), 0.0)


def rows_window(v, head, tail, row8, row40):
    first = v[0:8]
    own = jnp.concatenate([jnp.zeros((8, 128), f32), v[8:40]], axis=0)
    s = first + up_by(first, 1, row8)
    s = s + up_by(s, 2, row8)
    s = s + up_by(s, 4, row8)
    w = own + pltpu.roll(own, 39, 0)
    w = w + pltpu.roll(w, 38, 0)
    w = w + pltpu.roll(w, 36, 0)
    w = w[0:32] + own[8:40]
    top = head * s + tail * w[0:8]
    return jnp.concatenate([top, w[8:32]], axis=0)


def force_kernel(
    edge_ref,
    own_ref,
    zr_ref,
    xr_ref,
    yr_ref,
    xyr_ref,
    vel_ref,
    wxy_ref,
    wz_ref,
    out_ref,
    a_ref,
    h_ref,
    v_ref,
    dz_ref,
    xs_ref,
    hs_ref,
    fh_ref,
    fl_ref,
):
    ex = edge_ref[0]
    ey = edge_ref[1]
    ez = edge_ref[2]
    lane8 = lax.broadcasted_iota(jnp.int32, (8, 128), 1)
    row8 = lax.broadcasted_iota(jnp.int32, (8, 128), 0)
    lane32 = lax.broadcasted_iota(jnp.int32, (32, 128), 1)
    row32 = lax.broadcasted_iota(jnp.int32, (32, 128), 0)
    lane40 = lax.broadcasted_iota(jnp.int32, (40, 128), 1)
    row40 = lax.broadcasted_iota(jnp.int32, (40, 128), 0)
    head = jnp.where(row8 < 4, 1.0, ey)
    tail = jnp.where(row8 < 4, ey, 1.0)

    for h in range(2):
        for t in range(16):
            a_ref[h, 8 + t, 8:40] = own_ref[h, t]
            a_ref[h, 8 + t, 0:8] = yr_ref[h, t]
        for t in range(8):
            a_ref[h, t, 8:40] = xr_ref[h, t]
            a_ref[h, t, 0:8] = xyr_ref[h, t]
        h_ref[h, 0, 8:40] = zr_ref[h]
        h_ref[h, 0, 0:8] = yr_ref[h, 16]
        h_ref[h, 1, 8:40] = xr_ref[h, 8]
        h_ref[h, 1, 0:8] = xyr_ref[h, 8]

    plus_z = jnp.where(lane40 == 127, ez, 1.0)
    minus_z = jnp.where(lane40 == 0, ez, 1.0)
    for h in range(2):
        for l in range(3, 21):
            a = a_ref[h, l]
            if l >= 8:
                halo = pltpu.roll(h_ref[h, 0], (120 - 8 * (l - 8)) % 128, 1)
            else:
                halo = pltpu.roll(h_ref[h, 1], (120 - 8 * (l + 8)) % 128, 1)
            v_ref[h, l - 3] = jnp.where(lane40 >= 124, halo, a)
            if 4 <= l < 20:
                up = pltpu.roll(jnp.where(lane40 >= 125, halo, a), 127, 1)
                down = pltpu.roll(jnp.where(lane40 >= 123, halo, a), 1, 1)
                dz_ref[h, l - 4] = plus_z * up - minus_z * down

    def products(f, m):
        return (f, m, f * f, m * m, f * m)

    def x_step(tile, carry):
        rows = pl.ds(pl.multiple_of(tile * 8, 8), 8)
        for q in range(5):
            p = []
            for l in range(24):
                if q == 0:
                    p.append(a_ref[0, l, rows])
                elif q == 1:
                    p.append(a_ref[1, l, rows])
                elif q == 2:
                    f = a_ref[0, l, rows]
                    p.append(f * f)
                elif q == 3:
                    m = a_ref[1, l, rows]
                    p.append(m * m)
                else:
                    p.append(a_ref[0, l, rows] * a_ref[1, l, rows])
            left = [None] * 8
            left[7] = p[7]
            for o in range(6, -1, -1):
                left[o] = left[o + 1] + p[o]
            right = [None] * 8
            right[0] = p[8]
            for o in range(1, 8):
                right[o] = right[o - 1] + p[o + 8]
            for o in range(8):
                xs_ref[q, o, rows] = left[o] + ex * right[o] if o < 4 else ex * left[o] + right[o]
            s = p[8:24]
            b = [s[n] + s[n + 1] for n in range(15)]
            b = [b[n] + b[n + 2] for n in range(13)]
            b = [b[n] + b[n + 4] for n in range(9)]
            for o in range(8):
                xs_ref[q, 8 + o, rows] = b[o] + s[o + 8]
        return carry

    lax.fori_loop(0, 5, x_step, 0)

    src = lax.broadcasted_iota(jnp.int32, (256, 128), 0)
    dst = lax.broadcasted_iota(jnp.int32, (256, 128), 1)
    plane = jnp.where(src < 128, lax.shift_right_logical(src, 3) + 8, lax.shift_right_logical(src - 128, 3) - 8)
    goal = lax.shift_right_logical(dst, 3)
    near = (plane >= goal) & (plane <= goal + 8) & ((src & 7) == (dst & 7)) & (plane >= 0)
    across = (plane < 8) != (goal < 4)
    x_sum = jnp.where(near, jnp.where(across, ex, 1.0), 0.0).astype(bf16)
    for q in range(5):
        parts = []
        for side in range(2):
            f = h_ref[0, side]
            m = h_ref[1, side]
            parts.append(rows_window(products(f, m)[q], head, tail, row8, row40))
        both = jnp.concatenate(parts, axis=1)
        total = jnp.zeros((32, 128), f32)
        for piece in split3(both):
            total = total + dot(piece, x_sum)
        for n, piece in enumerate(split3(total)):
            hs_ref[q, n] = piece

    centre = jnp.where(dst < 124, dst, dst - 128)
    below = src >= 128
    place = jnp.where(below, (src & 7) - 8, src)
    gap = place - centre
    inside = (gap <= 4) & (gap >= -4)
    crossing = below != (dst >= 124)
    z_sum = jnp.where(inside, jnp.where(crossing, ez, 1.0), 0.0).astype(bf16)

    plus_y = jnp.where(row32 == 3, ey, 1.0)
    minus_y = jnp.where(row32 == 4, ey, 1.0)
    group = lax.shift_right_logical(lane32, 3)

    def o_step(o, carry):
        pieces = [[], [], []]
        mine = group == o
        for q in range(5):
            y = rows_window(xs_ref[q, o], head, tail, row8, row40)
            for n, piece in enumerate(split3(y)):
                halo = jnp.where(mine, hs_ref[q, n].astype(f32), 0.0).astype(bf16)
                pieces[n].append(jnp.concatenate([piece, halo], axis=1))
        sums = dot(jnp.concatenate(pieces[0], axis=0), z_sum)
        sums = sums + dot(jnp.concatenate(pieces[1], axis=0), z_sum)
        sums = sums + dot(jnp.concatenate(pieces[2], axis=0), z_sum)
        sums = sums * (1.0 / 729.0)
        mean_f = sums[0:32]
        mean_m = sums[32:64]
        var_f = sums[64:96] - mean_f * mean_f + epsilon_value
        var_m = sums[96:128] - mean_m * mean_m + epsilon_value
        cov = sums[128:160] - mean_f * mean_m
        off_f = v_ref[0, o + 1, 4:36] - mean_f
        off_m = v_ref[1, o + 1, 4:36] - mean_m
        inv = 1.0 / (var_f * var_m)
        factor = cov * inv
        pulls = (
            factor * (off_m - factor * var_m * off_f),
            factor * (off_f - factor * var_f * off_m),
        )
        plus_x = jnp.where(o == 3, ex, 1.0)
        minus_x = jnp.where(o == 4, ex, 1.0)
        where_to = pl.ds(pl.multiple_of(o * 32, 32), 32)
        for h in range(2):
            dx = plus_x * v_ref[h, o + 2, 4:36] - minus_x * v_ref[h, o, 4:36]
            dy = plus_y * v_ref[h, o + 1, 5:37] - minus_y * v_ref[h, o + 1, 3:35]
            dz = dz_ref[h, o, 4:36]
            for c, d in enumerate((dx, dy, dz)):
                hi, lo = split2(pulls[h] * d)
                fh_ref[3 * h + c, where_to] = hi
                fl_ref[3 * h + c, where_to] = lo
        return carry

    lax.fori_loop(0, 16, o_step, 0)

    total = jnp.zeros((40, 128), f32)
    for c in range(6):
        first = dot(wxy_ref[...], fh_ref[c])
        second = dot(wxy_ref[0:40], fl_ref[c])
        xy = first[0:40] + first[40:80] + second
        hi, lo = split2(xy)
        total = total + dot(hi, wz_ref[0, c]) + dot(hi, wz_ref[1, c]) + dot(lo, wz_ref[0, c])
    total = step_size * total
    out_ref[0:16] = total[0:16]
    out_ref[16:32] = total[16:32] + vel_ref[...]
    out_ref[32:40] = total[32:40]


def fold_kernel(mine_ref, low_ref, high_ref, out_ref):
    lane = lax.broadcasted_iota(jnp.int32, (40, 128), 1)
    spot = lax.rem(lane, 20)
    live = lane < 120
    low = pltpu.roll(low_ref[...], 112, 1)
    high = pltpu.roll(high_ref[...], 16, 1)
    total = mine_ref[...]
    total = total + jnp.where(live & (spot < 3), low, 0.0)
    total = total + jnp.where(live & (spot >= 16), high, 0.0)
    for n in range(32):
        out_ref[n] = total


def field_kernel(at_ref, g_ref, wxy_ref, wz_ref, nv_ref, field_ref, rows_ref):
    me_i = at_ref[0]
    me_j = at_ref[1]
    row8 = lax.broadcasted_iota(jnp.int32, (8, 128), 0)
    slot = [lax.rem(me_i + d, 4) * 8 for d in range(4)]

    def piece(d, j, p):
        return g_ref[slot[d] + j, 8 * p : 8 * p + 8]

    for side in range(2):
        cols = []
        for j in range(8):
            if side == 0:
                cols.append(piece(0, j, 2) + piece(3, j, 4) + piece(1, j, 0))
            else:
                cols.append(piece(0, j, 3) + piece(1, j, 1))
        turned = [pltpu.roll(c, 4, 0) for c in cols]
        tiles = []
        for n in range(5):
            zero = jnp.zeros((8, 128), f32)
            even = cols[2 * n] if n < 4 else zero
            high = turned[2 * n + 1] if n < 4 else zero
            low = turned[2 * n - 1] if n > 0 else zero
            tiles.append(even + jnp.where(row8 < 4, low, high))
        tiles[4] = tiles[4] + tiles[0]
        for n in range(5):
            rows_ref[8 * n : 8 * n + 8] = tiles[n]
        block = rows_ref[2:34]
        for c in range(6):
            nv_ref[c, side] = block[:, 20 * c + 2 : 20 * c + 18]

    window = []
    js = [lax.rem(me_j + 7, 8), me_j, lax.rem(me_j + 1, 8)]
    for w in range(6):
        sums = []
        for j in js:
            terms = []
            if w <= 4:
                terms.append(piece(0, j, w))
            if w <= 2:
                terms.append(piece(3, j, w + 2))
            if w >= 2:
                terms.append(piece(1, j, w - 2))
            if w == 0:
                terms.append(piece(2, j, 4))
            if w >= 4:
                terms.append(piece(2, j, w - 4))
            total = terms[0]
            for t in terms[1:]:
                total = total + t
            sums.append(total)
        before = pltpu.roll(sums[0], 4, 0)
        after = pltpu.roll(sums[2], 4, 0)
        window.append(sums[1] + jnp.where(row8 < 4, before, after))
    coefs = jnp.concatenate(window, axis=0)
    hi, lo = split2(coefs)
    for c in range(6):
        along = dot(hi, wz_ref[0, c]) + dot(hi, wz_ref[1, c]) + dot(lo, wz_ref[0, c])
        ch, cl = split2(along)
        rhs = jnp.concatenate([ch, cl, ch], axis=0)
        field_ref[c] = dot(wxy_ref[...], rhs).astype(bf16)


VMEM = pl.BlockSpec(memory_space=pltpu.VMEM)
SMEM = pl.BlockSpec(memory_space=pltpu.SMEM)


def call(body, out_shape, in_specs, scratch=(), flops=0, bytes_accessed=0):
    many = isinstance(out_shape, (list, tuple))
    return pl.pallas_call(
        body,
        out_shape=out_shape,
        in_specs=in_specs,
        out_specs=[VMEM] * len(out_shape) if many else VMEM,
        scratch_shapes=list(scratch),
        compiler_params=pltpu.CompilerParams(vmem_limit_bytes=48 << 20),
        cost_estimate=pl.CostEstimate(flops=flops, bytes_accessed=bytes_accessed, transcendentals=0),
    )


def pairs(mesh_sizes, di, dj, dk):
    ni, nj, nk = mesh_sizes
    out = []
    for i in range(ni):
        for j in range(nj):
            for k in range(nk):
                to = (((i + di) % ni) * nj + (j + dj) % nj) * nk + (k + dk) % nk
                out.append(((i * nj + j) * nk + k, to))
    return out


def at_edge(table, first, edge, is_first):
    return jnp.where(is_first, first, table) * edge


def shards(images, velocity):
    axes = ("gx", "gy", "gz")
    sizes = tuple(lax.axis_size(a) for a in axes)
    i, j, k = (lax.axis_index(a) for a in axes)
    ni, nj, nk = sizes

    def send(v, di, dj, dk):
        return lax.ppermute(v, axes, pairs(sizes, di, dj, dk))

    pack = call(pack_kernel, jax.ShapeDtypeStruct((2, 32, 128), f32), [VMEM])(images)
    zr = lax.ppermute(pack, "gz", [(n, (n + 1) % nk) for n in range(nk)])
    to_x = jnp.concatenate([images[:, 8:], zr[:, None]], axis=1)
    to_y = jnp.concatenate([images[:, :, 24:], zr[:, None, 24:]], axis=1)
    to_xy = jnp.concatenate([images[:, 8:, 24:], zr[:, None, 24:]], axis=1)
    xr = send(to_x, 1, 0, 0)
    yr = send(to_y, 0, 1, 0)
    xyr = send(to_xy, 1, 1, 0)

    def parts(size, points, fold_from, at, count):
        plain, first = seam_table(size, points, fold_from)
        keep = np.ones((points, 1))
        keep[-1] = 0.0
        return plain, first, keep

    wx, wx0, kx = parts(16, 5, 0, i, ni)
    wy, wy0, ky = parts(32, 7, 0, j, nj)
    pad = lambda t: np.concatenate([t, np.zeros((1,) + t.shape[1:])], axis=0)
    wy, wy0, ky = pad(wy), pad(wy0), pad(ky)
    ky[7] = 1.0
    flat = (np.einsum("po,qr->pqor", wx, wy)).reshape(40, 512)
    hi, lo = split_two(flat)
    side_x = np.broadcast_to(((wx0 != 0) | (wx == 0))[:, None, :, None], (5, 8, 16, 32)).reshape(40, 512)
    side_y = np.broadcast_to(((wy0 != 0) | (wy == 0))[None, :, None, :], (5, 8, 16, 32)).reshape(40, 512)
    last_x = np.broadcast_to(kx[:, None], (5, 8, 1)).reshape(40, 1)
    last_y = np.broadcast_to(ky[None], (5, 8, 1)).reshape(40, 1)
    mask = (
        jnp.where(i == 0, side_x.astype(jnp.bfloat16), bf16(1))
        * jnp.where(j == 0, side_y.astype(jnp.bfloat16), bf16(1))
        * jnp.where(i == ni - 1, last_x.astype(jnp.bfloat16), bf16(1))
        * jnp.where(j == nj - 1, last_y.astype(jnp.bfloat16), bf16(1))
    )
    wxy = jnp.concatenate([hi * mask, lo * mask], axis=0)
    wz, wz0, kz = parts(128, 19, 124, k, nk)
    canvas = np.zeros((3, 6, 128, 128))
    for c in range(6):
        canvas[0, c, :, 20 * c : 20 * c + 19] = wz.T
        canvas[1, c, :, 20 * c : 20 * c + 19] = (wz0 != 0).T | (wz == 0).T
        canvas[2, c, :, 20 * c : 20 * c + 19] = kz.T
    zhi, zlo = split_two(canvas[0])
    zmask = jnp.where(k == 0, canvas[1].astype(jnp.bfloat16), bf16(1)) * jnp.where(
        k == nk - 1, canvas[2].astype(jnp.bfloat16), bf16(1)
    )
    wzs = jnp.stack([zhi * zmask, zlo * zmask])

    rows = lax.dynamic_slice_in_dim(velocity, j * 4, 4, 3)
    vel = jnp.transpose(rows, (2, 3, 0, 1, 4)).reshape(2, 4, 6, 16)
    vel = jnp.pad(vel, ((0, 0), (2, 2), (0, 0), (2, 2))).reshape(16, 120)
    vel = jnp.pad(vel, ((0, 0), (0, 8)))

    edges = jnp.stack([i != 0, j != 0, k != 0]).astype(f32)
    part = call(
        force_kernel,
        jax.ShapeDtypeStruct((40, 128), f32),
        [SMEM] + [VMEM] * 8,
        [
            pltpu.VMEM((2, 24, 40, 128), f32),
            pltpu.VMEM((2, 2, 40, 128), f32),
            pltpu.VMEM((2, 18, 40, 128), f32),
            pltpu.VMEM((2, 16, 40, 128), f32),
            pltpu.VMEM((5, 16, 40, 128), f32),
            pltpu.VMEM((5, 3, 32, 128), bf16),
            pltpu.VMEM((6, 512, 128), bf16),
            pltpu.VMEM((6, 512, 128), bf16),
        ],
        flops=10**9,
        bytes_accessed=2 * 10**6,
    )(edges, images, zr, xr, yr, xyr, vel, wxy, wzs)

    low = lax.ppermute(part, "gz", [(n, (n + 1) % nk) for n in range(nk)])
    high = lax.ppermute(part, "gz", [((n + 1) % nk, n) for n in range(nk)])
    copies = call(fold_kernel, jax.ShapeDtypeStruct((32, 40, 128), f32), [VMEM] * 3)(part, low, high)
    everything = lax.all_to_all(copies, ("gx", "gy"), 0, 0, tiled=True)

    pos = lambda n: np.arange(n)[:, None]
    ex = spline((pos(16) - 8.0 * (np.arange(6)[None] - 2) - 3.5) / 8.0)
    ey = spline((pos(32) - 8.0 * (np.arange(8)[None] - 2) - 3.5) / 8.0)
    ez = spline((pos(128) - 8.0 * (np.arange(20)[None] - 2) - 3.5) / 8.0)
    ehi, elo = split_two(np.einsum("xp,yq->xypq", ex, ey).reshape(512, 48))
    pt_x = 2 * i - 2 + np.arange(48) // 8
    pt_y = 4 * j - 2 + np.arange(48) % 8
    real = ((pt_x >= 0) & (pt_x < 2 * ni) & (pt_y >= 0) & (pt_y < 4 * nj)).astype(bf16)[None]
    exy = jnp.concatenate([ehi * real, ehi * real, elo * real], axis=1)
    zc = np.zeros((6, 128, 128))
    for c in range(6):
        zc[c, 20 * c : 20 * c + 20] = ez.T
    chi, clo = split_two(zc)
    pt_z = 16 * k - 2 + np.arange(128) % 20
    zreal = ((pt_z >= 0) & (pt_z < 16 * nk)).astype(bf16)[:, None]
    ezs = jnp.stack([chi * zreal, clo * zreal])
    at = jnp.stack([i, j]).astype(jnp.int32)
    nv, field = call(
        field_kernel,
        [jax.ShapeDtypeStruct((6, 2, 32, 16), f32), jax.ShapeDtypeStruct((6, 512, 128), bf16)],
        [SMEM] + [VMEM] * 3,
        [pltpu.VMEM((40, 128), f32)],
        flops=10**8,
        bytes_accessed=10**6,
    )(at, everything, exy, ezs)
    return nv.reshape(2, 3, 2, 32, 16), field.reshape(2, 3, 16, 32, 128)


def solution(mesh):
    placed = (P(None, "gx", "gy", "gz"), P(None, None, "gx", None, "gz"))
    return jax.shard_map(
        shards,
        mesh=mesh,
        in_specs=placed,
        out_specs=(P(None, None, "gx", None, "gz"), P(None, None, "gx", "gy", "gz")),
        check_vma=False,
    )
```

```python
import jax
import jax.numpy as jnp
import numpy as np
from jax import lax
from jax.experimental import pallas as pl
from jax.experimental.pallas import tpu as pltpu
from jax.sharding import PartitionSpec as P

epsilon_value = 1e-05
step_size = 0.5
f32 = jnp.float32
bf16 = jnp.bfloat16


def spline(t):
    m = np.abs(t)
    inside = 2.0 / 3.0 - m * m + 0.5 * m * m * m
    out = np.maximum(2.0 - m, 0.0)
    return np.where(m < 1.0, inside, out * out * out / 6.0)


def split_two(w):
    hi = w.astype(np.float32).astype(jnp.bfloat16)
    lo = (w - hi.astype(np.float64)).astype(np.float32).astype(jnp.bfloat16)
    return hi, lo


def pack_kernel(img_ref, out_ref, x_ref, y_ref, xy_ref, buf_ref, sems):
    lane = lax.broadcasted_iota(jnp.int32, (32, 128), 1)
    copies = []
    for n in range(4):
        for h in range(2):
            planes = pl.ds(4 * n, 4)
            copy = pltpu.make_async_copy(img_ref.at[h, planes], buf_ref.at[h, planes], sems.at[2 * n + h])
            copy.start()
            copies.append(copy)
    packed = [jnp.zeros((32, 128), f32) for _ in range(2)]
    for n in range(4):
        for h in range(2):
            copies[2 * n + h].wait()
            for t in range(4 * n, 4 * n + 4):
                moved = pltpu.roll(buf_ref[h, t], (8 * t + 8) % 128, 1)
                packed[h] = jnp.where((lane >= 8 * t) & (lane < 8 * t + 8), moved, packed[h])
                y_ref[h, t] = buf_ref[h, t, 24:32]
                if t >= 8:
                    x_ref[h, t - 8] = buf_ref[h, t]
                    xy_ref[h, t - 8] = buf_ref[h, t, 24:32]
    for h in range(2):
        out_ref[h] = packed[h]
        y_ref[h, 16] = jnp.zeros((8, 128), f32)
        xy_ref[h, 8] = jnp.zeros((8, 128), f32)


def prep_kernel(at_ref, vel_ref, wxy_ref, wz_ref, vel_out, wxy_out, wz_out, xsum_out, zsum_out, rows_ref):
    i = at_ref[0]
    j = at_ref[1]
    k = at_ref[2]
    ex = jnp.where(i == 0, 0.0, 1.0)
    ez = jnp.where(k == 0, 0.0, 1.0)
    row = lax.broadcasted_iota(jnp.int32, (40, 512), 0)
    col = lax.broadcasted_iota(jnp.int32, (40, 512), 1)
    p = lax.shift_right_logical(row, 3)
    q = row & 7
    o = lax.shift_right_logical(col, 5)
    r = col & 31
    ok = ((p < 2) == (o < 4)) | (i != 0)
    ok = ok & (((q < 2) == (r < 4)) | (j != 0))
    ok = ok & ((p < 4) | (i != at_ref[3] - 1)) & ((q < 6) | (j != at_ref[4] - 1))
    keep = jnp.where(ok, 1.0, 0.0)
    for n in range(2):
        rows = pl.ds(40 * n, 40)
        wxy_out[rows] = wxy_ref[rows] * keep
    lane = lax.broadcasted_iota(jnp.int32, (128, 128), 1)
    sub = lax.broadcasted_iota(jnp.int32, (128, 128), 0)
    spot = lax.rem(lane, 20)
    ok = ((spot < 2) == (sub >= 124)) | (k != 0)
    ok = ok & ((spot < 18) | (k != at_ref[5] - 1))
    keep = jnp.where(ok, 1.0, 0.0)
    for n in range(2):
        for c in range(6):
            wz_out[n, c] = (wz_ref[n, c].astype(f32) * keep).astype(bf16)

    src = lax.broadcasted_iota(jnp.int32, (256, 128), 0)
    dst = lax.broadcasted_iota(jnp.int32, (256, 128), 1)
    plane = jnp.where(src < 128, lax.shift_right_logical(src, 3) + 8, lax.shift_right_logical(src - 128, 3) - 8)
    goal = lax.shift_right_logical(dst, 3)
    near = (plane >= goal) & (plane <= goal + 8) & ((src & 7) == (dst & 7)) & (plane >= 0)
    across = (plane < 8) != (goal < 4)
    xsum_out[...] = jnp.where(near, jnp.where(across, ex, 1.0), 0.0).astype(bf16)
    centre = jnp.where(dst < 124, dst, dst - 128)
    below = src >= 128
    place = jnp.where(below, (src & 7) - 8, src)
    gap = place - centre
    inside = (gap <= 4) & (gap >= -4)
    crossing = below != (dst >= 124)
    zsum_out[...] = jnp.where(inside, jnp.where(crossing, ez, 1.0), 0.0)

    pick_q = lax.broadcasted_iota(jnp.int32, (8, 32), 0)
    pick_y = lax.broadcasted_iota(jnp.int32, (8, 32), 1)
    pick = ((pick_y == 4 * j + pick_q - 2) & (pick_q >= 2) & (pick_q < 6)).astype(f32).astype(bf16)
    for side in range(2):
        rows_ref[...] = jnp.zeros((128, 32), f32)
        for c in range(6):
            rows_ref[20 * c + 2 : 20 * c + 18] = vel_ref[c, side]
        turned = jnp.transpose(rows_ref[...])
        total = jnp.zeros((8, 128), f32)
        for piece in split3(turned):
            total = total + dot(pick, piece)
        vel_out[8 * side : 8 * side + 8] = total


def split3(v):
    hi = v.astype(bf16)
    r = v - hi.astype(f32)
    mid = r.astype(bf16)
    lo = (r - mid.astype(f32)).astype(bf16)
    return hi, mid, lo


def split2(v):
    hi = v.astype(bf16)
    return hi, (v - hi.astype(f32)).astype(bf16)


def dot(a, b):
    return jnp.dot(a, b, preferred_element_type=f32)


def up_by(v, n, row):
    size = v.shape[0]
    return jnp.where(row < size - n, pltpu.roll(v, size - n, 0), 0.0)


def rows_window(v, head, tail, row8, row40):
    first = v[0:8]
    own = jnp.concatenate([jnp.zeros((8, 128), f32), v[8:40]], axis=0)
    s = first + up_by(first, 1, row8)
    s = s + up_by(s, 2, row8)
    s = s + up_by(s, 4, row8)
    w = own + pltpu.roll(own, 39, 0)
    w = w + pltpu.roll(w, 38, 0)
    w = w + pltpu.roll(w, 36, 0)
    w = w[0:32] + own[8:40]
    top = head * s + tail * w[0:8]
    return jnp.concatenate([top, w[8:32]], axis=0)


def force_kernel(
    edge_ref,
    own_ref,
    zr_ref,
    xr_ref,
    xzr_ref,
    yr_ref,
    xyr_ref,
    vel_ref,
    wxy_ref,
    wz_ref,
    xsum_ref,
    zsum_ref,
    out_ref,
    a_ref,
    h_ref,
    v_ref,
    dz_ref,
    xs_ref,
    hs_ref,
    fh_ref,
    fl_ref,
):
    ex = edge_ref[0]
    ey = edge_ref[1]
    ez = edge_ref[2]
    lane8 = lax.broadcasted_iota(jnp.int32, (8, 128), 1)
    row8 = lax.broadcasted_iota(jnp.int32, (8, 128), 0)
    lane32 = lax.broadcasted_iota(jnp.int32, (32, 128), 1)
    row32 = lax.broadcasted_iota(jnp.int32, (32, 128), 0)
    lane40 = lax.broadcasted_iota(jnp.int32, (40, 128), 1)
    row40 = lax.broadcasted_iota(jnp.int32, (40, 128), 0)
    head = jnp.where(row8 < 4, 1.0, ey)
    tail = jnp.where(row8 < 4, ey, 1.0)

    for h in range(2):
        for t in range(16):
            a_ref[h, 8 + t, 8:40] = own_ref[h, t]
            a_ref[h, 8 + t, 0:8] = yr_ref[h, t]
        for t in range(8):
            a_ref[h, t, 8:40] = xr_ref[h, t]
            a_ref[h, t, 0:8] = xyr_ref[h, t]
        h_ref[h, 0, 8:40] = zr_ref[h]
        h_ref[h, 0, 0:8] = yr_ref[h, 16]
        h_ref[h, 1, 8:40] = xzr_ref[h]
        h_ref[h, 1, 0:8] = xyr_ref[h, 8]

    plus_z = jnp.where(lane40 == 127, ez, 1.0)
    minus_z = jnp.where(lane40 == 0, ez, 1.0)
    for h in range(2):
        for l in range(3, 21):
            if l >= 8:
                halo = pltpu.roll(h_ref[h, 0], (120 - 8 * (l - 8)) % 128, 1)
            else:
                halo = pltpu.roll(h_ref[h, 1], (120 - 8 * (l + 8)) % 128, 1)
            v_ref[h, l - 3] = jnp.where(lane40 >= 124, halo, a_ref[h, l])
            if 4 <= l < 20:
                dz_ref[h, l - 4] = halo
    for h in range(2):
        for l in range(4, 20):
            a = a_ref[h, l]
            halo = dz_ref[h, l - 4]
            up = pltpu.roll(jnp.where(lane40 >= 125, halo, a), 127, 1)
            down = pltpu.roll(jnp.where(lane40 >= 123, halo, a), 1, 1)
            dz_ref[h, l - 4] = plus_z * up - minus_z * down

    def products(f, m):
        return (f, m, f * f, m * m, f * m)

    def x_step(tile, carry):
        rows = pl.ds(pl.multiple_of(tile * 8, 8), 8)
        for q in range(5):
            p = []
            for l in range(24):
                if q == 0:
                    p.append(a_ref[0, l, rows])
                elif q == 1:
                    p.append(a_ref[1, l, rows])
                elif q == 2:
                    f = a_ref[0, l, rows]
                    p.append(f * f)
                elif q == 3:
                    m = a_ref[1, l, rows]
                    p.append(m * m)
                else:
                    p.append(a_ref[0, l, rows] * a_ref[1, l, rows])
            left = [None] * 8
            left[7] = p[7]
            for o in range(6, -1, -1):
                left[o] = left[o + 1] + p[o]
            right = [None] * 8
            right[0] = p[8]
            for o in range(1, 8):
                right[o] = right[o - 1] + p[o + 8]
            for o in range(8):
                xs_ref[q, o, rows] = left[o] + ex * right[o] if o < 4 else ex * left[o] + right[o]
            s = p[8:24]
            b = [s[n] + s[n + 1] for n in range(15)]
            b = [b[n] + b[n + 2] for n in range(13)]
            b = [b[n] + b[n + 4] for n in range(9)]
            for o in range(8):
                xs_ref[q, 8 + o, rows] = b[o] + s[o + 8]
        return carry

    lax.fori_loop(0, 5, x_step, 0)

    x_sum = xsum_ref[...]
    for q in range(5):
        parts = []
        for side in range(2):
            f = h_ref[0, side]
            m = h_ref[1, side]
            parts.append(rows_window(products(f, m)[q], head, tail, row8, row40))
        both = jnp.concatenate(parts, axis=1)
        total = jnp.zeros((32, 128), f32)
        for piece in split3(both):
            total = total + dot(piece, x_sum)
        for n, piece in enumerate(split3(total)):
            hs_ref[q, n] = piece

    from_row = lax.broadcasted_iota(jnp.int32, (256, 128), 0)
    plus_y = jnp.where(row32 == 3, ey, 1.0)
    minus_y = jnp.where(row32 == 4, ey, 1.0)

    def o_step(o, carry):
        mine = (from_row < 128) | (lax.shift_right_logical(from_row - 128, 3) == o)
        z_sum = jnp.where(mine, zsum_ref[...], 0.0).astype(bf16)
        pieces = [[], [], []]
        for q in range(5):
            y = rows_window(xs_ref[q, o], head, tail, row8, row40)
            for n, piece in enumerate(split3(y)):
                pieces[n].append(jnp.concatenate([piece, hs_ref[q, n]], axis=1))
        big = dot(jnp.concatenate(pieces[0] + pieces[1] + pieces[2], axis=0), z_sum)
        sums = (big[0:160] + big[160:320]) + big[320:480]
        sums = sums * (1.0 / 729.0)
        mean_f = sums[0:32]
        mean_m = sums[32:64]
        var_f = sums[64:96] - mean_f * mean_f + epsilon_value
        var_m = sums[96:128] - mean_m * mean_m + epsilon_value
        cov = sums[128:160] - mean_f * mean_m
        off_f = v_ref[0, o + 1, 4:36] - mean_f
        off_m = v_ref[1, o + 1, 4:36] - mean_m
        inv = 1.0 / (var_f * var_m)
        factor = cov * inv
        pulls = (
            factor * (off_m - factor * var_m * off_f),
            factor * (off_f - factor * var_f * off_m),
        )
        plus_x = jnp.where(o == 3, ex, 1.0)
        minus_x = jnp.where(o == 4, ex, 1.0)
        where_to = pl.ds(pl.multiple_of(o * 32, 32), 32)
        for h in range(2):
            dx = plus_x * v_ref[h, o + 2, 4:36] - minus_x * v_ref[h, o, 4:36]
            dy = plus_y * v_ref[h, o + 1, 5:37] - minus_y * v_ref[h, o + 1, 3:35]
            dz = dz_ref[h, o, 4:36]
            for c, d in enumerate((dx, dy, dz)):
                hi, lo = split2(pulls[h] * d)
                fh_ref[3 * h + c, where_to] = hi
                fl_ref[3 * h + c, where_to] = lo
        return carry

    lax.fori_loop(0, 16, o_step, 0, unroll=8)

    total = jnp.zeros((40, 128), f32)
    wxy = wxy_ref[...].astype(bf16)
    wxy_hi = wxy_ref[0:40].astype(bf16)
    for c in range(6):
        first = dot(wxy, fh_ref[c])
        second = dot(wxy_hi, fl_ref[c])
        xy = first[0:40] + first[40:80] + second
        hi, lo = split2(xy)
        total = total + dot(hi, wz_ref[0, c]) + dot(hi, wz_ref[1, c]) + dot(lo, wz_ref[0, c])
    total = step_size * total
    out_ref[0:16] = total[0:16]
    out_ref[16:32] = total[16:32] + vel_ref[...]
    out_ref[32:40] = total[32:40]


def fold_kernel(mine_ref, low_ref, high_ref, out_ref):
    lane = lax.broadcasted_iota(jnp.int32, (40, 128), 1)
    spot = lax.rem(lane, 20)
    live = lane < 120
    low = pltpu.roll(low_ref[...], 112, 1)
    high = pltpu.roll(high_ref[...], 16, 1)
    total = mine_ref[...]
    total = total + jnp.where(live & (spot < 3), low, 0.0)
    out_ref[...] = total + jnp.where(live & (spot >= 16), high, 0.0)


def across_kernel(own_ref, below_ref, above_ref, far_ref, out_ref):
    tiles = lambda ref: [ref[8 * p : 8 * p + 8] for p in range(5)]
    own, below, above, far = tiles(own_ref), tiles(below_ref), tiles(above_ref), tiles(far_ref)
    window = [
        own[0] + below[2] + far[4],
        own[1] + below[3],
        own[2] + below[4] + above[0],
        own[3] + above[1],
        own[4] + above[2] + far[0],
        above[3] + far[1],
    ]
    for n in range(8):
        for w in range(6):
            out_ref[n, 8 * w : 8 * w + 8] = window[w]


def field_kernel(at_ref, g_ref, wxy_ref, wz_ref, nv_ref, field_ref, rows_ref, buf_ref, sems):
    me_j = at_ref[1]
    row8 = lax.broadcasted_iota(jnp.int32, (8, 128), 0)

    window = []
    js = [lax.rem(me_j + 7, 8), me_j, lax.rem(me_j + 1, 8)]
    for w in range(6):
        before, own, after = (g_ref[j, 8 * w : 8 * w + 8] for j in js)
        window.append(own + jnp.where(row8 < 4, pltpu.roll(before, 4, 0), pltpu.roll(after, 4, 0)))
    coefs = jnp.concatenate(window, axis=0)
    row = lax.broadcasted_iota(jnp.int32, (48, 128), 0)
    lane = lax.broadcasted_iota(jnp.int32, (48, 128), 1)
    at_x = 2 * at_ref[0] - 2 + lax.shift_right_logical(row, 3)
    at_y = 4 * me_j - 2 + (row & 7)
    at_z = 16 * at_ref[2] - 2 + lax.rem(lane, 20)
    real = (at_x >= 0) & (at_x < 2 * at_ref[3]) & (at_y >= 0) & (at_y < 4 * at_ref[4])
    real = real & (at_z >= 0) & (at_z < 16 * at_ref[5]) & (lane < 120)
    coefs = jnp.where(real, coefs, 0.0)
    hi, lo = split2(coefs)
    copies = []
    for pair in range(3):
        rhs = []
        for c in (2 * pair, 2 * pair + 1):
            along = dot(hi, wz_ref[0, c]) + dot(hi, wz_ref[1, c]) + dot(lo, wz_ref[0, c])
            ch, cl = split2(along)
            rhs.append(jnp.concatenate([ch, cl, ch], axis=0))
        both = dot(wxy_ref[...], jnp.concatenate(rhs, axis=1)).astype(bf16)
        for n in range(2):
            buf_ref[2 * pair + n] = both[:, 128 * n : 128 * n + 128]
        there = pl.ds(2 * pair, 2)
        copy = pltpu.make_async_copy(buf_ref.at[there], field_ref.at[there], sems.at[pair])
        copy.start()
        copies.append(copy)

    for side in range(2):
        cols = [g_ref[j, 16 + 8 * side : 24 + 8 * side] for j in range(8)]
        turned = [pltpu.roll(c, 4, 0) for c in cols]
        tiles = []
        zero = jnp.zeros((8, 128), f32)
        for n in range(5):
            even = cols[2 * n] if n < 4 else zero
            high = turned[2 * n + 1] if n < 4 else zero
            low = turned[2 * n - 1] if n > 0 else zero
            tiles.append(even + jnp.where(row8 < 4, low, high))
        tiles[4] = tiles[4] + tiles[0]
        for n in range(5):
            rows_ref[side, 8 * n : 8 * n + 8] = tiles[n]
        block = jnp.transpose(rows_ref[side, 2:34])
        for c in range(6):
            nv_ref[c, side] = block[20 * c + 2 : 20 * c + 18]
    for copy in copies:
        copy.wait()


VMEM = pl.BlockSpec(memory_space=pltpu.VMEM)
SMEM = pl.BlockSpec(memory_space=pltpu.SMEM)


HBM = pl.BlockSpec(memory_space=pltpu.HBM)


def call(body, out_shape, in_specs, scratch=(), out_specs=None, flops=0, bytes_accessed=0):
    return pl.pallas_call(
        body,
        out_shape=[jax.ShapeDtypeStruct(shape, dtype) for shape, dtype in out_shape],
        in_specs=in_specs,
        out_specs=out_specs or [VMEM] * len(out_shape),
        scratch_shapes=list(scratch),
        compiler_params=pltpu.CompilerParams(vmem_limit_bytes=48 << 20),
        cost_estimate=pl.CostEstimate(flops=flops, bytes_accessed=bytes_accessed, transcendentals=0),
    )


def pairs(mesh_sizes, di, dj, dk):
    ni, nj, nk = mesh_sizes
    out = []
    for i in range(ni):
        for j in range(nj):
            for k in range(nk):
                to = (((i + di) % ni) * nj + (j + dj) % nj) * nk + (k + dk) % nk
                out.append(((i * nj + j) * nk + k, to))
    return out


def fixed_tables():
    position = lambda n: np.arange(n) - 4
    weight = lambda pos, points: spline((pos[None, :] - 8.0 * (np.arange(points) - 2)[:, None] - 3.5) / 8.0)
    wx = weight(position(16), 5)
    wy = np.concatenate([weight(position(32), 7), np.zeros((1, 32))])
    hi, lo = split_two(np.einsum("po,qr->pqor", wx, wy).reshape(40, 512))
    wxy = np.concatenate([hi, lo]).astype(np.float32)
    lanes = np.arange(128)
    wz = weight(np.where(lanes >= 124, lanes - 128, lanes), 19)
    canvas = np.zeros((6, 128, 128))
    for c in range(6):
        canvas[c, :, 20 * c : 20 * c + 19] = wz.T
    wzs = np.stack(split_two(canvas))
    ex, ey, ez = (weight(np.arange(n), points) for n, points in ((16, 6), (32, 8), (128, 20)))
    hi, lo = split_two(np.einsum("px,qy->xypq", ex, ey).reshape(512, 48))
    exy = np.concatenate([hi, hi, lo], axis=1)
    canvas = np.zeros((6, 128, 128))
    for c in range(6):
        canvas[c, 20 * c : 20 * c + 20] = ez
    ezs = np.stack(split_two(canvas))
    return wxy, wzs, exy, ezs


def shards(images, velocity):
    axes = ("gx", "gy", "gz")
    sizes = tuple(lax.axis_size(a) for a in axes)
    spot = [lax.axis_index(a) for a in axes]
    nk = sizes[2]
    at = jnp.stack([jnp.int32(v) for v in (*spot, *sizes)])
    wxy, wzs, exy, ezs = fixed_tables()

    def send(v, di, dj, dk):
        return lax.ppermute(v, axes, pairs(sizes, di, dj, dk))

    pack, to_x, to_y, to_xy = call(
        pack_kernel,
        [((2, 32, 128), f32), ((2, 8, 32, 128), f32), ((2, 17, 8, 128), f32), ((2, 9, 8, 128), f32)],
        [HBM],
        [pltpu.VMEM((2, 16, 32, 128), f32), pltpu.SemaphoreType.DMA((8,))],
        bytes_accessed=10**6,
    )(images)
    zr = lax.ppermute(pack, "gz", [(n, (n + 1) % nk) for n in range(nk)])
    xr = send(to_x, 1, 0, 0)
    yr = send(to_y.at[:, 16].set(zr[:, 24:]), 0, 1, 0)
    xyr = send(to_xy.at[:, 8].set(zr[:, 24:]), 1, 1, 0)
    xzr = send(zr, 1, 0, 0)

    velocity = jnp.swapaxes(velocity, 3, 4).reshape(6, 2, 16, 32)
    vel, wxy, wzs, xsum, zsum = call(
        prep_kernel,
        [((16, 128), f32), ((80, 512), f32), ((2, 6, 128, 128), bf16), ((256, 128), bf16), ((256, 128), f32)],
        [SMEM] + [VMEM] * 3,
        [pltpu.VMEM((128, 32), f32)],
        bytes_accessed=10**6,
    )(at, velocity, wxy, wzs)

    edges = jnp.minimum(at, 1).astype(f32)
    (part,) = call(
        force_kernel,
        [((40, 128), f32)],
        [SMEM] + [VMEM] * 11,
        [
            pltpu.VMEM((2, 24, 40, 128), f32),
            pltpu.VMEM((2, 2, 40, 128), f32),
            pltpu.VMEM((2, 18, 40, 128), f32),
            pltpu.VMEM((2, 16, 40, 128), f32),
            pltpu.VMEM((5, 16, 40, 128), f32),
            pltpu.VMEM((5, 3, 32, 128), bf16),
            pltpu.VMEM((6, 512, 128), bf16),
            pltpu.VMEM((6, 512, 128), bf16),
        ],
        flops=10**9,
        bytes_accessed=2 * 10**6,
    )(edges, images, zr, xr, xzr, yr, xyr, vel, wxy, wzs, xsum, zsum)

    low = lax.ppermute(part, "gz", [(n, (n + 1) % nk) for n in range(nk)])
    high = lax.ppermute(part, "gz", [((n + 1) % nk, n) for n in range(nk)])
    (own,) = call(fold_kernel, [((40, 128), f32)], [VMEM] * 3)(part, low, high)
    below = send(own, 1, 0, 0)
    above = send(own, -1, 0, 0)
    far = send(own, 2, 0, 0)
    (copies,) = call(across_kernel, [((8, 48, 128), f32)], [VMEM] * 4)(own, below, above, far)
    everything = lax.all_to_all(copies, "gy", 0, 0, tiled=True)

    nv, field = call(
        field_kernel,
        [((6, 2, 16, 32), f32), ((6, 512, 128), bf16)],
        [SMEM] + [VMEM] * 3,
        [pltpu.VMEM((2, 40, 128), f32), pltpu.VMEM((6, 512, 128), bf16), pltpu.SemaphoreType.DMA((3,))],
        out_specs=[VMEM, HBM],
        flops=10**8,
        bytes_accessed=10**6,
    )(at, everything, exy, ezs)
    nv = jnp.swapaxes(nv.reshape(2, 3, 2, 16, 32), 3, 4)
    return nv, field.reshape(2, 3, 16, 32, 128)


def solution(mesh):
    placed = (P(None, "gx", "gy", "gz"), P(None, None, "gx", None, "gz"))
    return jax.shard_map(
        shards,
        mesh=mesh,
        in_specs=placed,
        out_specs=(P(None, None, "gx", None, "gz"), P(None, None, "gx", "gy", "gz")),
        check_vma=False,
    )
```

```python
import functools

import jax
import jax.numpy as jnp
import numpy as np
from jax import lax
from jax.experimental import pallas as pl
from jax.experimental.pallas import tpu as pltpu
from jax.sharding import PartitionSpec as P

epsilon_value = 1e-05
step_size = 0.5
f32 = jnp.float32
bf16 = jnp.bfloat16


def spline(t):
    m = np.abs(t)
    inside = 2.0 / 3.0 - m * m + 0.5 * m * m * m
    out = np.maximum(2.0 - m, 0.0)
    return np.where(m < 1.0, inside, out * out * out / 6.0)


def split_two(w):
    hi = w.astype(np.float32).astype(jnp.bfloat16)
    lo = (w - hi.astype(np.float64)).astype(np.float32).astype(jnp.bfloat16)
    return hi, lo


def pack_kernel(img_ref, out_ref):
    lane = lax.broadcasted_iota(jnp.int32, (32, 128), 1)
    for h in range(2):
        packed = jnp.zeros((32, 128), f32)
        for t in range(16):
            moved = pltpu.roll(img_ref[h, t], (8 * t + 8) % 128, 1)
            packed = jnp.where((lane >= 8 * t) & (lane < 8 * t + 8), moved, packed)
        out_ref[h] = packed


def slab_kernel(img_ref, x_ref, y_ref, xy_ref):
    for h in range(2):
        for t in range(16):
            y_ref[h, t] = img_ref[h, t, 24:32]
            if t >= 8:
                x_ref[h, t - 8] = img_ref[h, t]
                xy_ref[h, t - 8] = img_ref[h, t, 24:32]
        y_ref[h, 16] = jnp.zeros((8, 128), f32)
        xy_ref[h, 8] = jnp.zeros((8, 128), f32)


def spline_at(t):
    m = jnp.abs(t)
    inside = 2.0 / 3.0 - m * m + 0.5 * m * m * m
    out = jnp.maximum(2.0 - m, 0.0)
    return jnp.where(m < 1.0, inside, out * out * out / 6.0)


def weights(voxel, point):
    return spline_at((voxel.astype(f32) - 8.0 * point.astype(f32) - 3.5) * 0.125)


def prep_kernel(at_ref, vel_ref, vel_out, wxy_out, wz_out, xsum_out, zsum_out, rows_ref):
    i = at_ref[0]
    j = at_ref[1]
    k = at_ref[2]
    ex = jnp.where(i == 0, 0.0, 1.0)
    ez = jnp.where(k == 0, 0.0, 1.0)
    row = lax.broadcasted_iota(jnp.int32, (40, 512), 0)
    col = lax.broadcasted_iota(jnp.int32, (40, 512), 1)
    p = lax.shift_right_logical(row, 3)
    q = row & 7
    o = lax.shift_right_logical(col, 5)
    r = col & 31
    ok = ((p < 2) == (o < 4)) | (i != 0)
    ok = ok & (((q < 2) == (r < 4)) | (j != 0)) & (q < 7)
    ok = ok & ((p < 4) | (i != at_ref[3] - 1)) & ((q < 6) | (j != at_ref[4] - 1))
    table = jnp.where(ok, weights(o - 4, p - 2) * weights(r - 4, q - 2), 0.0)
    hi, lo = split2(table)
    wxy_out[...] = jnp.concatenate([hi.astype(f32), lo.astype(f32)], axis=0).astype(bf16)
    lane = lax.broadcasted_iota(jnp.int32, (128, 128), 1)
    sub = lax.broadcasted_iota(jnp.int32, (128, 128), 0)
    spot = lax.rem(lane, 20)
    ok = ((spot < 2) == (sub >= 124)) | (k != 0)
    ok = ok & (spot < 19) & ((spot < 18) | (k != at_ref[5] - 1))
    voxel = jnp.where(sub >= 124, sub - 128, sub)
    hi, lo = split2(jnp.where(ok, weights(voxel, spot - 2), 0.0))
    wz_out[...] = jnp.concatenate([hi, lo], axis=1)

    src = lax.broadcasted_iota(jnp.int32, (256, 128), 0)
    dst = lax.broadcasted_iota(jnp.int32, (256, 128), 1)
    plane = jnp.where(src < 128, lax.shift_right_logical(src, 3) + 8, lax.shift_right_logical(src - 128, 3) - 8)
    goal = lax.shift_right_logical(dst, 3)
    near = (plane >= goal) & (plane <= goal + 8) & ((src & 7) == (dst & 7)) & (plane >= 0)
    across = (plane < 8) != (goal < 4)
    xsum_out[...] = jnp.where(near, jnp.where(across, ex, 1.0), 0.0).astype(bf16)
    centre = jnp.where(dst < 124, dst, dst - 128)
    below = src >= 128
    place = jnp.where(below, (src & 7) - 8, src)
    gap = place - centre
    inside = (gap <= 4) & (gap >= -4)
    crossing = below != (dst >= 124)
    zsum_out[...] = jnp.where(inside, jnp.where(crossing, ez, 1.0), 0.0)

    pick_q = lax.broadcasted_iota(jnp.int32, (8, 32), 0)
    pick_y = lax.broadcasted_iota(jnp.int32, (8, 32), 1)
    pick = ((pick_y == 4 * j + pick_q - 2) & (pick_q >= 2) & (pick_q < 6)).astype(f32).astype(bf16)
    for side in range(2):
        rows_ref[...] = jnp.zeros((128, 32), f32)
        for c in range(6):
            rows_ref[20 * c + 2 : 20 * c + 18] = vel_ref[c, side]
        turned = jnp.transpose(rows_ref[...])
        total = jnp.zeros((8, 128), f32)
        for piece in split3(turned):
            total = total + dot(pick, piece)
        vel_out[8 * side : 8 * side + 8] = total


def split3(v):
    hi = v.astype(bf16)
    r = v - hi.astype(f32)
    mid = r.astype(bf16)
    lo = (r - mid.astype(f32)).astype(bf16)
    return hi, mid, lo


def split2(v):
    hi = v.astype(bf16)
    return hi, (v - hi.astype(f32)).astype(bf16)


def dot(a, b):
    return jnp.dot(a, b, preferred_element_type=f32)


def up_by(v, n, row):
    size = v.shape[0]
    return jnp.where(row < size - n, pltpu.roll(v, size - n, 0), 0.0)


def rows_window(v, head, tail, row8):
    first = v[0:8]
    own = jnp.concatenate([jnp.zeros((8, 128), f32), v[8:40]], axis=0)
    s = first + up_by(first, 1, row8)
    s = s + up_by(s, 2, row8)
    s = s + up_by(s, 4, row8)
    w = own + pltpu.roll(own, 39, 0)
    w = w + pltpu.roll(w, 38, 0)
    w = w + pltpu.roll(w, 36, 0)
    w = w[0:32] + own[8:40]
    top = head * s + tail * w[0:8]
    return jnp.concatenate([top, w[8:32]], axis=0)


def force_kernel(upper, at_ref, own_ref, zr_ref, yr_ref, *refs):
    if upper:
        base_ref, *refs = refs
    else:
        xr_ref, xzr_ref, xyr_ref, base_ref, *refs = refs
    wxy_ref, wz_ref, xsum_ref, zsum_ref, out_ref, a_ref, h_ref, v_ref, dz_ref, xs_ref, hs_ref, fh_ref, fl_ref = refs
    first = 8 if upper else 0
    ex, ey, ez = (jnp.where(at_ref[n] == 0, 0.0, 1.0) for n in range(3))
    row8 = lax.broadcasted_iota(jnp.int32, (8, 128), 0)
    row32 = lax.broadcasted_iota(jnp.int32, (32, 128), 0)
    lane40 = lax.broadcasted_iota(jnp.int32, (40, 128), 1)
    head = jnp.where(row8 < 4, 1.0, ey)
    tail = jnp.where(row8 < 4, ey, 1.0)

    for h in range(2):
        for n in range(16):
            if upper or n >= 8:
                t = n if upper else n - 8
                a_ref[h, n, 8:40] = own_ref[h, t]
                a_ref[h, n, 0:8] = yr_ref[h, t]
            else:
                a_ref[h, n, 8:40] = xr_ref[h, n]
                a_ref[h, n, 0:8] = xyr_ref[h, n]
        h_ref[h, 0, 8:40] = zr_ref[h]
        h_ref[h, 0, 0:8] = yr_ref[h, 16]
        if not upper:
            h_ref[h, 1, 8:40] = xzr_ref[h]
            h_ref[h, 1, 0:8] = xyr_ref[h, 8]

    plus_z = jnp.where(lane40 == 127, ez, 1.0)
    minus_z = jnp.where(lane40 == 0, ez, 1.0)
    for h in range(2):
        for n in range(3, 13):
            l = n + first
            if l >= 8:
                halo = pltpu.roll(h_ref[h, 0], (120 - 8 * (l - 8)) % 128, 1)
            else:
                halo = pltpu.roll(h_ref[h, 1], (120 - 8 * (l + 8)) % 128, 1)
            v_ref[h, n - 3] = jnp.where(lane40 >= 124, halo, a_ref[h, n])
            if 4 <= n < 12:
                dz_ref[h, n - 4] = halo
    for h in range(2):
        for n in range(4, 12):
            a = a_ref[h, n]
            halo = dz_ref[h, n - 4]
            up = pltpu.roll(jnp.where(lane40 >= 125, halo, a), 127, 1)
            down = pltpu.roll(jnp.where(lane40 >= 123, halo, a), 1, 1)
            dz_ref[h, n - 4] = plus_z * up - minus_z * down

    def x_step(tile, carry):
        rows = pl.ds(pl.multiple_of(tile * 8, 8), 8)
        for q in range(5):
            p = []
            for n in range(16):
                if q == 4:
                    p.append(a_ref[0, n, rows] * a_ref[1, n, rows])
                else:
                    value = a_ref[q % 2, n, rows]
                    p.append(value if q < 2 else value * value)
            if upper:
                b = [p[n] + p[n + 1] for n in range(15)]
                b = [b[n] + b[n + 2] for n in range(13)]
                b = [b[n] + b[n + 4] for n in range(9)]
                for o in range(8):
                    xs_ref[q, o, rows] = b[o] + p[o + 8]
                continue
            left = [None] * 8
            left[7] = p[7]
            for o in range(6, -1, -1):
                left[o] = left[o + 1] + p[o]
            right = p[8]
            for o in range(8):
                if o > 0:
                    right = right + p[o + 8]
                xs_ref[q, o, rows] = left[o] + ex * right if o < 4 else ex * left[o] + right
        return carry

    lax.fori_loop(0, 5, x_step, 0)

    sides = 1 if upper else 2
    x_sum = xsum_ref[0 : 128 * sides]
    for q in range(5):
        parts = []
        for side in range(sides):
            f = h_ref[0, side]
            m = h_ref[1, side]
            value = (f, m, f * f, m * m, f * m)[q]
            parts.append(rows_window(value, head, tail, row8))
        total = jnp.zeros((32, 128), f32)
        for piece in split3(jnp.concatenate(parts, axis=1)):
            total = total + dot(piece, x_sum)
        for n, piece in enumerate(split3(total)):
            hs_ref[q, n] = piece

    from_row = lax.broadcasted_iota(jnp.int32, (256, 128), 0)
    plus_y = jnp.where(row32 == 3, ey, 1.0)
    minus_y = jnp.where(row32 == 4, ey, 1.0)

    def o_step(o, carry):
        mine = (from_row < 128) | (lax.shift_right_logical(from_row - 128, 3) == o + first)
        z_sum = jnp.where(mine, zsum_ref[...], 0.0).astype(bf16)
        pieces = [[], [], []]
        for q in range(5):
            y = rows_window(xs_ref[q, o], head, tail, row8)
            for n, piece in enumerate(split3(y)):
                pieces[n].append(jnp.concatenate([piece, hs_ref[q, n]], axis=1))
        big = dot(jnp.concatenate(pieces[0] + pieces[1] + pieces[2], axis=0), z_sum)
        sums = (big[0:160] + big[160:320]) + big[320:480]
        sums = sums * (1.0 / 729.0)
        mean_f = sums[0:32]
        mean_m = sums[32:64]
        var_f = sums[64:96] - mean_f * mean_f + epsilon_value
        var_m = sums[96:128] - mean_m * mean_m + epsilon_value
        cov = sums[128:160] - mean_f * mean_m
        off_f = v_ref[0, o + 1, 4:36] - mean_f
        off_m = v_ref[1, o + 1, 4:36] - mean_m
        inv = 1.0 / (var_f * var_m)
        factor = cov * inv
        pulls = (
            factor * (off_m - factor * var_m * off_f),
            factor * (off_f - factor * var_f * off_m),
        )
        plus_x = jnp.where(o + first == 3, ex, 1.0)
        minus_x = jnp.where(o + first == 4, ex, 1.0)
        where_to = pl.ds(pl.multiple_of(o * 32, 32), 32)
        for h in range(2):
            dx = plus_x * v_ref[h, o + 2, 4:36] - minus_x * v_ref[h, o, 4:36]
            dy = plus_y * v_ref[h, o + 1, 5:37] - minus_y * v_ref[h, o + 1, 3:35]
            dz = dz_ref[h, o, 4:36]
            for c, d in enumerate((dx, dy, dz)):
                hi, lo = split2(pulls[h] * d)
                fh_ref[3 * h + c, where_to] = hi
                fl_ref[3 * h + c, where_to] = lo
        return carry

    lax.fori_loop(0, 8, o_step, 0, unroll=8)

    cols = slice(32 * first, 32 * first + 256)
    wxy = wxy_ref[:, cols]
    wxy_hi = wxy_ref[0:40, cols]
    planes = []
    for c in range(6):
        one = dot(wxy, fh_ref[c])
        planes.append(one[0:40] + one[40:80] + dot(wxy_hi, fl_ref[c]))
    hi, lo = split2(jnp.concatenate(planes, axis=0))
    along = dot(jnp.concatenate([hi, lo], axis=0), wz_ref[...])
    along = (along[0:240, 0:128] + along[0:240, 128:256]) + along[240:480, 0:128]
    which = lax.div(lax.broadcasted_iota(jnp.int32, (40, 128), 1), 20)
    total = jnp.zeros((40, 128), f32)
    for c in range(6):
        total = total + jnp.where(which == c, along[40 * c : 40 * c + 40], 0.0)
    total = step_size * total
    if upper:
        out_ref[0:16] = total[0:16]
        out_ref[16:32] = total[16:32] + base_ref[...]
        out_ref[32:40] = total[32:40]
    else:
        out_ref[...] = total + base_ref[...]


def fold_kernel(mine_ref, low_ref, high_ref, out_ref):
    lane = lax.broadcasted_iota(jnp.int32, (40, 128), 1)
    spot = lax.rem(lane, 20)
    live = lane < 120
    low = pltpu.roll(low_ref[...], 112, 1)
    high = pltpu.roll(high_ref[...], 16, 1)
    total = mine_ref[...]
    total = total + jnp.where(live & (spot < 3), low, 0.0)
    out_ref[...] = total + jnp.where(live & (spot >= 16), high, 0.0)


def across_kernel(own_ref, below_ref, above_ref, far_ref, out_ref):
    tiles = lambda ref: [ref[8 * p : 8 * p + 8] for p in range(5)]
    own, below, above, far = tiles(own_ref), tiles(below_ref), tiles(above_ref), tiles(far_ref)
    window = [
        own[0] + below[2] + far[4],
        own[1] + below[3],
        own[2] + below[4] + above[0],
        own[3] + above[1],
        own[4] + above[2] + far[0],
        above[3] + far[1],
    ]
    for n in range(8):
        for w in range(6):
            out_ref[n, 8 * w : 8 * w + 8] = window[w]


def field_kernel(at_ref, g_ref, wxy_ref, wz_ref, nv_ref, field_ref, rows_ref, buf_ref, sems):
    me_j = at_ref[1]
    row8 = lax.broadcasted_iota(jnp.int32, (8, 128), 0)

    window = []
    js = [lax.rem(me_j + 7, 8), me_j, lax.rem(me_j + 1, 8)]
    for w in range(6):
        before, own, after = (g_ref[j, 8 * w : 8 * w + 8] for j in js)
        window.append(own + jnp.where(row8 < 4, pltpu.roll(before, 4, 0), pltpu.roll(after, 4, 0)))
    coefs = jnp.concatenate(window, axis=0)
    row = lax.broadcasted_iota(jnp.int32, (48, 128), 0)
    lane = lax.broadcasted_iota(jnp.int32, (48, 128), 1)
    at_x = 2 * at_ref[0] - 2 + lax.shift_right_logical(row, 3)
    at_y = 4 * me_j - 2 + (row & 7)
    at_z = 16 * at_ref[2] - 2 + lax.rem(lane, 20)
    real = (at_x >= 0) & (at_x < 2 * at_ref[3]) & (at_y >= 0) & (at_y < 4 * at_ref[4])
    real = real & (at_z >= 0) & (at_z < 16 * at_ref[5]) & (lane < 120)
    part = lax.div(lane, 20)
    coefs = jnp.where(real, coefs, 0.0)
    hi, lo = split2(jnp.concatenate([jnp.where(part == c, coefs, 0.0) for c in range(6)], axis=0))
    along = dot(jnp.concatenate([hi, lo], axis=0), wz_ref[...])
    along = (along[0:288, 0:128] + along[0:288, 128:256]) + along[288:576, 0:128]
    ch, cl = split2(along)
    copies = []
    for pair in range(3):
        rhs = []
        for c in (2 * pair, 2 * pair + 1):
            rows = slice(48 * c, 48 * c + 48)
            rhs.append(jnp.concatenate([ch[rows], cl[rows], ch[rows]], axis=0))
        both = dot(wxy_ref[...], jnp.concatenate(rhs, axis=1)).astype(bf16)
        for n in range(2):
            buf_ref[2 * pair + n] = both[:, 128 * n : 128 * n + 128]
        there = pl.ds(2 * pair, 2)
        copy = pltpu.make_async_copy(buf_ref.at[there], field_ref.at[there], sems.at[pair])
        copy.start()
        copies.append(copy)

    for side in range(2):
        cols = [g_ref[j, 16 + 8 * side : 24 + 8 * side] for j in range(8)]
        turned = [pltpu.roll(c, 4, 0) for c in cols]
        tiles = []
        zero = jnp.zeros((8, 128), f32)
        for n in range(5):
            even = cols[2 * n] if n < 4 else zero
            high = turned[2 * n + 1] if n < 4 else zero
            low = turned[2 * n - 1] if n > 0 else zero
            tiles.append(even + jnp.where(row8 < 4, low, high))
        tiles[4] = tiles[4] + tiles[0]
        for n in range(5):
            rows_ref[side, 8 * n : 8 * n + 8] = tiles[n]
        block = jnp.transpose(rows_ref[side, 2:34])
        for c in range(6):
            nv_ref[c, side] = block[20 * c + 2 : 20 * c + 18]
    for copy in copies:
        copy.wait()


VMEM = pl.BlockSpec(memory_space=pltpu.VMEM)
SMEM = pl.BlockSpec(memory_space=pltpu.SMEM)


HBM = pl.BlockSpec(memory_space=pltpu.HBM)


def call(body, out_shape, in_specs, scratch=(), out_specs=None, flops=0, bytes_accessed=0):
    return pl.pallas_call(
        body,
        out_shape=[jax.ShapeDtypeStruct(shape, dtype) for shape, dtype in out_shape],
        in_specs=in_specs,
        out_specs=out_specs or [VMEM] * len(out_shape),
        scratch_shapes=list(scratch),
        compiler_params=pltpu.CompilerParams(vmem_limit_bytes=48 << 20),
        cost_estimate=pl.CostEstimate(flops=flops, bytes_accessed=bytes_accessed, transcendentals=0),
    )


def pairs(mesh_sizes, di, dj, dk):
    ni, nj, nk = mesh_sizes
    out = []
    for i in range(ni):
        for j in range(nj):
            for k in range(nk):
                to = (((i + di) % ni) * nj + (j + dj) % nj) * nk + (k + dk) % nk
                out.append(((i * nj + j) * nk + k, to))
    return out


def fixed_tables():
    weight = lambda n, points: spline((np.arange(n)[None, :] - 8.0 * (np.arange(points) - 2)[:, None] - 3.5) / 8.0)
    ex, ey, ez = (weight(n, points) for n, points in ((16, 6), (32, 8), (128, 20)))
    hi, lo = split_two(np.einsum("px,qy->xypq", ex, ey).reshape(512, 48))
    exy = np.concatenate([hi, hi, lo], axis=1)
    padded = lambda part: np.concatenate([np.tile(part, (6, 1)), np.zeros((8, 128), part.dtype)])
    return exy, np.concatenate([padded(part) for part in split_two(ez)], axis=1)


def shards(images, velocity):
    axes = ("gx", "gy", "gz")
    sizes = tuple(lax.axis_size(a) for a in axes)
    spot = [lax.axis_index(a) for a in axes]
    nk = sizes[2]
    at = jnp.stack([jnp.int32(v) for v in (*spot, *sizes)])
    exy, ezs = fixed_tables()

    def send(v, di, dj, dk):
        return lax.ppermute(v, axes, pairs(sizes, di, dj, dk))

    (pack,) = call(pack_kernel, [((2, 32, 128), f32)], [VMEM], bytes_accessed=6 * 10**5)(images)
    to_x, to_y, to_xy = call(
        slab_kernel,
        [((2, 8, 32, 128), f32), ((2, 17, 8, 128), f32), ((2, 9, 8, 128), f32)],
        [VMEM],
        bytes_accessed=10**6,
    )(images)
    zr = lax.ppermute(pack, "gz", [(n, (n + 1) % nk) for n in range(nk)])
    xr = send(to_x, 1, 0, 0)
    yr = send(to_y.at[:, 16].set(zr[:, 24:]), 0, 1, 0)
    xyr = send(to_xy.at[:, 8].set(zr[:, 24:]), 1, 1, 0)
    xzr = send(zr, 1, 0, 0)

    velocity = jnp.swapaxes(velocity, 3, 4).reshape(6, 2, 16, 32)
    vel, wxy, wzs, xsum, zsum = call(
        prep_kernel,
        [((16, 128), f32), ((80, 512), bf16), ((128, 256), bf16), ((256, 128), bf16), ((256, 128), f32)],
        [SMEM, VMEM],
        [pltpu.VMEM((128, 32), f32)],
        bytes_accessed=10**6,
    )(at, velocity)

    def forces(upper, *arrays):
        return call(
            functools.partial(force_kernel, upper),
            [((40, 128), f32)],
            [SMEM] + [VMEM] * (len(arrays) + 4),
            [
                pltpu.VMEM((2, 16, 40, 128), f32),
                pltpu.VMEM((2, 2, 40, 128), f32),
                pltpu.VMEM((2, 10, 40, 128), f32),
                pltpu.VMEM((2, 8, 40, 128), f32),
                pltpu.VMEM((5, 8, 40, 128), f32),
                pltpu.VMEM((5, 3, 32, 128), bf16),
                pltpu.VMEM((6, 256, 128), bf16),
                pltpu.VMEM((6, 256, 128), bf16),
            ],
            flops=5 * 10**8,
            bytes_accessed=10**6,
        )(at, *arrays, wxy, wzs, xsum, zsum)[0]

    part = forces(True, images, zr, yr, vel)
    part = forces(False, images, zr, yr, xr, xzr, xyr, part)

    low = lax.ppermute(part, "gz", [(n, (n + 1) % nk) for n in range(nk)])
    high = lax.ppermute(part, "gz", [((n + 1) % nk, n) for n in range(nk)])
    (own,) = call(fold_kernel, [((40, 128), f32)], [VMEM] * 3)(part, low, high)
    below = send(own, 1, 0, 0)
    above = send(own, -1, 0, 0)
    far = send(own, 2, 0, 0)
    (copies,) = call(across_kernel, [((8, 48, 128), f32)], [VMEM] * 4)(own, below, above, far)
    everything = lax.all_to_all(copies, "gy", 0, 0, tiled=True)

    nv, field = call(
        field_kernel,
        [((6, 2, 16, 32), f32), ((6, 512, 128), bf16)],
        [SMEM] + [VMEM] * 3,
        [pltpu.VMEM((2, 40, 128), f32), pltpu.VMEM((6, 512, 128), bf16), pltpu.SemaphoreType.DMA((3,))],
        out_specs=[VMEM, HBM],
        flops=10**8,
        bytes_accessed=10**6,
    )(at, everything, exy, ezs)
    nv = jnp.swapaxes(nv.reshape(2, 3, 2, 16, 32), 3, 4)
    return nv, field.reshape(2, 3, 16, 32, 128)


def solution(mesh):
    placed = (P(None, "gx", "gy", "gz"), P(None, None, "gx", None, "gz"))
    return jax.shard_map(
        shards,
        mesh=mesh,
        in_specs=placed,
        out_specs=(P(None, None, "gx", None, "gz"), P(None, None, "gx", "gy", "gz")),
        check_vma=False,
    )
```

```python
import functools

import jax
import jax.numpy as jnp
import numpy as np
from jax import lax
from jax.experimental import pallas as pl
from jax.experimental.pallas import tpu as pltpu
from jax.sharding import PartitionSpec as P

epsilon_value = 1e-05
step_size = 0.5
f32 = jnp.float32
bf16 = jnp.bfloat16


def spline(t):
    m = np.abs(t)
    inside = 2.0 / 3.0 - m * m + 0.5 * m * m * m
    out = np.maximum(2.0 - m, 0.0)
    return np.where(m < 1.0, inside, out * out * out / 6.0)


def split_two(w):
    hi = w.astype(np.float32).astype(jnp.bfloat16)
    lo = (w - hi.astype(np.float64)).astype(np.float32).astype(jnp.bfloat16)
    return hi, lo


def pack_kernel(img_ref, out_ref, buf_ref, sems):
    lane = lax.broadcasted_iota(jnp.int32, (32, 128), 1)
    copies = []
    for n in range(4):
        for h in range(2):
            planes = pl.ds(4 * n, 4)
            copy = pltpu.make_async_copy(img_ref.at[h, planes], buf_ref.at[h, planes], sems.at[2 * n + h])
            copy.start()
            copies.append(copy)
    packed = [jnp.zeros((32, 128), f32) for _ in range(2)]
    for n in range(4):
        for h in range(2):
            copies[2 * n + h].wait()
            for t in range(4 * n, 4 * n + 4):
                moved = pltpu.roll(buf_ref[h, t], (8 * t + 8) % 128, 1)
                packed[h] = jnp.where((lane >= 8 * t) & (lane < 8 * t + 8), moved, packed[h])
    for h in range(2):
        out_ref[h] = packed[h]


def slab_kernel(img_ref, x_ref, y_ref, xy_ref):
    for h in range(2):
        for t in range(16):
            y_ref[h, t] = img_ref[h, t, 24:32]
            if t >= 8:
                x_ref[h, t - 8] = img_ref[h, t]
                xy_ref[h, t - 8] = img_ref[h, t, 24:32]
        y_ref[h, 16] = jnp.zeros((8, 128), f32)
        xy_ref[h, 8] = jnp.zeros((8, 128), f32)


def spline_at(t):
    m = jnp.abs(t)
    inside = 2.0 / 3.0 - m * m + 0.5 * m * m * m
    out = jnp.maximum(2.0 - m, 0.0)
    return jnp.where(m < 1.0, inside, out * out * out / 6.0)


def weights(voxel, point):
    return spline_at((voxel.astype(f32) - 8.0 * point.astype(f32) - 3.5) * 0.125)


def prep_kernel(at_ref, vel_ref, vel_out, wxy_out, wz_out, xsum_out, zsum_out, rows_ref):
    i = at_ref[0]
    j = at_ref[1]
    k = at_ref[2]
    ex = jnp.where(i == 0, 0.0, 1.0)
    ez = jnp.where(k == 0, 0.0, 1.0)
    row = lax.broadcasted_iota(jnp.int32, (40, 512), 0)
    col = lax.broadcasted_iota(jnp.int32, (40, 512), 1)
    p = lax.shift_right_logical(row, 3)
    q = row & 7
    o = lax.shift_right_logical(col, 5)
    r = col & 31
    ok = ((p < 2) == (o < 4)) | (i != 0)
    ok = ok & (((q < 2) == (r < 4)) | (j != 0)) & (q < 7)
    ok = ok & ((p < 4) | (i != at_ref[3] - 1)) & ((q < 6) | (j != at_ref[4] - 1))
    table = jnp.where(ok, weights(o - 4, p - 2) * weights(r - 4, q - 2), 0.0)
    hi, lo = split2(table)
    wxy_out[...] = jnp.concatenate([hi.astype(f32), lo.astype(f32)], axis=0).astype(bf16)
    lane = lax.broadcasted_iota(jnp.int32, (128, 128), 1)
    sub = lax.broadcasted_iota(jnp.int32, (128, 128), 0)
    spot = lax.rem(lane, 20)
    ok = ((spot < 2) == (sub >= 124)) | (k != 0)
    ok = ok & (spot < 19) & ((spot < 18) | (k != at_ref[5] - 1))
    voxel = jnp.where(sub >= 124, sub - 128, sub)
    hi, lo = split2(jnp.where(ok, weights(voxel, spot - 2), 0.0))
    wz_out[...] = jnp.concatenate([hi, lo], axis=1)

    src = lax.broadcasted_iota(jnp.int32, (256, 128), 0)
    dst = lax.broadcasted_iota(jnp.int32, (256, 128), 1)
    plane = jnp.where(src < 128, lax.shift_right_logical(src, 3) + 8, lax.shift_right_logical(src - 128, 3) - 8)
    goal = lax.shift_right_logical(dst, 3)
    near = (plane >= goal) & (plane <= goal + 8) & ((src & 7) == (dst & 7)) & (plane >= 0)
    across = (plane < 8) != (goal < 4)
    xsum_out[...] = jnp.where(near, jnp.where(across, ex, 1.0), 0.0).astype(bf16)
    centre = jnp.where(dst < 124, dst, dst - 128)
    below = src >= 128
    place = jnp.where(below, (src & 7) - 8, src)
    gap = place - centre
    inside = (gap <= 4) & (gap >= -4)
    crossing = below != (dst >= 124)
    zsum_out[...] = jnp.where(inside, jnp.where(crossing, ez, 1.0), 0.0)

    pick_q = lax.broadcasted_iota(jnp.int32, (8, 32), 0)
    pick_y = lax.broadcasted_iota(jnp.int32, (8, 32), 1)
    pick = ((pick_y == 4 * j + pick_q - 2) & (pick_q >= 2) & (pick_q < 6)).astype(f32).astype(bf16)
    for side in range(2):
        rows_ref[...] = jnp.zeros((128, 32), f32)
        for c in range(6):
            rows_ref[20 * c + 2 : 20 * c + 18] = vel_ref[c, side]
        turned = jnp.transpose(rows_ref[...])
        total = jnp.zeros((8, 128), f32)
        for piece in split3(turned):
            total = total + dot(pick, piece)
        vel_out[8 * side : 8 * side + 8] = total


def split3(v):
    hi = v.astype(bf16)
    r = v - hi.astype(f32)
    mid = r.astype(bf16)
    lo = (r - mid.astype(f32)).astype(bf16)
    return hi, mid, lo


def split2(v):
    hi = v.astype(bf16)
    return hi, (v - hi.astype(f32)).astype(bf16)


def dot(a, b):
    return jnp.dot(a, b, preferred_element_type=f32)


def up_by(v, n, row):
    size = v.shape[0]
    return jnp.where(row < size - n, pltpu.roll(v, size - n, 0), 0.0)


def rows_window(v, head, tail, row8):
    first = v[0:8]
    own = jnp.concatenate([jnp.zeros((8, 128), f32), v[8:40]], axis=0)
    s = first + up_by(first, 1, row8)
    s = s + up_by(s, 2, row8)
    s = s + up_by(s, 4, row8)
    w = own + pltpu.roll(own, 39, 0)
    w = w + pltpu.roll(w, 38, 0)
    w = w + pltpu.roll(w, 36, 0)
    w = w[0:32] + own[8:40]
    top = head * s + tail * w[0:8]
    return jnp.concatenate([top, w[8:32]], axis=0)


def force_kernel(upper, at_ref, own_ref, zr_ref, yr_ref, *refs):
    if upper:
        base_ref, *refs = refs
    else:
        xr_ref, xzr_ref, xyr_ref, base_ref, *refs = refs
    wxy_ref, wz_ref, xsum_ref, zsum_ref, out_ref, a_ref, h_ref, v_ref, dz_ref, xs_ref, hs_ref, fh_ref, fl_ref = refs
    first = 8 if upper else 0
    ex, ey, ez = (jnp.where(at_ref[n] == 0, 0.0, 1.0) for n in range(3))
    row8 = lax.broadcasted_iota(jnp.int32, (8, 128), 0)
    row32 = lax.broadcasted_iota(jnp.int32, (32, 128), 0)
    lane40 = lax.broadcasted_iota(jnp.int32, (40, 128), 1)
    head = jnp.where(row8 < 4, 1.0, ey)
    tail = jnp.where(row8 < 4, ey, 1.0)

    for h in range(2):
        for n in range(16):
            if upper or n >= 8:
                t = n if upper else n - 8
                a_ref[h, n, 8:40] = own_ref[h, t]
                a_ref[h, n, 0:8] = yr_ref[h, t]
            else:
                a_ref[h, n, 8:40] = xr_ref[h, n]
                a_ref[h, n, 0:8] = xyr_ref[h, n]
        h_ref[h, 0, 8:40] = zr_ref[h]
        h_ref[h, 0, 0:8] = yr_ref[h, 16]
        if not upper:
            h_ref[h, 1, 8:40] = xzr_ref[h]
            h_ref[h, 1, 0:8] = xyr_ref[h, 8]

    plus_z = jnp.where(lane40 == 127, ez, 1.0)
    minus_z = jnp.where(lane40 == 0, ez, 1.0)
    for h in range(2):
        for n in range(3, 13):
            l = n + first
            if l >= 8:
                halo = pltpu.roll(h_ref[h, 0], (120 - 8 * (l - 8)) % 128, 1)
            else:
                halo = pltpu.roll(h_ref[h, 1], (120 - 8 * (l + 8)) % 128, 1)
            v_ref[h, n - 3] = jnp.where(lane40 >= 124, halo, a_ref[h, n])
            if 4 <= n < 12:
                dz_ref[h, n - 4] = halo
    for h in range(2):
        for n in range(4, 12):
            a = a_ref[h, n]
            halo = dz_ref[h, n - 4]
            up = pltpu.roll(jnp.where(lane40 >= 125, halo, a), 127, 1)
            down = pltpu.roll(jnp.where(lane40 >= 123, halo, a), 1, 1)
            dz_ref[h, n - 4] = plus_z * up - minus_z * down

    def x_step(tile, carry):
        rows = pl.ds(pl.multiple_of(tile * 8, 8), 8)
        for q in range(5):
            p = []
            for n in range(16):
                if q == 4:
                    p.append(a_ref[0, n, rows] * a_ref[1, n, rows])
                else:
                    value = a_ref[q % 2, n, rows]
                    p.append(value if q < 2 else value * value)
            if upper:
                b = [p[n] + p[n + 1] for n in range(15)]
                b = [b[n] + b[n + 2] for n in range(13)]
                b = [b[n] + b[n + 4] for n in range(9)]
                for o in range(8):
                    xs_ref[q, o, rows] = b[o] + p[o + 8]
                continue
            left = [None] * 8
            left[7] = p[7]
            for o in range(6, -1, -1):
                left[o] = left[o + 1] + p[o]
            right = p[8]
            for o in range(8):
                if o > 0:
                    right = right + p[o + 8]
                xs_ref[q, o, rows] = left[o] + ex * right if o < 4 else ex * left[o] + right
        return carry

    lax.fori_loop(0, 5, x_step, 0)

    sides = 1 if upper else 2
    x_sum = xsum_ref[0 : 128 * sides]
    for q in range(5):
        parts = []
        for side in range(sides):
            f = h_ref[0, side]
            m = h_ref[1, side]
            value = (f, m, f * f, m * m, f * m)[q]
            parts.append(rows_window(value, head, tail, row8))
        total = jnp.zeros((32, 128), f32)
        for piece in split3(jnp.concatenate(parts, axis=1)):
            total = total + dot(piece, x_sum)
        for n, piece in enumerate(split3(total)):
            hs_ref[q, n] = piece

    from_row = lax.broadcasted_iota(jnp.int32, (256, 128), 0)
    plus_y = jnp.where(row32 == 3, ey, 1.0)
    minus_y = jnp.where(row32 == 4, ey, 1.0)

    def o_step(o, carry):
        mine = (from_row < 128) | (lax.shift_right_logical(from_row - 128, 3) == o + first)
        z_sum = jnp.where(mine, zsum_ref[...], 0.0).astype(bf16)
        pieces = [[], [], []]
        for q in range(5):
            y = rows_window(xs_ref[q, o], head, tail, row8)
            for n, piece in enumerate(split3(y)):
                pieces[n].append(jnp.concatenate([piece, hs_ref[q, n]], axis=1))
        big = dot(jnp.concatenate(pieces[0] + pieces[1] + pieces[2], axis=0), z_sum)
        sums = (big[0:160] + big[160:320]) + big[320:480]
        sums = sums * (1.0 / 729.0)
        mean_f = sums[0:32]
        mean_m = sums[32:64]
        var_f = sums[64:96] - mean_f * mean_f + epsilon_value
        var_m = sums[96:128] - mean_m * mean_m + epsilon_value
        cov = sums[128:160] - mean_f * mean_m
        off_f = v_ref[0, o + 1, 4:36] - mean_f
        off_m = v_ref[1, o + 1, 4:36] - mean_m
        inv = 1.0 / (var_f * var_m)
        factor = cov * inv
        pulls = (
            factor * (off_m - factor * var_m * off_f),
            factor * (off_f - factor * var_f * off_m),
        )
        plus_x = jnp.where(o + first == 3, ex, 1.0)
        minus_x = jnp.where(o + first == 4, ex, 1.0)
        where_to = pl.ds(pl.multiple_of(o * 32, 32), 32)
        for h in range(2):
            dx = plus_x * v_ref[h, o + 2, 4:36] - minus_x * v_ref[h, o, 4:36]
            dy = plus_y * v_ref[h, o + 1, 5:37] - minus_y * v_ref[h, o + 1, 3:35]
            dz = dz_ref[h, o, 4:36]
            for c, d in enumerate((dx, dy, dz)):
                hi, lo = split2(pulls[h] * d)
                fh_ref[3 * h + c, where_to] = hi
                fl_ref[3 * h + c, where_to] = lo
        return carry

    lax.fori_loop(0, 8, o_step, 0, unroll=8)

    cols = slice(32 * first, 32 * first + 256)
    wxy = wxy_ref[:, cols]
    wxy_hi = wxy_ref[0:40, cols]
    planes = []
    for c in range(6):
        one = dot(wxy, fh_ref[c])
        planes.append(one[0:40] + one[40:80] + dot(wxy_hi, fl_ref[c]))
    hi, lo = split2(jnp.concatenate(planes, axis=0))
    along = dot(jnp.concatenate([hi, lo], axis=0), wz_ref[...])
    along = (along[0:240, 0:128] + along[0:240, 128:256]) + along[240:480, 0:128]
    which = lax.div(lax.broadcasted_iota(jnp.int32, (40, 128), 1), 20)
    total = jnp.zeros((40, 128), f32)
    for c in range(6):
        total = total + jnp.where(which == c, along[40 * c : 40 * c + 40], 0.0)
    total = step_size * total
    if upper:
        out_ref[0:16] = total[0:16]
        out_ref[16:32] = total[16:32] + base_ref[...]
        out_ref[32:40] = total[32:40]
    else:
        out_ref[...] = total + base_ref[...]


def fold_kernel(at_ref, mine_ref, chip_ref, core_ref, out_ref):
    lane = lax.broadcasted_iota(jnp.int32, (40, 128), 1)
    spot = lax.rem(lane, 20)
    live = lane < 120
    odd = (at_ref[2] & 1) == 1
    chip, core = chip_ref[...], core_ref[...]
    low = pltpu.roll(jnp.where(odd, core, chip), 112, 1)
    high = pltpu.roll(jnp.where(odd, chip, core), 16, 1)
    total = mine_ref[...]
    total = total + jnp.where(live & (spot < 3), low, 0.0)
    out_ref[...] = total + jnp.where(live & (spot >= 16), high, 0.0)


def across_kernel(at_ref, own_ref, one_ref, two_ref, far_ref, out_ref):
    odd = (at_ref[0] & 1) == 1
    tiles = lambda ref: [ref[8 * p : 8 * p + 8] for p in range(5)]
    own, one, two, far = tiles(own_ref), tiles(one_ref), tiles(two_ref), tiles(far_ref)
    below = [jnp.where(odd, a, b) for a, b in zip(one, two)]
    above = [jnp.where(odd, b, a) for a, b in zip(one, two)]
    window = [
        own[0] + below[2] + far[4],
        own[1] + below[3],
        own[2] + below[4] + above[0],
        own[3] + above[1],
        own[4] + above[2] + far[0],
        above[3] + far[1],
    ]
    for n in range(8):
        for w in range(6):
            out_ref[n, 8 * w : 8 * w + 8] = window[w]


def field_kernel(at_ref, g_ref, wxy_ref, wz_ref, nv_ref, field_ref, rows_ref, buf_ref, sems):
    me_j = at_ref[1]
    row8 = lax.broadcasted_iota(jnp.int32, (8, 128), 0)

    window = []
    js = [lax.rem(me_j + 7, 8), me_j, lax.rem(me_j + 1, 8)]
    for w in range(6):
        before, own, after = (g_ref[j, 8 * w : 8 * w + 8] for j in js)
        window.append(own + jnp.where(row8 < 4, pltpu.roll(before, 4, 0), pltpu.roll(after, 4, 0)))
    coefs = jnp.concatenate(window, axis=0)
    row = lax.broadcasted_iota(jnp.int32, (48, 128), 0)
    lane = lax.broadcasted_iota(jnp.int32, (48, 128), 1)
    at_x = 2 * at_ref[0] - 2 + lax.shift_right_logical(row, 3)
    at_y = 4 * me_j - 2 + (row & 7)
    at_z = 16 * at_ref[2] - 2 + lax.rem(lane, 20)
    real = (at_x >= 0) & (at_x < 2 * at_ref[3]) & (at_y >= 0) & (at_y < 4 * at_ref[4])
    real = real & (at_z >= 0) & (at_z < 16 * at_ref[5]) & (lane < 120)
    part = lax.div(lane, 20)
    coefs = jnp.where(real, coefs, 0.0)
    hi, lo = split2(jnp.concatenate([jnp.where(part == c, coefs, 0.0) for c in range(6)], axis=0))
    along = dot(jnp.concatenate([hi, lo], axis=0), wz_ref[...])
    along = (along[0:288, 0:128] + along[0:288, 128:256]) + along[288:576, 0:128]
    ch, cl = split2(along)
    copies = []
    for pair in range(3):
        rhs = []
        for c in (2 * pair, 2 * pair + 1):
            rows = slice(48 * c, 48 * c + 48)
            rhs.append(jnp.concatenate([ch[rows], cl[rows], ch[rows]], axis=0))
        both = dot(wxy_ref[...], jnp.concatenate(rhs, axis=1)).astype(bf16)
        for n in range(2):
            buf_ref[2 * pair + n] = both[:, 128 * n : 128 * n + 128]
        there = pl.ds(2 * pair, 2)
        copy = pltpu.make_async_copy(buf_ref.at[there], field_ref.at[there], sems.at[pair])
        copy.start()
        copies.append(copy)

    for side in range(2):
        cols = [g_ref[j, 16 + 8 * side : 24 + 8 * side] for j in range(8)]
        turned = [pltpu.roll(c, 4, 0) for c in cols]
        tiles = []
        zero = jnp.zeros((8, 128), f32)
        for n in range(5):
            even = cols[2 * n] if n < 4 else zero
            high = turned[2 * n + 1] if n < 4 else zero
            low = turned[2 * n - 1] if n > 0 else zero
            tiles.append(even + jnp.where(row8 < 4, low, high))
        tiles[4] = tiles[4] + tiles[0]
        for n in range(5):
            rows_ref[side, 8 * n : 8 * n + 8] = tiles[n]
        block = jnp.transpose(rows_ref[side, 2:34])
        for c in range(6):
            nv_ref[c, side] = block[20 * c + 2 : 20 * c + 18]
    for copy in copies:
        copy.wait()


VMEM = pl.BlockSpec(memory_space=pltpu.VMEM)
SMEM = pl.BlockSpec(memory_space=pltpu.SMEM)


HBM = pl.BlockSpec(memory_space=pltpu.HBM)


def call(body, out_shape, in_specs, scratch=(), out_specs=None, vmem=48 << 20, flops=0, bytes_accessed=0):
    return pl.pallas_call(
        body,
        out_shape=[jax.ShapeDtypeStruct(shape, dtype) for shape, dtype in out_shape],
        in_specs=in_specs,
        out_specs=out_specs or [VMEM] * len(out_shape),
        scratch_shapes=list(scratch),
        compiler_params=pltpu.CompilerParams(vmem_limit_bytes=vmem),
        cost_estimate=pl.CostEstimate(flops=flops, bytes_accessed=bytes_accessed, transcendentals=0),
    )


def pairs(mesh_sizes, di, dj, dk):
    ni, nj, nk = mesh_sizes
    out = []
    for i in range(ni):
        for j in range(nj):
            for k in range(nk):
                to = (((i + di) % ni) * nj + (j + dj) % nj) * nk + (k + dk) % nk
                out.append(((i * nj + j) * nk + k, to))
    return out


def fixed_tables():
    weight = lambda n, points: spline((np.arange(n)[None, :] - 8.0 * (np.arange(points) - 2)[:, None] - 3.5) / 8.0)
    ex, ey, ez = (weight(n, points) for n, points in ((16, 6), (32, 8), (128, 20)))
    hi, lo = split_two(np.einsum("px,qy->xypq", ex, ey).reshape(512, 48))
    exy = np.concatenate([hi, hi, lo], axis=1)
    padded = lambda part: np.concatenate([np.tile(part, (6, 1)), np.zeros((8, 128), part.dtype)])
    return exy, np.concatenate([padded(part) for part in split_two(ez)], axis=1)


def shards(images, velocity):
    axes = ("gx", "gy", "gz")
    sizes = tuple(lax.axis_size(a) for a in axes)
    spot = [lax.axis_index(a) for a in axes]
    nk = sizes[2]
    at = jnp.stack([jnp.int32(v) for v in (*spot, *sizes)])
    exy, ezs = fixed_tables()

    def send(v, di, dj, dk):
        return lax.ppermute(v, axes, pairs(sizes, di, dj, dk))

    (pack,) = call(
        pack_kernel,
        [((2, 32, 128), f32)],
        [HBM],
        [pltpu.VMEM((2, 16, 32, 128), f32), pltpu.SemaphoreType.DMA((8,))],
        vmem=60 << 20,
        bytes_accessed=6 * 10**5,
    )(images)
    to_x, to_y, to_xy = call(
        slab_kernel,
        [((2, 8, 32, 128), f32), ((2, 17, 8, 128), f32), ((2, 9, 8, 128), f32)],
        [VMEM],
        bytes_accessed=10**6,
    )(images)
    zr = lax.ppermute(pack, "gz", [(n, (n + 1) % nk) for n in range(nk)])
    velocity = jnp.swapaxes(velocity, 3, 4).reshape(6, 2, 16, 32)
    vel, wxy, wzs, xsum, zsum = call(
        prep_kernel,
        [((16, 128), f32), ((80, 512), bf16), ((128, 256), bf16), ((256, 128), bf16), ((256, 128), f32)],
        [SMEM, VMEM],
        [pltpu.VMEM((128, 32), f32)],
        bytes_accessed=10**6,
    )(at, velocity)
    zr, vel = lax.optimization_barrier((zr, vel))
    xr = send(to_x, 1, 0, 0)
    yr = send(to_y.at[:, 16].set(zr[:, 24:]), 0, 1, 0)
    xyr = send(to_xy.at[:, 8].set(zr[:, 24:]), 1, 1, 0)
    xzr = send(zr, 1, 0, 0)

    def forces(upper, *arrays):
        return call(
            functools.partial(force_kernel, upper),
            [((40, 128), f32)],
            [SMEM] + [VMEM] * (len(arrays) + 4),
            [
                pltpu.VMEM((2, 16, 40, 128), f32),
                pltpu.VMEM((2, 2, 40, 128), f32),
                pltpu.VMEM((2, 10, 40, 128), f32),
                pltpu.VMEM((2, 8, 40, 128), f32),
                pltpu.VMEM((5, 8, 40, 128), f32),
                pltpu.VMEM((5, 3, 32, 128), bf16),
                pltpu.VMEM((6, 256, 128), bf16),
                pltpu.VMEM((6, 256, 128), bf16),
            ],
            flops=5 * 10**8,
            bytes_accessed=10**6,
        )(at, *arrays, wxy, wzs, xsum, zsum)[0]

    part = forces(True, images, zr, yr, vel)
    part = forces(False, images, zr, yr, xr, xzr, xyr, part)

    swap = lambda v, axis, couples: lax.ppermute(v, axis, couples + [(b, a) for a, b in couples])
    chip = swap(part, "gz", [(1, 2), (3, 0)])
    core = swap(part, "gz", [(0, 1), (2, 3)])
    (own,) = call(fold_kernel, [((40, 128), f32)], [SMEM] + [VMEM] * 3)(at, part, chip, core)
    far = swap(own, "gx", [(0, 2), (1, 3)])
    one = swap(own, "gx", [(0, 1), (2, 3)])
    two = swap(own, "gx", [(1, 2), (3, 0)])
    (copies,) = call(across_kernel, [((8, 48, 128), f32)], [SMEM] + [VMEM] * 4)(at, own, one, two, far)
    everything = lax.all_to_all(copies, "gy", 0, 0, tiled=True)

    nv, field = call(
        field_kernel,
        [((6, 2, 16, 32), f32), ((6, 512, 128), bf16)],
        [SMEM] + [VMEM] * 3,
        [pltpu.VMEM((2, 40, 128), f32), pltpu.VMEM((6, 512, 128), bf16), pltpu.SemaphoreType.DMA((3,))],
        out_specs=[VMEM, HBM],
        flops=10**8,
        bytes_accessed=10**6,
    )(at, everything, exy, ezs)
    nv = jnp.swapaxes(nv.reshape(2, 3, 2, 16, 32), 3, 4)
    return nv, field.reshape(2, 3, 16, 32, 128)


def solution(mesh):
    placed = (P(None, "gx", "gy", "gz"), P(None, None, "gx", None, "gz"))
    return jax.shard_map(
        shards,
        mesh=mesh,
        in_specs=placed,
        out_specs=(P(None, None, "gx", None, "gz"), P(None, None, "gx", "gy", "gz")),
        check_vma=False,
    )
```

```python
import functools

import jax
import jax.numpy as jnp
import numpy as np
from jax import lax
from jax.experimental import pallas as pl
from jax.experimental.pallas import tpu as pltpu
from jax.sharding import PartitionSpec as P

epsilon_value = 1e-05
step_size = 0.5
AXES = ("gx", "gy", "gz")
f32 = jnp.float32
bf16 = jnp.bfloat16


def spline(t):
    m = np.abs(t)
    inside = 2.0 / 3.0 - m * m + 0.5 * m * m * m
    out = np.maximum(2.0 - m, 0.0)
    return np.where(m < 1.0, inside, out * out * out / 6.0)


def split_two(w):
    hi = w.astype(np.float32).astype(jnp.bfloat16)
    lo = (w - hi.astype(np.float64)).astype(np.float32).astype(jnp.bfloat16)
    return hi, lo


def pack_kernel(img_ref, out_ref):
    lane = lax.broadcasted_iota(jnp.int32, (32, 128), 1)
    for h in range(2):
        packed = jnp.zeros((32, 128), f32)
        for t in range(16):
            moved = pltpu.roll(img_ref[h, t], (8 * t + 8) % 128, 1)
            packed = jnp.where((lane >= 8 * t) & (lane < 8 * t + 8), moved, packed)
        out_ref[h] = packed


def slab_kernel(img_ref, x_ref, y_ref, xy_ref):
    for h in range(2):
        for t in range(16):
            y_ref[h, t] = img_ref[h, t, 24:32]
            if t >= 8:
                x_ref[h, t - 8] = img_ref[h, t]
                xy_ref[h, t - 8] = img_ref[h, t, 24:32]
        y_ref[h, 16] = jnp.zeros((8, 128), f32)
        xy_ref[h, 8] = jnp.zeros((8, 128), f32)


def spline_at(t):
    m = jnp.abs(t)
    inside = 2.0 / 3.0 - m * m + 0.5 * m * m * m
    out = jnp.maximum(2.0 - m, 0.0)
    return jnp.where(m < 1.0, inside, out * out * out / 6.0)


def weights(voxel, point):
    return spline_at((voxel.astype(f32) - 8.0 * point.astype(f32) - 3.5) * 0.125)


def prep_kernel(vel_ref, vel_out, wxy_out, wz_out, xsum_out, zsum_out, rows_ref):
    i, j, k = coords()
    ni, nj, nk = (lax.axis_size(a) for a in AXES)
    ex = jnp.where(i == 0, 0.0, 1.0)
    ez = jnp.where(k == 0, 0.0, 1.0)
    row = lax.broadcasted_iota(jnp.int32, (40, 512), 0)
    col = lax.broadcasted_iota(jnp.int32, (40, 512), 1)
    p = lax.shift_right_logical(row, 3)
    q = row & 7
    o = lax.shift_right_logical(col, 5)
    r = col & 31
    ok = ((p < 2) == (o < 4)) | (i != 0)
    ok = ok & (((q < 2) == (r < 4)) | (j != 0)) & (q < 7)
    ok = ok & ((p < 4) | (i != ni - 1)) & ((q < 6) | (j != nj - 1))
    table = jnp.where(ok, weights(o - 4, p - 2) * weights(r - 4, q - 2), 0.0)
    hi, lo = split2(table)
    wxy_out[...] = jnp.concatenate([hi.astype(f32), lo.astype(f32)], axis=0).astype(bf16)
    lane = lax.broadcasted_iota(jnp.int32, (128, 128), 1)
    sub = lax.broadcasted_iota(jnp.int32, (128, 128), 0)
    spot = lax.rem(lane, 20)
    ok = ((spot < 2) == (sub >= 124)) | (k != 0)
    ok = ok & (spot < 19) & ((spot < 18) | (k != nk - 1))
    voxel = jnp.where(sub >= 124, sub - 128, sub)
    hi, lo = split2(jnp.where(ok, weights(voxel, spot - 2), 0.0))
    wz_out[...] = jnp.concatenate([hi, lo], axis=1)

    src = lax.broadcasted_iota(jnp.int32, (256, 128), 0)
    dst = lax.broadcasted_iota(jnp.int32, (256, 128), 1)
    plane = jnp.where(src < 128, lax.shift_right_logical(src, 3) + 8, lax.shift_right_logical(src - 128, 3) - 8)
    goal = lax.shift_right_logical(dst, 3)
    near = (plane >= goal) & (plane <= goal + 8) & ((src & 7) == (dst & 7)) & (plane >= 0)
    across = (plane < 8) != (goal < 4)
    xsum_out[...] = jnp.where(near, jnp.where(across, ex, 1.0), 0.0).astype(bf16)
    centre = jnp.where(dst < 124, dst, dst - 128)
    below = src >= 128
    place = jnp.where(below, (src & 7) - 8, src)
    gap = place - centre
    inside = (gap <= 4) & (gap >= -4)
    crossing = below != (dst >= 124)
    zsum_out[...] = jnp.where(inside, jnp.where(crossing, ez, 1.0), 0.0)

    pick_q = lax.broadcasted_iota(jnp.int32, (8, 32), 0)
    pick_y = lax.broadcasted_iota(jnp.int32, (8, 32), 1)
    pick = ((pick_y == 4 * j + pick_q - 2) & (pick_q >= 2) & (pick_q < 6)).astype(f32).astype(bf16)
    for side in range(2):
        rows_ref[...] = jnp.zeros((128, 32), f32)
        for c in range(6):
            rows_ref[20 * c + 2 : 20 * c + 18] = vel_ref[c, side]
        turned = jnp.transpose(rows_ref[...])
        total = jnp.zeros((8, 128), f32)
        for piece in split3(turned):
            total = total + dot(pick, piece)
        vel_out[8 * side : 8 * side + 8] = total


def coords():
    return tuple(lax.axis_index(a) for a in AXES)


def split3(v):
    hi = v.astype(bf16)
    r = v - hi.astype(f32)
    mid = r.astype(bf16)
    lo = (r - mid.astype(f32)).astype(bf16)
    return hi, mid, lo


def split2(v):
    hi = v.astype(bf16)
    return hi, (v - hi.astype(f32)).astype(bf16)


def dot(a, b):
    return jnp.dot(a, b, preferred_element_type=f32)


def up_by(v, n, row):
    size = v.shape[0]
    return jnp.where(row < size - n, pltpu.roll(v, size - n, 0), 0.0)


def rows_window(v, head, tail, row8):
    first = v[0:8]
    own = jnp.concatenate([jnp.zeros((8, 128), f32), v[8:40]], axis=0)
    s = first + up_by(first, 1, row8)
    s = s + up_by(s, 2, row8)
    s = s + up_by(s, 4, row8)
    w = own + pltpu.roll(own, 39, 0)
    w = w + pltpu.roll(w, 38, 0)
    w = w + pltpu.roll(w, 36, 0)
    w = w[0:32] + own[8:40]
    top = head * s + tail * w[0:8]
    return jnp.concatenate([top, w[8:32]], axis=0)


def force_kernel(upper, own_ref, zr_ref, yr_ref, *refs):
    if upper:
        base_ref, *refs = refs
    else:
        xr_ref, xzr_ref, xyr_ref, base_ref, *refs = refs
    wxy_ref, wz_ref, xsum_ref, zsum_ref, out_ref, a_ref, h_ref, v_ref, dz_ref, xs_ref, hs_ref, fh_ref, fl_ref = refs
    first = 8 if upper else 0
    ex, ey, ez = (jnp.where(at == 0, 0.0, 1.0) for at in coords())
    row8 = lax.broadcasted_iota(jnp.int32, (8, 128), 0)
    row32 = lax.broadcasted_iota(jnp.int32, (32, 128), 0)
    lane40 = lax.broadcasted_iota(jnp.int32, (40, 128), 1)
    head = jnp.where(row8 < 4, 1.0, ey)
    tail = jnp.where(row8 < 4, ey, 1.0)

    for h in range(2):
        for n in range(16):
            if upper or n >= 8:
                t = n if upper else n - 8
                a_ref[h, n, 8:40] = own_ref[h, t]
                a_ref[h, n, 0:8] = yr_ref[h, t]
            else:
                a_ref[h, n, 8:40] = xr_ref[h, n]
                a_ref[h, n, 0:8] = xyr_ref[h, n]
        h_ref[h, 0, 8:40] = zr_ref[h]
        h_ref[h, 0, 0:8] = yr_ref[h, 16]
        if not upper:
            h_ref[h, 1, 8:40] = xzr_ref[h]
            h_ref[h, 1, 0:8] = xyr_ref[h, 8]

    plus_z = jnp.where(lane40 == 127, ez, 1.0)
    minus_z = jnp.where(lane40 == 0, ez, 1.0)
    for h in range(2):
        for n in range(3, 13):
            l = n + first
            if l >= 8:
                halo = pltpu.roll(h_ref[h, 0], (120 - 8 * (l - 8)) % 128, 1)
            else:
                halo = pltpu.roll(h_ref[h, 1], (120 - 8 * (l + 8)) % 128, 1)
            v_ref[h, n - 3] = jnp.where(lane40 >= 124, halo, a_ref[h, n])
            if 4 <= n < 12:
                dz_ref[h, n - 4] = halo
    for h in range(2):
        for n in range(4, 12):
            a = a_ref[h, n]
            halo = dz_ref[h, n - 4]
            up = pltpu.roll(jnp.where(lane40 >= 125, halo, a), 127, 1)
            down = pltpu.roll(jnp.where(lane40 >= 123, halo, a), 1, 1)
            dz_ref[h, n - 4] = plus_z * up - minus_z * down

    def x_step(tile, carry):
        rows = pl.ds(pl.multiple_of(tile * 8, 8), 8)
        for q in range(5):
            p = []
            for n in range(16):
                if q == 4:
                    p.append(a_ref[0, n, rows] * a_ref[1, n, rows])
                else:
                    value = a_ref[q % 2, n, rows]
                    p.append(value if q < 2 else value * value)
            if upper:
                b = [p[n] + p[n + 1] for n in range(15)]
                b = [b[n] + b[n + 2] for n in range(13)]
                b = [b[n] + b[n + 4] for n in range(9)]
                for o in range(8):
                    xs_ref[q, o, rows] = b[o] + p[o + 8]
                continue
            left = [None] * 8
            left[7] = p[7]
            for o in range(6, -1, -1):
                left[o] = left[o + 1] + p[o]
            right = p[8]
            for o in range(8):
                if o > 0:
                    right = right + p[o + 8]
                xs_ref[q, o, rows] = left[o] + ex * right if o < 4 else ex * left[o] + right
        return carry

    lax.fori_loop(0, 5, x_step, 0)

    sides = 1 if upper else 2
    x_sum = xsum_ref[0 : 128 * sides]
    for q in range(5):
        parts = []
        for side in range(sides):
            f = h_ref[0, side]
            m = h_ref[1, side]
            value = (f, m, f * f, m * m, f * m)[q]
            parts.append(rows_window(value, head, tail, row8))
        total = jnp.zeros((32, 128), f32)
        for piece in split3(jnp.concatenate(parts, axis=1)):
            total = total + dot(piece, x_sum)
        for n, piece in enumerate(split3(total)):
            hs_ref[q, n] = piece

    from_row = lax.broadcasted_iota(jnp.int32, (256, 128), 0)
    plus_y = jnp.where(row32 == 3, ey, 1.0)
    minus_y = jnp.where(row32 == 4, ey, 1.0)

    def o_step(o, carry):
        mine = (from_row < 128) | (lax.shift_right_logical(from_row - 128, 3) == o + first)
        z_sum = jnp.where(mine, zsum_ref[...], 0.0).astype(bf16)
        pieces = [[], [], []]
        for q in range(5):
            y = rows_window(xs_ref[q, o], head, tail, row8)
            for n, piece in enumerate(split3(y)):
                pieces[n].append(jnp.concatenate([piece, hs_ref[q, n]], axis=1))
        big = dot(jnp.concatenate(pieces[0] + pieces[1] + pieces[2], axis=0), z_sum)
        sums = (big[0:160] + big[160:320]) + big[320:480]
        sums = sums * (1.0 / 729.0)
        mean_f = sums[0:32]
        mean_m = sums[32:64]
        var_f = sums[64:96] - mean_f * mean_f + epsilon_value
        var_m = sums[96:128] - mean_m * mean_m + epsilon_value
        cov = sums[128:160] - mean_f * mean_m
        off_f = v_ref[0, o + 1, 4:36] - mean_f
        off_m = v_ref[1, o + 1, 4:36] - mean_m
        inv = 1.0 / (var_f * var_m)
        factor = cov * inv
        pulls = (
            factor * (off_m - factor * var_m * off_f),
            factor * (off_f - factor * var_f * off_m),
        )
        plus_x = jnp.where(o + first == 3, ex, 1.0)
        minus_x = jnp.where(o + first == 4, ex, 1.0)
        where_to = pl.ds(pl.multiple_of(o * 32, 32), 32)
        for h in range(2):
            dx = plus_x * v_ref[h, o + 2, 4:36] - minus_x * v_ref[h, o, 4:36]
            dy = plus_y * v_ref[h, o + 1, 5:37] - minus_y * v_ref[h, o + 1, 3:35]
            dz = dz_ref[h, o, 4:36]
            for c, d in enumerate((dx, dy, dz)):
                hi, lo = split2(pulls[h] * d)
                fh_ref[3 * h + c, where_to] = hi
                fl_ref[3 * h + c, where_to] = lo
        return carry

    lax.fori_loop(0, 8, o_step, 0, unroll=8)

    cols = slice(32 * first, 32 * first + 256)
    wxy = wxy_ref[:, cols]
    wxy_hi = wxy_ref[0:40, cols]
    planes = []
    for c in range(6):
        one = dot(wxy, fh_ref[c])
        planes.append(one[0:40] + one[40:80] + dot(wxy_hi, fl_ref[c]))
    hi, lo = split2(jnp.concatenate(planes, axis=0))
    along = dot(jnp.concatenate([hi, lo], axis=0), wz_ref[...])
    along = (along[0:240, 0:128] + along[0:240, 128:256]) + along[240:480, 0:128]
    which = lax.div(lax.broadcasted_iota(jnp.int32, (40, 128), 1), 20)
    total = jnp.zeros((40, 128), f32)
    for c in range(6):
        total = total + jnp.where(which == c, along[40 * c : 40 * c + 40], 0.0)
    total = step_size * total
    if upper:
        out_ref[0:16] = total[0:16]
        out_ref[16:32] = total[16:32] + base_ref[...]
        out_ref[32:40] = total[32:40]
    else:
        out_ref[...] = total + base_ref[...]


def fold_kernel(mine_ref, chip_ref, core_ref, out_ref):
    lane = lax.broadcasted_iota(jnp.int32, (40, 128), 1)
    spot = lax.rem(lane, 20)
    live = lane < 120
    odd = (lax.axis_index("gz") & 1) == 1
    chip, core = chip_ref[...], core_ref[...]
    low = pltpu.roll(jnp.where(odd, core, chip), 112, 1)
    high = pltpu.roll(jnp.where(odd, chip, core), 16, 1)
    total = mine_ref[...]
    total = total + jnp.where(live & (spot < 3), low, 0.0)
    out_ref[...] = total + jnp.where(live & (spot >= 16), high, 0.0)


def across_kernel(own_ref, one_ref, two_ref, far_ref, out_ref):
    odd = (lax.axis_index("gx") & 1) == 1
    tiles = lambda ref: [ref[8 * p : 8 * p + 8] for p in range(5)]
    own, one, two, far = tiles(own_ref), tiles(one_ref), tiles(two_ref), tiles(far_ref)
    below = [jnp.where(odd, a, b) for a, b in zip(one, two)]
    above = [jnp.where(odd, b, a) for a, b in zip(one, two)]
    window = [
        own[0] + below[2] + far[4],
        own[1] + below[3],
        own[2] + below[4] + above[0],
        own[3] + above[1],
        own[4] + above[2] + far[0],
        above[3] + far[1],
    ]
    for n in range(8):
        for w in range(6):
            out_ref[n, 8 * w : 8 * w + 8] = window[w]


def field_kernel(g_ref, wxy_ref, wz_ref, nv_ref, field_ref, rows_ref, buf_ref, sems):
    me_i, me_j, me_k = coords()
    ni, nj, nk = (lax.axis_size(a) for a in AXES)
    row8 = lax.broadcasted_iota(jnp.int32, (8, 128), 0)

    window = []
    js = [lax.rem(me_j + 7, 8), me_j, lax.rem(me_j + 1, 8)]
    for w in range(6):
        before, own, after = (g_ref[j, 8 * w : 8 * w + 8] for j in js)
        window.append(own + jnp.where(row8 < 4, pltpu.roll(before, 4, 0), pltpu.roll(after, 4, 0)))
    coefs = jnp.concatenate(window, axis=0)
    row = lax.broadcasted_iota(jnp.int32, (48, 128), 0)
    lane = lax.broadcasted_iota(jnp.int32, (48, 128), 1)
    at_x = 2 * me_i - 2 + lax.shift_right_logical(row, 3)
    at_y = 4 * me_j - 2 + (row & 7)
    at_z = 16 * me_k - 2 + lax.rem(lane, 20)
    real = (at_x >= 0) & (at_x < 2 * ni) & (at_y >= 0) & (at_y < 4 * nj)
    real = real & (at_z >= 0) & (at_z < 16 * nk) & (lane < 120)
    part = lax.div(lane, 20)
    coefs = jnp.where(real, coefs, 0.0)
    hi, lo = split2(jnp.concatenate([jnp.where(part == c, coefs, 0.0) for c in range(6)], axis=0))
    along = dot(jnp.concatenate([hi, lo], axis=0), wz_ref[...])
    along = (along[0:288, 0:128] + along[0:288, 128:256]) + along[288:576, 0:128]
    ch, cl = split2(along)
    copies = []
    for pair in range(3):
        rhs = []
        for c in (2 * pair, 2 * pair + 1):
            rows = slice(48 * c, 48 * c + 48)
            rhs.append(jnp.concatenate([ch[rows], cl[rows], ch[rows]], axis=0))
        both = dot(wxy_ref[...], jnp.concatenate(rhs, axis=1)).astype(bf16)
        for n in range(2):
            buf_ref[2 * pair + n] = both[:, 128 * n : 128 * n + 128]
        there = pl.ds(2 * pair, 2)
        copy = pltpu.make_async_copy(buf_ref.at[there], field_ref.at[there], sems.at[pair])
        copy.start()
        copies.append(copy)

    for side in range(2):
        cols = [g_ref[j, 16 + 8 * side : 24 + 8 * side] for j in range(8)]
        turned = [pltpu.roll(c, 4, 0) for c in cols]
        tiles = []
        zero = jnp.zeros((8, 128), f32)
        for n in range(5):
            even = cols[2 * n] if n < 4 else zero
            high = turned[2 * n + 1] if n < 4 else zero
            low = turned[2 * n - 1] if n > 0 else zero
            tiles.append(even + jnp.where(row8 < 4, low, high))
        tiles[4] = tiles[4] + tiles[0]
        for n in range(5):
            rows_ref[side, 8 * n : 8 * n + 8] = tiles[n]
        block = jnp.transpose(rows_ref[side, 2:34])
        for c in range(6):
            nv_ref[c, side] = block[20 * c + 2 : 20 * c + 18]
    for copy in copies:
        copy.wait()


VMEM = pl.BlockSpec(memory_space=pltpu.VMEM)


HBM = pl.BlockSpec(memory_space=pltpu.HBM)


def call(body, out_shape, in_specs, scratch=(), out_specs=None, flops=0, bytes_accessed=0):
    return pl.pallas_call(
        body,
        out_shape=[jax.ShapeDtypeStruct(shape, dtype) for shape, dtype in out_shape],
        in_specs=in_specs,
        out_specs=out_specs or [VMEM] * len(out_shape),
        scratch_shapes=list(scratch),
        compiler_params=pltpu.CompilerParams(vmem_limit_bytes=48 << 20),
        cost_estimate=pl.CostEstimate(flops=flops, bytes_accessed=bytes_accessed, transcendentals=0),
    )


def pairs(mesh_sizes, di, dj, dk):
    ni, nj, nk = mesh_sizes
    out = []
    for i in range(ni):
        for j in range(nj):
            for k in range(nk):
                to = (((i + di) % ni) * nj + (j + dj) % nj) * nk + (k + dk) % nk
                out.append(((i * nj + j) * nk + k, to))
    return out


def fixed_tables():
    weight = lambda n, points: spline((np.arange(n)[None, :] - 8.0 * (np.arange(points) - 2)[:, None] - 3.5) / 8.0)
    ex, ey, ez = (weight(n, points) for n, points in ((16, 6), (32, 8), (128, 20)))
    hi, lo = split_two(np.einsum("px,qy->xypq", ex, ey).reshape(512, 48))
    exy = np.concatenate([hi, hi, lo], axis=1)
    padded = lambda part: np.concatenate([np.tile(part, (6, 1)), np.zeros((8, 128), part.dtype)])
    return exy, np.concatenate([padded(part) for part in split_two(ez)], axis=1)


def shards(images, velocity):
    sizes = tuple(lax.axis_size(a) for a in AXES)
    nk = sizes[2]
    exy, ezs = fixed_tables()

    def send(v, di, dj, dk):
        return lax.ppermute(v, AXES, pairs(sizes, di, dj, dk))

    (pack,) = call(pack_kernel, [((2, 32, 128), f32)], [VMEM], bytes_accessed=6 * 10**5)(images)
    to_x, to_y, to_xy = call(
        slab_kernel,
        [((2, 8, 32, 128), f32), ((2, 17, 8, 128), f32), ((2, 9, 8, 128), f32)],
        [VMEM],
        bytes_accessed=10**6,
    )(images)
    zr = lax.ppermute(pack, "gz", [(n, (n + 1) % nk) for n in range(nk)])
    velocity = jnp.swapaxes(velocity, 3, 4).reshape(6, 2, 16, 32)
    vel, wxy, wzs, xsum, zsum = call(
        prep_kernel,
        [((16, 128), f32), ((80, 512), bf16), ((128, 256), bf16), ((256, 128), bf16), ((256, 128), f32)],
        [VMEM],
        [pltpu.VMEM((128, 32), f32)],
        bytes_accessed=10**6,
    )(velocity)
    zr, vel = lax.optimization_barrier((zr, vel))
    xr = send(to_x, 1, 0, 0)
    yr = send(to_y.at[:, 16].set(zr[:, 24:]), 0, 1, 0)
    xyr = send(to_xy.at[:, 8].set(zr[:, 24:]), 1, 1, 0)
    xzr = send(zr, 1, 0, 0)

    def forces(upper, *arrays):
        return call(
            functools.partial(force_kernel, upper),
            [((40, 128), f32)],
            [VMEM] * (len(arrays) + 4),
            [
                pltpu.VMEM((2, 16, 40, 128), f32),
                pltpu.VMEM((2, 2, 40, 128), f32),
                pltpu.VMEM((2, 10, 40, 128), f32),
                pltpu.VMEM((2, 8, 40, 128), f32),
                pltpu.VMEM((5, 8, 40, 128), f32),
                pltpu.VMEM((5, 3, 32, 128), bf16),
                pltpu.VMEM((6, 256, 128), bf16),
                pltpu.VMEM((6, 256, 128), bf16),
            ],
            flops=5 * 10**8,
            bytes_accessed=10**6,
        )(*arrays, wxy, wzs, xsum, zsum)[0]

    part = forces(True, images, zr, yr, vel)
    part = forces(False, images, zr, yr, xr, xzr, xyr, part)

    swap = lambda v, axis, couples: lax.ppermute(v, axis, couples + [(b, a) for a, b in couples])
    chip = swap(part, "gz", [(1, 2), (3, 0)])
    core = swap(part, "gz", [(0, 1), (2, 3)])
    (own,) = call(fold_kernel, [((40, 128), f32)], [VMEM] * 3)(part, chip, core)
    far = swap(own, "gx", [(0, 2), (1, 3)])
    one = swap(own, "gx", [(0, 1), (2, 3)])
    two = swap(own, "gx", [(1, 2), (3, 0)])
    (copies,) = call(across_kernel, [((8, 48, 128), f32)], [VMEM] * 4)(own, one, two, far)
    everything = lax.all_to_all(copies, "gy", 0, 0, tiled=True)

    nv, field = call(
        field_kernel,
        [((6, 2, 16, 32), f32), ((6, 512, 128), bf16)],
        [VMEM] * 3,
        [pltpu.VMEM((2, 40, 128), f32), pltpu.VMEM((6, 512, 128), bf16), pltpu.SemaphoreType.DMA((3,))],
        out_specs=[VMEM, HBM],
        flops=10**8,
        bytes_accessed=10**6,
    )(everything, exy, ezs)
    nv = jnp.swapaxes(nv.reshape(2, 3, 2, 16, 32), 3, 4)
    return nv, field.reshape(2, 3, 16, 32, 128)


def solution(mesh):
    placed = (P(None, "gx", "gy", "gz"), P(None, None, "gx", None, "gz"))
    return jax.shard_map(
        shards,
        mesh=mesh,
        in_specs=placed,
        out_specs=(P(None, None, "gx", None, "gz"), P(None, None, "gx", "gy", "gz")),
        check_vma=False,
    )
```

```python
import functools

import jax
import jax.numpy as jnp
import numpy as np
from jax import lax
from jax.experimental import pallas as pl
from jax.experimental.pallas import tpu as pltpu
from jax.sharding import PartitionSpec as P

epsilon_value = 1e-05
step_size = 0.5
AXES = ("gx", "gy", "gz")
f32 = jnp.float32
bf16 = jnp.bfloat16


def spline(t):
    m = np.abs(t)
    inside = 2.0 / 3.0 - m * m + 0.5 * m * m * m
    out = np.maximum(2.0 - m, 0.0)
    return np.where(m < 1.0, inside, out * out * out / 6.0)


def split_two(w):
    hi = w.astype(np.float32).astype(jnp.bfloat16)
    lo = (w - hi.astype(np.float64)).astype(np.float32).astype(jnp.bfloat16)
    return hi, lo


def pack_kernel(img_ref, out_ref):
    lane = lax.broadcasted_iota(jnp.int32, (32, 128), 1)
    for h in range(2):
        packed = jnp.zeros((32, 128), f32)
        for t in range(16):
            moved = pltpu.roll(img_ref[h, t], (8 * t + 8) % 128, 1)
            packed = jnp.where((lane >= 8 * t) & (lane < 8 * t + 8), moved, packed)
        out_ref[h] = packed


def slab_kernel(after_ref, img_ref, x_ref, y_ref, xy_ref):
    for h in range(2):
        for t in range(16):
            y_ref[h, t] = img_ref[h, t, 24:32]
            if t >= 8:
                x_ref[h, t - 8] = img_ref[h, t]
                xy_ref[h, t - 8] = img_ref[h, t, 24:32]
        xy_ref[h, 8] = jnp.zeros((8, 128), f32)


def spline_at(t):
    m = jnp.abs(t)
    inside = 2.0 / 3.0 - m * m + 0.5 * m * m * m
    out = jnp.maximum(2.0 - m, 0.0)
    return jnp.where(m < 1.0, inside, out * out * out / 6.0)


def weights(voxel, point):
    return spline_at((voxel.astype(f32) - 8.0 * point.astype(f32) - 3.5) * 0.125)


def prep_kernel(vel_ref, vel_out, wxy_out, wz_out, xsum_out, zsum_out, rows_ref):
    i, j, k = coords()
    ni, nj, nk = (lax.axis_size(a) for a in AXES)
    ex = jnp.where(i == 0, 0.0, 1.0)
    ez = jnp.where(k == 0, 0.0, 1.0)
    row = lax.broadcasted_iota(jnp.int32, (40, 512), 0)
    col = lax.broadcasted_iota(jnp.int32, (40, 512), 1)
    p = lax.shift_right_logical(row, 3)
    q = row & 7
    o = lax.shift_right_logical(col, 5)
    r = col & 31
    ok = ((p < 2) == (o < 4)) | (i != 0)
    ok = ok & (((q < 2) == (r < 4)) | (j != 0)) & (q < 7)
    ok = ok & ((p < 4) | (i != ni - 1)) & ((q < 6) | (j != nj - 1))
    table = jnp.where(ok, weights(o - 4, p - 2) * weights(r - 4, q - 2), 0.0)
    hi, lo = split2(table)
    wxy_out[...] = jnp.concatenate([hi.astype(f32), lo.astype(f32)], axis=0).astype(bf16)
    lane = lax.broadcasted_iota(jnp.int32, (128, 128), 1)
    sub = lax.broadcasted_iota(jnp.int32, (128, 128), 0)
    spot = lax.rem(lane, 20)
    ok = ((spot < 2) == (sub >= 124)) | (k != 0)
    ok = ok & (spot < 19) & ((spot < 18) | (k != nk - 1))
    voxel = jnp.where(sub >= 124, sub - 128, sub)
    hi, lo = split2(jnp.where(ok, weights(voxel, spot - 2), 0.0))
    wz_out[...] = jnp.concatenate([hi, lo], axis=1)

    src = lax.broadcasted_iota(jnp.int32, (256, 128), 0)
    dst = lax.broadcasted_iota(jnp.int32, (256, 128), 1)
    plane = jnp.where(src < 128, lax.shift_right_logical(src, 3) + 8, lax.shift_right_logical(src - 128, 3) - 8)
    goal = lax.shift_right_logical(dst, 3)
    near = (plane >= goal) & (plane <= goal + 8) & ((src & 7) == (dst & 7)) & (plane >= 0)
    across = (plane < 8) != (goal < 4)
    xsum_out[...] = jnp.where(near, jnp.where(across, ex, 1.0), 0.0).astype(bf16)
    centre = jnp.where(dst < 124, dst, dst - 128)
    below = src >= 128
    place = jnp.where(below, (src & 7) - 8, src)
    gap = place - centre
    inside = (gap <= 4) & (gap >= -4)
    crossing = below != (dst >= 124)
    zsum_out[...] = jnp.where(inside, jnp.where(crossing, ez, 1.0), 0.0)

    pick_q = lax.broadcasted_iota(jnp.int32, (8, 32), 0)
    pick_y = lax.broadcasted_iota(jnp.int32, (8, 32), 1)
    pick = ((pick_y == 4 * j + pick_q - 2) & (pick_q >= 2) & (pick_q < 6)).astype(f32).astype(bf16)
    for side in range(2):
        rows_ref[...] = jnp.zeros((128, 32), f32)
        for c in range(6):
            rows_ref[20 * c + 2 : 20 * c + 18] = vel_ref[c, side]
        turned = jnp.transpose(rows_ref[...])
        total = jnp.zeros((8, 128), f32)
        for piece in split3(turned):
            total = total + dot(pick, piece)
        vel_out[8 * side : 8 * side + 8] = total


def coords():
    return tuple(lax.axis_index(a) for a in AXES)


def split3(v):
    hi = v.astype(bf16)
    r = v - hi.astype(f32)
    mid = r.astype(bf16)
    lo = (r - mid.astype(f32)).astype(bf16)
    return hi, mid, lo


def split2(v):
    hi = v.astype(bf16)
    return hi, (v - hi.astype(f32)).astype(bf16)


def dot(a, b):
    return jnp.dot(a, b, preferred_element_type=f32)


def up_by(v, n, row):
    size = v.shape[0]
    return jnp.where(row < size - n, pltpu.roll(v, size - n, 0), 0.0)


def rows_window(v, head, tail, row8):
    first = v[0:8]
    own = jnp.concatenate([jnp.zeros((8, 128), f32), v[8:40]], axis=0)
    s = first + up_by(first, 1, row8)
    s = s + up_by(s, 2, row8)
    s = s + up_by(s, 4, row8)
    w = own + pltpu.roll(own, 39, 0)
    w = w + pltpu.roll(w, 38, 0)
    w = w + pltpu.roll(w, 36, 0)
    w = w[0:32] + own[8:40]
    top = head * s + tail * w[0:8]
    return jnp.concatenate([top, w[8:32]], axis=0)


def force_kernel(upper, own_ref, zr_ref, yr_ref, yzr_ref, *refs):
    if upper:
        base_ref, *refs = refs
    else:
        xr_ref, xyr_ref, xzr_ref, base_ref, *refs = refs
    wxy_ref, wz_ref, xsum_ref, zsum_ref, out_ref, a_ref, h_ref, v_ref, dz_ref, xs_ref, hs_ref, fh_ref, fl_ref = refs
    first = 8 if upper else 0
    ex, ey, ez = (jnp.where(at == 0, 0.0, 1.0) for at in coords())
    row8 = lax.broadcasted_iota(jnp.int32, (8, 128), 0)
    row32 = lax.broadcasted_iota(jnp.int32, (32, 128), 0)
    lane40 = lax.broadcasted_iota(jnp.int32, (40, 128), 1)
    head = jnp.where(row8 < 4, 1.0, ey)
    tail = jnp.where(row8 < 4, ey, 1.0)

    for h in range(2):
        for n in range(16):
            if upper or n >= 8:
                t = n if upper else n - 8
                a_ref[h, n, 8:40] = own_ref[h, t]
                a_ref[h, n, 0:8] = yr_ref[h, t]
            else:
                a_ref[h, n, 8:40] = xr_ref[h, n]
                a_ref[h, n, 0:8] = xyr_ref[h, n]
        h_ref[h, 0, 8:40] = zr_ref[h]
        h_ref[h, 0, 0:8] = yzr_ref[h]
        if not upper:
            h_ref[h, 1, 8:40] = xzr_ref[h]
            h_ref[h, 1, 0:8] = xyr_ref[h, 8]

    plus_z = jnp.where(lane40 == 127, ez, 1.0)
    minus_z = jnp.where(lane40 == 0, ez, 1.0)
    for h in range(2):
        for n in range(3, 13):
            l = n + first
            if l >= 8:
                halo = pltpu.roll(h_ref[h, 0], (120 - 8 * (l - 8)) % 128, 1)
            else:
                halo = pltpu.roll(h_ref[h, 1], (120 - 8 * (l + 8)) % 128, 1)
            v_ref[h, n - 3] = jnp.where(lane40 >= 124, halo, a_ref[h, n])
            if 4 <= n < 12:
                dz_ref[h, n - 4] = halo
    for h in range(2):
        for n in range(4, 12):
            a = a_ref[h, n]
            halo = dz_ref[h, n - 4]
            up = pltpu.roll(jnp.where(lane40 >= 125, halo, a), 127, 1)
            down = pltpu.roll(jnp.where(lane40 >= 123, halo, a), 1, 1)
            dz_ref[h, n - 4] = plus_z * up - minus_z * down

    def x_step(tile, carry):
        rows = pl.ds(pl.multiple_of(tile * 8, 8), 8)
        for q in range(5):
            p = []
            for n in range(16):
                if q == 4:
                    p.append(a_ref[0, n, rows] * a_ref[1, n, rows])
                else:
                    value = a_ref[q % 2, n, rows]
                    p.append(value if q < 2 else value * value)
            if upper:
                b = [p[n] + p[n + 1] for n in range(15)]
                b = [b[n] + b[n + 2] for n in range(13)]
                b = [b[n] + b[n + 4] for n in range(9)]
                for o in range(8):
                    xs_ref[q, o, rows] = b[o] + p[o + 8]
                continue
            left = [None] * 8
            left[7] = p[7]
            for o in range(6, -1, -1):
                left[o] = left[o + 1] + p[o]
            right = p[8]
            for o in range(8):
                if o > 0:
                    right = right + p[o + 8]
                xs_ref[q, o, rows] = left[o] + ex * right if o < 4 else ex * left[o] + right
        return carry

    lax.fori_loop(0, 5, x_step, 0)

    sides = 1 if upper else 2
    x_sum = xsum_ref[0 : 128 * sides]
    for q in range(5):
        parts = []
        for side in range(sides):
            f = h_ref[0, side]
            m = h_ref[1, side]
            value = (f, m, f * f, m * m, f * m)[q]
            parts.append(rows_window(value, head, tail, row8))
        total = jnp.zeros((32, 128), f32)
        for piece in split3(jnp.concatenate(parts, axis=1)):
            total = total + dot(piece, x_sum)
        for n, piece in enumerate(split3(total)):
            hs_ref[q, n] = piece

    from_row = lax.broadcasted_iota(jnp.int32, (256, 128), 0)
    plus_y = jnp.where(row32 == 3, ey, 1.0)
    minus_y = jnp.where(row32 == 4, ey, 1.0)

    def o_step(o, carry):
        mine = (from_row < 128) | (lax.shift_right_logical(from_row - 128, 3) == o + first)
        z_sum = jnp.where(mine, zsum_ref[...], 0.0).astype(bf16)
        pieces = [[], [], []]
        for q in range(5):
            y = rows_window(xs_ref[q, o], head, tail, row8)
            for n, piece in enumerate(split3(y)):
                pieces[n].append(jnp.concatenate([piece, hs_ref[q, n]], axis=1))
        big = dot(jnp.concatenate(pieces[0] + pieces[1] + pieces[2], axis=0), z_sum)
        sums = (big[0:160] + big[160:320]) + big[320:480]
        sums = sums * (1.0 / 729.0)
        mean_f = sums[0:32]
        mean_m = sums[32:64]
        var_f = sums[64:96] - mean_f * mean_f + epsilon_value
        var_m = sums[96:128] - mean_m * mean_m + epsilon_value
        cov = sums[128:160] - mean_f * mean_m
        off_f = v_ref[0, o + 1, 4:36] - mean_f
        off_m = v_ref[1, o + 1, 4:36] - mean_m
        inv = 1.0 / (var_f * var_m)
        factor = cov * inv
        pulls = (
            factor * (off_m - factor * var_m * off_f),
            factor * (off_f - factor * var_f * off_m),
        )
        plus_x = jnp.where(o + first == 3, ex, 1.0)
        minus_x = jnp.where(o + first == 4, ex, 1.0)
        where_to = pl.ds(pl.multiple_of(o * 32, 32), 32)
        for h in range(2):
            dx = plus_x * v_ref[h, o + 2, 4:36] - minus_x * v_ref[h, o, 4:36]
            dy = plus_y * v_ref[h, o + 1, 5:37] - minus_y * v_ref[h, o + 1, 3:35]
            dz = dz_ref[h, o, 4:36]
            for c, d in enumerate((dx, dy, dz)):
                hi, lo = split2(pulls[h] * d)
                fh_ref[3 * h + c, where_to] = hi
                fl_ref[3 * h + c, where_to] = lo
        return carry

    lax.fori_loop(0, 8, o_step, 0, unroll=8)

    cols = slice(32 * first, 32 * first + 256)
    wxy = wxy_ref[:, cols]
    wxy_hi = wxy_ref[0:40, cols]
    planes = []
    for c in range(6):
        one = dot(wxy, fh_ref[c])
        planes.append(one[0:40] + one[40:80] + dot(wxy_hi, fl_ref[c]))
    hi, lo = split2(jnp.concatenate(planes, axis=0))
    along = dot(jnp.concatenate([hi, lo], axis=0), wz_ref[...])
    along = (along[0:240, 0:128] + along[0:240, 128:256]) + along[240:480, 0:128]
    which = lax.div(lax.broadcasted_iota(jnp.int32, (40, 128), 1), 20)
    total = jnp.zeros((40, 128), f32)
    for c in range(6):
        total = total + jnp.where(which == c, along[40 * c : 40 * c + 40], 0.0)
    total = step_size * total
    if upper:
        out_ref[0:16] = total[0:16]
        out_ref[16:32] = total[16:32] + base_ref[...]
        out_ref[32:40] = total[32:40]
    else:
        out_ref[...] = total + base_ref[...]


def fold_kernel(mine_ref, chip_ref, core_ref, out_ref):
    lane = lax.broadcasted_iota(jnp.int32, (40, 128), 1)
    spot = lax.rem(lane, 20)
    live = lane < 120
    odd = (lax.axis_index("gz") & 1) == 1
    chip, core = chip_ref[...], core_ref[...]
    low = pltpu.roll(jnp.where(odd, core, chip), 112, 1)
    high = pltpu.roll(jnp.where(odd, chip, core), 16, 1)
    total = mine_ref[...]
    total = total + jnp.where(live & (spot < 3), low, 0.0)
    out_ref[...] = total + jnp.where(live & (spot >= 16), high, 0.0)


def across_kernel(own_ref, far_ref, one_ref, two_ref, out_ref):
    odd = (lax.axis_index("gx") & 1) == 1
    tiles = lambda ref: [ref[8 * p : 8 * p + 8] for p in range(5)]
    own, one, two, far = tiles(own_ref), tiles(one_ref), tiles(two_ref), tiles(far_ref)
    below = [jnp.where(odd, a, b) for a, b in zip(one, two)]
    above = [jnp.where(odd, b, a) for a, b in zip(one, two)]
    window = [
        own[0] + below[2] + far[4],
        own[1] + below[3],
        own[2] + below[4] + above[0],
        own[3] + above[1],
        own[4] + above[2] + far[0],
        above[3] + far[1],
    ]
    for n in range(8):
        for w in range(6):
            out_ref[n, 8 * w : 8 * w + 8] = window[w]


def field_kernel(g_ref, wxy_ref, wz_ref, nv_ref, field_ref, rows_ref, buf_ref, sems):
    me_i, me_j, me_k = coords()
    ni, nj, nk = (lax.axis_size(a) for a in AXES)
    row8 = lax.broadcasted_iota(jnp.int32, (8, 128), 0)

    window = []
    js = [lax.rem(me_j + 7, 8), me_j, lax.rem(me_j + 1, 8)]
    for w in range(6):
        before, own, after = (g_ref[j, 8 * w : 8 * w + 8] for j in js)
        window.append(own + jnp.where(row8 < 4, pltpu.roll(before, 4, 0), pltpu.roll(after, 4, 0)))
    coefs = jnp.concatenate(window, axis=0)
    row = lax.broadcasted_iota(jnp.int32, (48, 128), 0)
    lane = lax.broadcasted_iota(jnp.int32, (48, 128), 1)
    at_x = 2 * me_i - 2 + lax.shift_right_logical(row, 3)
    at_y = 4 * me_j - 2 + (row & 7)
    at_z = 16 * me_k - 2 + lax.rem(lane, 20)
    real = (at_x >= 0) & (at_x < 2 * ni) & (at_y >= 0) & (at_y < 4 * nj)
    real = real & (at_z >= 0) & (at_z < 16 * nk) & (lane < 120)
    part = lax.div(lane, 20)
    coefs = jnp.where(real, coefs, 0.0)
    hi, lo = split2(jnp.concatenate([jnp.where(part == c, coefs, 0.0) for c in range(6)], axis=0))
    along = dot(jnp.concatenate([hi, lo], axis=0), wz_ref[...])
    along = (along[0:288, 0:128] + along[0:288, 128:256]) + along[288:576, 0:128]
    ch, cl = split2(along)
    copies = []
    for pair in range(3):
        rhs = []
        for c in (2 * pair, 2 * pair + 1):
            rows = slice(48 * c, 48 * c + 48)
            rhs.append(jnp.concatenate([ch[rows], cl[rows], ch[rows]], axis=0))
        both = dot(wxy_ref[...], jnp.concatenate(rhs, axis=1)).astype(bf16)
        for n in range(2):
            buf_ref[2 * pair + n] = both[:, 128 * n : 128 * n + 128]
        there = pl.ds(2 * pair, 2)
        copy = pltpu.make_async_copy(buf_ref.at[there], field_ref.at[there], sems.at[pair])
        copy.start()
        copies.append(copy)

    for side in range(2):
        cols = [g_ref[j, 16 + 8 * side : 24 + 8 * side] for j in range(8)]
        turned = [pltpu.roll(c, 4, 0) for c in cols]
        tiles = []
        zero = jnp.zeros((8, 128), f32)
        for n in range(5):
            even = cols[2 * n] if n < 4 else zero
            high = turned[2 * n + 1] if n < 4 else zero
            low = turned[2 * n - 1] if n > 0 else zero
            tiles.append(even + jnp.where(row8 < 4, low, high))
        tiles[4] = tiles[4] + tiles[0]
        for n in range(5):
            rows_ref[side, 8 * n : 8 * n + 8] = tiles[n]
        block = jnp.transpose(rows_ref[side, 2:34])
        for c in range(6):
            nv_ref[c, side] = block[20 * c + 2 : 20 * c + 18]
    for copy in copies:
        copy.wait()


VMEM = pl.BlockSpec(memory_space=pltpu.VMEM)


HBM = pl.BlockSpec(memory_space=pltpu.HBM)


def call(body, out_shape, in_specs, scratch=(), out_specs=None, flops=0, bytes_accessed=0):
    return pl.pallas_call(
        body,
        out_shape=[jax.ShapeDtypeStruct(shape, dtype) for shape, dtype in out_shape],
        in_specs=in_specs,
        out_specs=out_specs or [VMEM] * len(out_shape),
        scratch_shapes=list(scratch),
        compiler_params=pltpu.CompilerParams(vmem_limit_bytes=48 << 20),
        cost_estimate=pl.CostEstimate(flops=flops, bytes_accessed=bytes_accessed, transcendentals=0),
    )


def pairs(mesh_sizes, di, dj, dk):
    ni, nj, nk = mesh_sizes
    out = []
    for i in range(ni):
        for j in range(nj):
            for k in range(nk):
                to = (((i + di) % ni) * nj + (j + dj) % nj) * nk + (k + dk) % nk
                out.append(((i * nj + j) * nk + k, to))
    return out


def fixed_tables():
    weight = lambda n, points: spline((np.arange(n)[None, :] - 8.0 * (np.arange(points) - 2)[:, None] - 3.5) / 8.0)
    ex, ey, ez = (weight(n, points) for n, points in ((16, 6), (32, 8), (128, 20)))
    hi, lo = split_two(np.einsum("px,qy->xypq", ex, ey).reshape(512, 48))
    exy = np.concatenate([hi, hi, lo], axis=1)
    padded = lambda part: np.concatenate([np.tile(part, (6, 1)), np.zeros((8, 128), part.dtype)])
    return exy, np.concatenate([padded(part) for part in split_two(ez)], axis=1)


def shards(images, velocity):
    sizes = tuple(lax.axis_size(a) for a in AXES)
    nk = sizes[2]
    exy, ezs = fixed_tables()

    def send(v, di, dj, dk):
        return lax.ppermute(v, AXES, pairs(sizes, di, dj, dk))

    (pack,) = call(pack_kernel, [((2, 32, 128), f32)], [VMEM], bytes_accessed=6 * 10**5)(images)
    to_x, to_y, to_xy = call(
        slab_kernel,
        [((2, 8, 32, 128), f32), ((2, 16, 8, 128), f32), ((2, 9, 8, 128), f32)],
        [pl.BlockSpec(memory_space=pl.ANY), VMEM],
        bytes_accessed=10**6,
    )(pack, images)
    zr = lax.ppermute(pack, "gz", [(n, (n + 1) % nk) for n in range(nk)])
    yr = send(to_y, 0, 1, 0)
    xr = send(to_x, 1, 0, 0)

    velocity = jnp.swapaxes(velocity, 3, 4).reshape(6, 2, 16, 32)
    vel, wxy, wzs, xsum, zsum = call(
        prep_kernel,
        [((16, 128), f32), ((80, 512), bf16), ((128, 256), bf16), ((256, 128), bf16), ((256, 128), f32)],
        [VMEM],
        [pltpu.VMEM((128, 32), f32)],
        bytes_accessed=10**6,
    )(velocity)
    zr, vel = lax.optimization_barrier((zr, vel))
    top = zr[:, 24:]
    yzr = send(top, 0, 1, 0)
    xyr = send(to_xy.at[:, 8].set(top), 1, 1, 0)
    xzr = send(zr, 1, 0, 0)

    def forces(upper, *arrays):
        return call(
            functools.partial(force_kernel, upper),
            [((40, 128), f32)],
            [VMEM] * (len(arrays) + 4),
            [
                pltpu.VMEM((2, 16, 40, 128), f32),
                pltpu.VMEM((2, 2, 40, 128), f32),
                pltpu.VMEM((2, 10, 40, 128), f32),
                pltpu.VMEM((2, 8, 40, 128), f32),
                pltpu.VMEM((5, 8, 40, 128), f32),
                pltpu.VMEM((5, 3, 32, 128), bf16),
                pltpu.VMEM((6, 256, 128), bf16),
                pltpu.VMEM((6, 256, 128), bf16),
            ],
            flops=5 * 10**8,
            bytes_accessed=10**6,
        )(*arrays, wxy, wzs, xsum, zsum)[0]

    part = forces(True, images, zr, yr, yzr, vel)
    part = forces(False, images, zr, yr, yzr, xr, xyr, xzr, part)

    swap = lambda v, axis, couples: lax.ppermute(v, axis, couples + [(b, a) for a, b in couples])
    chip = swap(part, "gz", [(1, 2), (3, 0)])
    core = swap(part, "gz", [(0, 1), (2, 3)])
    (own,) = call(fold_kernel, [((40, 128), f32)], [VMEM] * 3)(part, chip, core)
    far = swap(own, "gx", [(0, 2), (1, 3)])
    one = swap(own, "gx", [(0, 1), (2, 3)])
    two = swap(own, "gx", [(1, 2), (3, 0)])
    (copies,) = call(across_kernel, [((8, 48, 128), f32)], [VMEM] * 4)(own, far, one, two)
    everything = lax.all_to_all(copies, "gy", 0, 0, tiled=True)

    nv, field = call(
        field_kernel,
        [((6, 2, 16, 32), f32), ((6, 512, 128), bf16)],
        [VMEM] * 3,
        [pltpu.VMEM((2, 40, 128), f32), pltpu.VMEM((6, 512, 128), bf16), pltpu.SemaphoreType.DMA((3,))],
        out_specs=[VMEM, HBM],
        flops=10**8,
        bytes_accessed=10**6,
    )(everything, exy, ezs)
    nv = jnp.swapaxes(nv.reshape(2, 3, 2, 16, 32), 3, 4)
    return nv, field.reshape(2, 3, 16, 32, 128)


def solution(mesh):
    placed = (P(None, "gx", "gy", "gz"), P(None, None, "gx", None, "gz"))
    return jax.shard_map(
        shards,
        mesh=mesh,
        in_specs=placed,
        out_specs=(P(None, None, "gx", None, "gz"), P(None, None, "gx", "gy", "gz")),
        check_vma=False,
    )
```

```python
import functools

import jax
import jax.numpy as jnp
import numpy as np
from jax import lax
from jax.experimental import pallas as pl
from jax.experimental.pallas import tpu as pltpu
from jax.sharding import PartitionSpec as P

epsilon_value = 1e-05
step_size = 0.5
AXES = ("gx", "gy", "gz")
f32 = jnp.float32
bf16 = jnp.bfloat16


def spline(t):
    m = np.abs(t)
    inside = 2.0 / 3.0 - m * m + 0.5 * m * m * m
    out = np.maximum(2.0 - m, 0.0)
    return np.where(m < 1.0, inside, out * out * out / 6.0)


def split_two(w):
    hi = w.astype(np.float32).astype(jnp.bfloat16)
    lo = (w - hi.astype(np.float64)).astype(np.float32).astype(jnp.bfloat16)
    return hi, lo


def pack_kernel(img_ref, out_ref):
    lane = lax.broadcasted_iota(jnp.int32, (32, 128), 1)
    for h in range(2):
        packed = jnp.zeros((32, 128), f32)
        for t in range(16):
            moved = pltpu.roll(img_ref[h, t], (8 * t + 8) % 128, 1)
            packed = jnp.where((lane >= 8 * t) & (lane < 8 * t + 8), moved, packed)
        out_ref[h] = packed


def slab_kernel(after_ref, img_ref, x_ref, y_ref):
    for h in range(2):
        for t in range(16):
            y_ref[h, t] = img_ref[h, t, 24:32]
            if t >= 8:
                x_ref[h, t - 8] = img_ref[h, t]


def spline_at(t):
    m = jnp.abs(t)
    inside = 2.0 / 3.0 - m * m + 0.5 * m * m * m
    out = jnp.maximum(2.0 - m, 0.0)
    return jnp.where(m < 1.0, inside, out * out * out / 6.0)


def weights(voxel, point):
    return spline_at((voxel.astype(f32) - 8.0 * point.astype(f32) - 3.5) * 0.125)


def prep_kernel(vel_ref, vel_out, wxy_out, wz_out, xsum_out, zsum_out, rows_ref):
    i, j, k = coords()
    ni, nj, nk = (lax.axis_size(a) for a in AXES)
    ex = jnp.where(i == 0, 0.0, 1.0)
    ez = jnp.where(k == 0, 0.0, 1.0)
    row = lax.broadcasted_iota(jnp.int32, (40, 512), 0)
    col = lax.broadcasted_iota(jnp.int32, (40, 512), 1)
    p = lax.shift_right_logical(row, 3)
    q = row & 7
    o = lax.shift_right_logical(col, 5)
    r = col & 31
    ok = ((p < 2) == (o < 4)) | (i != 0)
    ok = ok & (((q < 2) == (r < 4)) | (j != 0)) & (q < 7)
    ok = ok & ((p < 4) | (i != ni - 1)) & ((q < 6) | (j != nj - 1))
    table = jnp.where(ok, weights(o - 4, p - 2) * weights(r - 4, q - 2), 0.0)
    hi, lo = split2(table)
    wxy_out[...] = jnp.concatenate([hi.astype(f32), lo.astype(f32)], axis=0).astype(bf16)
    lane = lax.broadcasted_iota(jnp.int32, (128, 128), 1)
    sub = lax.broadcasted_iota(jnp.int32, (128, 128), 0)
    spot = lax.rem(lane, 20)
    ok = ((spot < 2) == (sub >= 124)) | (k != 0)
    ok = ok & (spot < 19) & ((spot < 18) | (k != nk - 1))
    voxel = jnp.where(sub >= 124, sub - 128, sub)
    hi, lo = split2(jnp.where(ok, weights(voxel, spot - 2), 0.0))
    wz_out[...] = jnp.concatenate([hi, lo], axis=1)

    src = lax.broadcasted_iota(jnp.int32, (256, 128), 0)
    dst = lax.broadcasted_iota(jnp.int32, (256, 128), 1)
    plane = jnp.where(src < 128, lax.shift_right_logical(src, 3) + 8, lax.shift_right_logical(src - 128, 3) - 8)
    goal = lax.shift_right_logical(dst, 3)
    near = (plane >= goal) & (plane <= goal + 8) & ((src & 7) == (dst & 7)) & (plane >= 0)
    across = (plane < 8) != (goal < 4)
    xsum_out[...] = jnp.where(near, jnp.where(across, ex, 1.0), 0.0).astype(bf16)
    centre = jnp.where(dst < 124, dst, dst - 128)
    below = src >= 128
    place = jnp.where(below, (src & 7) - 8, src)
    gap = place - centre
    inside = (gap <= 4) & (gap >= -4)
    crossing = below != (dst >= 124)
    zsum_out[...] = jnp.where(inside, jnp.where(crossing, ez, 1.0), 0.0)

    pick_q = lax.broadcasted_iota(jnp.int32, (8, 32), 0)
    pick_y = lax.broadcasted_iota(jnp.int32, (8, 32), 1)
    pick = ((pick_y == 4 * j + pick_q - 2) & (pick_q >= 2) & (pick_q < 6)).astype(f32).astype(bf16)
    for side in range(2):
        rows_ref[...] = jnp.zeros((128, 32), f32)
        for c in range(6):
            rows_ref[20 * c + 2 : 20 * c + 18] = vel_ref[c, side]
        turned = jnp.transpose(rows_ref[...])
        total = jnp.zeros((8, 128), f32)
        for piece in split3(turned):
            total = total + dot(pick, piece)
        vel_out[8 * side : 8 * side + 8] = total


def coords():
    return tuple(lax.axis_index(a) for a in AXES)


def split3(v):
    hi = v.astype(bf16)
    r = v - hi.astype(f32)
    mid = r.astype(bf16)
    lo = (r - mid.astype(f32)).astype(bf16)
    return hi, mid, lo


def split2(v):
    hi = v.astype(bf16)
    return hi, (v - hi.astype(f32)).astype(bf16)


def dot(a, b):
    return jnp.dot(a, b, preferred_element_type=f32)


def up_by(v, n, row):
    size = v.shape[0]
    return jnp.where(row < size - n, pltpu.roll(v, size - n, 0), 0.0)


def rows_window(v, head, tail, row8):
    first = v[0:8]
    own = jnp.concatenate([jnp.zeros((8, 128), f32), v[8:40]], axis=0)
    s = first + up_by(first, 1, row8)
    s = s + up_by(s, 2, row8)
    s = s + up_by(s, 4, row8)
    w = own + pltpu.roll(own, 39, 0)
    w = w + pltpu.roll(w, 38, 0)
    w = w + pltpu.roll(w, 36, 0)
    w = w[0:32] + own[8:40]
    top = head * s + tail * w[0:8]
    return jnp.concatenate([top, w[8:32]], axis=0)


def force_kernel(upper, own_ref, zr_ref, yr_ref, *refs):
    if upper:
        base_ref, *refs = refs
    else:
        xr_ref, xyr_ref, xzr_ref, base_ref, *refs = refs
    wxy_ref, wz_ref, xsum_ref, zsum_ref, out_ref, a_ref, h_ref, v_ref, dz_ref, xs_ref, hs_ref, fh_ref, fl_ref = refs
    first = 8 if upper else 0
    ex, ey, ez = (jnp.where(at == 0, 0.0, 1.0) for at in coords())
    row8 = lax.broadcasted_iota(jnp.int32, (8, 128), 0)
    row32 = lax.broadcasted_iota(jnp.int32, (32, 128), 0)
    lane40 = lax.broadcasted_iota(jnp.int32, (40, 128), 1)
    head = jnp.where(row8 < 4, 1.0, ey)
    tail = jnp.where(row8 < 4, ey, 1.0)

    for h in range(2):
        for n in range(16):
            if upper or n >= 8:
                t = n if upper else n - 8
                a_ref[h, n, 8:40] = own_ref[h, t]
                a_ref[h, n, 0:8] = yr_ref[h, t]
            else:
                a_ref[h, n, 8:40] = xr_ref[h, n]
                a_ref[h, n, 0:8] = xyr_ref[h, n]
        h_ref[h, 0] = zr_ref[h]
        if not upper:
            h_ref[h, 1] = xzr_ref[h]

    plus_z = jnp.where(lane40 == 127, ez, 1.0)
    minus_z = jnp.where(lane40 == 0, ez, 1.0)
    for h in range(2):
        for n in range(3, 13):
            l = n + first
            if l >= 8:
                halo = pltpu.roll(h_ref[h, 0], (120 - 8 * (l - 8)) % 128, 1)
            else:
                halo = pltpu.roll(h_ref[h, 1], (120 - 8 * (l + 8)) % 128, 1)
            v_ref[h, n - 3] = jnp.where(lane40 >= 124, halo, a_ref[h, n])
            if 4 <= n < 12:
                dz_ref[h, n - 4] = halo
    for h in range(2):
        for n in range(4, 12):
            a = a_ref[h, n]
            halo = dz_ref[h, n - 4]
            up = pltpu.roll(jnp.where(lane40 >= 125, halo, a), 127, 1)
            down = pltpu.roll(jnp.where(lane40 >= 123, halo, a), 1, 1)
            dz_ref[h, n - 4] = plus_z * up - minus_z * down

    def x_step(tile, carry):
        rows = pl.ds(pl.multiple_of(tile * 8, 8), 8)
        for q in range(5):
            p = []
            for n in range(16):
                if q == 4:
                    p.append(a_ref[0, n, rows] * a_ref[1, n, rows])
                else:
                    value = a_ref[q % 2, n, rows]
                    p.append(value if q < 2 else value * value)
            if upper:
                b = [p[n] + p[n + 1] for n in range(15)]
                b = [b[n] + b[n + 2] for n in range(13)]
                b = [b[n] + b[n + 4] for n in range(9)]
                for o in range(8):
                    xs_ref[q, o, rows] = b[o] + p[o + 8]
                continue
            left = [None] * 8
            left[7] = p[7]
            for o in range(6, -1, -1):
                left[o] = left[o + 1] + p[o]
            right = p[8]
            for o in range(8):
                if o > 0:
                    right = right + p[o + 8]
                xs_ref[q, o, rows] = left[o] + ex * right if o < 4 else ex * left[o] + right
        return carry

    lax.fori_loop(0, 5, x_step, 0)

    sides = 1 if upper else 2
    x_sum = xsum_ref[0 : 128 * sides]
    for q in range(5):
        parts = []
        for side in range(sides):
            f = h_ref[0, side]
            m = h_ref[1, side]
            value = (f, m, f * f, m * m, f * m)[q]
            parts.append(rows_window(value, head, tail, row8))
        total = jnp.zeros((32, 128), f32)
        for piece in split3(jnp.concatenate(parts, axis=1)):
            total = total + dot(piece, x_sum)
        for n, piece in enumerate(split3(total)):
            hs_ref[q, n] = piece

    from_row = lax.broadcasted_iota(jnp.int32, (256, 128), 0)
    plus_y = jnp.where(row32 == 3, ey, 1.0)
    minus_y = jnp.where(row32 == 4, ey, 1.0)

    def o_step(o, carry):
        mine = (from_row < 128) | (lax.shift_right_logical(from_row - 128, 3) == o + first)
        z_sum = jnp.where(mine, zsum_ref[...], 0.0).astype(bf16)
        pieces = [[], [], []]
        for q in range(5):
            y = rows_window(xs_ref[q, o], head, tail, row8)
            for n, piece in enumerate(split3(y)):
                pieces[n].append(jnp.concatenate([piece, hs_ref[q, n]], axis=1))
        big = dot(jnp.concatenate(pieces[0] + pieces[1] + pieces[2], axis=0), z_sum)
        sums = (big[0:160] + big[160:320]) + big[320:480]
        sums = sums * (1.0 / 729.0)
        mean_f = sums[0:32]
        mean_m = sums[32:64]
        var_f = sums[64:96] - mean_f * mean_f + epsilon_value
        var_m = sums[96:128] - mean_m * mean_m + epsilon_value
        cov = sums[128:160] - mean_f * mean_m
        off_f = v_ref[0, o + 1, 4:36] - mean_f
        off_m = v_ref[1, o + 1, 4:36] - mean_m
        inv = 1.0 / (var_f * var_m)
        factor = cov * inv
        pulls = (
            factor * (off_m - factor * var_m * off_f),
            factor * (off_f - factor * var_f * off_m),
        )
        plus_x = jnp.where(o + first == 3, ex, 1.0)
        minus_x = jnp.where(o + first == 4, ex, 1.0)
        where_to = pl.ds(pl.multiple_of(o * 32, 32), 32)
        for h in range(2):
            dx = plus_x * v_ref[h, o + 2, 4:36] - minus_x * v_ref[h, o, 4:36]
            dy = plus_y * v_ref[h, o + 1, 5:37] - minus_y * v_ref[h, o + 1, 3:35]
            dz = dz_ref[h, o, 4:36]
            for c, d in enumerate((dx, dy, dz)):
                hi, lo = split2(pulls[h] * d)
                fh_ref[3 * h + c, where_to] = hi
                fl_ref[3 * h + c, where_to] = lo
        return carry

    lax.fori_loop(0, 8, o_step, 0, unroll=8)

    cols = slice(32 * first, 32 * first + 256)
    wxy = wxy_ref[:, cols]
    wxy_hi = wxy_ref[0:40, cols]
    planes = []
    for c in range(6):
        one = dot(wxy, fh_ref[c])
        planes.append(one[0:40] + one[40:80] + dot(wxy_hi, fl_ref[c]))
    hi, lo = split2(jnp.concatenate(planes, axis=0))
    along = dot(jnp.concatenate([hi, lo], axis=0), wz_ref[...])
    along = (along[0:240, 0:128] + along[0:240, 128:256]) + along[240:480, 0:128]
    which = lax.div(lax.broadcasted_iota(jnp.int32, (40, 128), 1), 20)
    total = jnp.zeros((40, 128), f32)
    for c in range(6):
        total = total + jnp.where(which == c, along[40 * c : 40 * c + 40], 0.0)
    total = step_size * total
    if upper:
        out_ref[0:16] = total[0:16]
        out_ref[16:32] = total[16:32] + base_ref[...]
        out_ref[32:40] = total[32:40]
    else:
        out_ref[...] = total + base_ref[...]


def fold_kernel(mine_ref, chip_ref, core_ref, out_ref):
    lane = lax.broadcasted_iota(jnp.int32, (40, 128), 1)
    spot = lax.rem(lane, 20)
    live = lane < 120
    odd = (lax.axis_index("gz") & 1) == 1
    chip, core = chip_ref[...], core_ref[...]
    low = pltpu.roll(jnp.where(odd, core, chip), 112, 1)
    high = pltpu.roll(jnp.where(odd, chip, core), 16, 1)
    total = mine_ref[...]
    total = total + jnp.where(live & (spot < 3), low, 0.0)
    out_ref[...] = total + jnp.where(live & (spot >= 16), high, 0.0)


def across_kernel(own_ref, far_ref, one_ref, two_ref, out_ref):
    odd = (lax.axis_index("gx") & 1) == 1
    tiles = lambda ref: [ref[8 * p : 8 * p + 8] for p in range(5)]
    own, one, two, far = tiles(own_ref), tiles(one_ref), tiles(two_ref), tiles(far_ref)
    below = [jnp.where(odd, a, b) for a, b in zip(one, two)]
    above = [jnp.where(odd, b, a) for a, b in zip(one, two)]
    window = [
        own[0] + below[2] + far[4],
        own[1] + below[3],
        own[2] + below[4] + above[0],
        own[3] + above[1],
        own[4] + above[2] + far[0],
        above[3] + far[1],
    ]
    for n in range(8):
        for w in range(6):
            out_ref[n, 8 * w : 8 * w + 8] = window[w]


def field_kernel(g_ref, wxy_ref, wz_ref, nv_ref, field_ref, rows_ref, buf_ref, sems):
    me_i, me_j, me_k = coords()
    ni, nj, nk = (lax.axis_size(a) for a in AXES)
    row8 = lax.broadcasted_iota(jnp.int32, (8, 128), 0)

    window = []
    js = [lax.rem(me_j + 7, 8), me_j, lax.rem(me_j + 1, 8)]
    for w in range(6):
        before, own, after = (g_ref[j, 8 * w : 8 * w + 8] for j in js)
        window.append(own + jnp.where(row8 < 4, pltpu.roll(before, 4, 0), pltpu.roll(after, 4, 0)))
    coefs = jnp.concatenate(window, axis=0)
    row = lax.broadcasted_iota(jnp.int32, (48, 128), 0)
    lane = lax.broadcasted_iota(jnp.int32, (48, 128), 1)
    at_x = 2 * me_i - 2 + lax.shift_right_logical(row, 3)
    at_y = 4 * me_j - 2 + (row & 7)
    at_z = 16 * me_k - 2 + lax.rem(lane, 20)
    real = (at_x >= 0) & (at_x < 2 * ni) & (at_y >= 0) & (at_y < 4 * nj)
    real = real & (at_z >= 0) & (at_z < 16 * nk) & (lane < 120)
    part = lax.div(lane, 20)
    coefs = jnp.where(real, coefs, 0.0)
    hi, lo = split2(jnp.concatenate([jnp.where(part == c, coefs, 0.0) for c in range(6)], axis=0))
    along = dot(jnp.concatenate([hi, lo], axis=0), wz_ref[...])
    along = (along[0:288, 0:128] + along[0:288, 128:256]) + along[288:576, 0:128]
    ch, cl = split2(along)
    copies = []
    for pair in range(3):
        rhs = []
        for c in (2 * pair, 2 * pair + 1):
            rows = slice(48 * c, 48 * c + 48)
            rhs.append(jnp.concatenate([ch[rows], cl[rows], ch[rows]], axis=0))
        both = dot(wxy_ref[...], jnp.concatenate(rhs, axis=1)).astype(bf16)
        for n in range(2):
            buf_ref[2 * pair + n] = both[:, 128 * n : 128 * n + 128]
        there = pl.ds(2 * pair, 2)
        copy = pltpu.make_async_copy(buf_ref.at[there], field_ref.at[there], sems.at[pair])
        copy.start()
        copies.append(copy)

    for side in range(2):
        cols = [g_ref[j, 16 + 8 * side : 24 + 8 * side] for j in range(8)]
        turned = [pltpu.roll(c, 4, 0) for c in cols]
        tiles = []
        zero = jnp.zeros((8, 128), f32)
        for n in range(5):
            even = cols[2 * n] if n < 4 else zero
            high = turned[2 * n + 1] if n < 4 else zero
            low = turned[2 * n - 1] if n > 0 else zero
            tiles.append(even + jnp.where(row8 < 4, low, high))
        tiles[4] = tiles[4] + tiles[0]
        for n in range(5):
            rows_ref[side, 8 * n : 8 * n + 8] = tiles[n]
        block = jnp.transpose(rows_ref[side, 2:34])
        for c in range(6):
            nv_ref[c, side] = block[20 * c + 2 : 20 * c + 18]
    for copy in copies:
        copy.wait()


VMEM = pl.BlockSpec(memory_space=pltpu.VMEM)


HBM = pl.BlockSpec(memory_space=pltpu.HBM)


def call(body, out_shape, in_specs, scratch=(), out_specs=None, flops=0, bytes_accessed=0):
    return pl.pallas_call(
        body,
        out_shape=[jax.ShapeDtypeStruct(shape, dtype) for shape, dtype in out_shape],
        in_specs=in_specs,
        out_specs=out_specs or [VMEM] * len(out_shape),
        scratch_shapes=list(scratch),
        compiler_params=pltpu.CompilerParams(vmem_limit_bytes=48 << 20),
        cost_estimate=pl.CostEstimate(flops=flops, bytes_accessed=bytes_accessed, transcendentals=0),
    )


def pairs(mesh_sizes, di, dj, dk):
    ni, nj, nk = mesh_sizes
    out = []
    for i in range(ni):
        for j in range(nj):
            for k in range(nk):
                to = (((i + di) % ni) * nj + (j + dj) % nj) * nk + (k + dk) % nk
                out.append(((i * nj + j) * nk + k, to))
    return out


def fixed_tables():
    weight = lambda n, points: spline((np.arange(n)[None, :] - 8.0 * (np.arange(points) - 2)[:, None] - 3.5) / 8.0)
    ex, ey, ez = (weight(n, points) for n, points in ((16, 6), (32, 8), (128, 20)))
    hi, lo = split_two(np.einsum("px,qy->xypq", ex, ey).reshape(512, 48))
    exy = np.concatenate([hi, hi, lo], axis=1)
    padded = lambda part: np.concatenate([np.tile(part, (6, 1)), np.zeros((8, 128), part.dtype)])
    return exy, np.concatenate([padded(part) for part in split_two(ez)], axis=1)


def shards(images, velocity):
    sizes = tuple(lax.axis_size(a) for a in AXES)
    nk = sizes[2]
    exy, ezs = fixed_tables()

    def send(v, di, dj, dk):
        return lax.ppermute(v, AXES, pairs(sizes, di, dj, dk))

    (pack,) = call(pack_kernel, [((2, 32, 128), f32)], [VMEM], bytes_accessed=6 * 10**5)(images)
    to_x, to_y = call(
        slab_kernel,
        [((2, 8, 32, 128), f32), ((2, 16, 8, 128), f32)],
        [pl.BlockSpec(memory_space=pl.ANY), VMEM],
        bytes_accessed=10**6,
    )(pack, images)
    zr = lax.ppermute(pack, "gz", [(n, (n + 1) % nk) for n in range(nk)])
    yr = send(to_y, 0, 1, 0)
    xr = send(to_x, 1, 0, 0)

    velocity = jnp.swapaxes(velocity, 3, 4).reshape(6, 2, 16, 32)
    vel, wxy, wzs, xsum, zsum = call(
        prep_kernel,
        [((16, 128), f32), ((80, 512), bf16), ((128, 256), bf16), ((256, 128), bf16), ((256, 128), f32)],
        [VMEM],
        [pltpu.VMEM((128, 32), f32)],
        bytes_accessed=10**6,
    )(velocity)
    zr, vel = lax.optimization_barrier((zr, vel))
    zr, vel = lax.optimization_barrier((zr, vel))
    yzr = send(zr[:, 24:], 0, 1, 0)
    xyr = send(yr[:, 8:], 1, 0, 0)
    below_z = jnp.concatenate([yzr, zr], axis=1)
    xzr = send(below_z, 1, 0, 0)

    def forces(upper, *arrays):
        return call(
            functools.partial(force_kernel, upper),
            [((40, 128), f32)],
            [VMEM] * (len(arrays) + 4),
            [
                pltpu.VMEM((2, 16, 40, 128), f32),
                pltpu.VMEM((2, 2, 40, 128), f32),
                pltpu.VMEM((2, 10, 40, 128), f32),
                pltpu.VMEM((2, 8, 40, 128), f32),
                pltpu.VMEM((5, 8, 40, 128), f32),
                pltpu.VMEM((5, 3, 32, 128), bf16),
                pltpu.VMEM((6, 256, 128), bf16),
                pltpu.VMEM((6, 256, 128), bf16),
            ],
            flops=5 * 10**8,
            bytes_accessed=10**6,
        )(*arrays, wxy, wzs, xsum, zsum)[0]

    part = forces(True, images, below_z, yr, vel)
    part = forces(False, images, below_z, yr, xr, xyr, xzr, part)

    swap = lambda v, axis, couples: lax.ppermute(v, axis, couples + [(b, a) for a, b in couples])
    chip = swap(part, "gz", [(1, 2), (3, 0)])
    core = swap(part, "gz", [(0, 1), (2, 3)])
    (own,) = call(fold_kernel, [((40, 128), f32)], [VMEM] * 3)(part, chip, core)
    far = swap(own, "gx", [(0, 2), (1, 3)])
    one = swap(own, "gx", [(0, 1), (2, 3)])
    two = swap(own, "gx", [(1, 2), (3, 0)])
    (copies,) = call(across_kernel, [((8, 48, 128), f32)], [VMEM] * 4)(own, far, one, two)
    everything = lax.all_to_all(copies, "gy", 0, 0, tiled=True)

    nv, field = call(
        field_kernel,
        [((6, 2, 16, 32), f32), ((6, 512, 128), bf16)],
        [VMEM] * 3,
        [pltpu.VMEM((2, 40, 128), f32), pltpu.VMEM((6, 512, 128), bf16), pltpu.SemaphoreType.DMA((3,))],
        out_specs=[VMEM, HBM],
        flops=10**8,
        bytes_accessed=10**6,
    )(everything, exy, ezs)
    nv = jnp.swapaxes(nv.reshape(2, 3, 2, 16, 32), 3, 4)
    return nv, field.reshape(2, 3, 16, 32, 128)


def solution(mesh):
    placed = (P(None, "gx", "gy", "gz"), P(None, None, "gx", None, "gz"))
    return jax.shard_map(
        shards,
        mesh=mesh,
        in_specs=placed,
        out_specs=(P(None, None, "gx", None, "gz"), P(None, None, "gx", "gy", "gz")),
        check_vma=False,
    )
```

```python
import functools

import jax
import jax.numpy as jnp
import numpy as np
from jax import lax
from jax.experimental import pallas as pl
from jax.experimental.pallas import tpu as pltpu
from jax.sharding import PartitionSpec as P

epsilon_value = 1e-05
step_size = 0.5
AXES = ("gx", "gy", "gz")
f32 = jnp.float32
bf16 = jnp.bfloat16


def spline(t):
    m = np.abs(t)
    inside = 2.0 / 3.0 - m * m + 0.5 * m * m * m
    out = np.maximum(2.0 - m, 0.0)
    return np.where(m < 1.0, inside, out * out * out / 6.0)


def split_two(w):
    hi = w.astype(np.float32).astype(jnp.bfloat16)
    lo = (w - hi.astype(np.float64)).astype(np.float32).astype(jnp.bfloat16)
    return hi, lo


def pack_kernel(img_ref, out_ref):
    lane = lax.broadcasted_iota(jnp.int32, (32, 128), 1)
    for h in range(2):
        packed = jnp.zeros((32, 128), f32)
        for t in range(16):
            moved = pltpu.roll(img_ref[h, t], (8 * t + 8) % 128, 1)
            packed = jnp.where((lane >= 8 * t) & (lane < 8 * t + 8), moved, packed)
        out_ref[h] = packed


def slab_kernel(after_ref, img_ref, x_ref, y_ref, xy_ref):
    for h in range(2):
        for t in range(16):
            y_ref[h, t] = img_ref[h, t, 24:32]
            if t >= 8:
                x_ref[h, t - 8] = img_ref[h, t]
                xy_ref[h, t - 8] = img_ref[h, t, 24:32]
        xy_ref[h, 8] = jnp.zeros((8, 128), f32)


def spline_at(t):
    m = jnp.abs(t)
    inside = 2.0 / 3.0 - m * m + 0.5 * m * m * m
    out = jnp.maximum(2.0 - m, 0.0)
    return jnp.where(m < 1.0, inside, out * out * out / 6.0)


def weights(voxel, point):
    return spline_at((voxel.astype(f32) - 8.0 * point.astype(f32) - 3.5) * 0.125)


def prep_kernel(vel_ref, vel_out, wxy_out, wz_out, xsum_out, zsum_out, rows_ref):
    i, j, k = coords()
    ni, nj, nk = (lax.axis_size(a) for a in AXES)
    ex = jnp.where(i == 0, 0.0, 1.0)
    ez = jnp.where(k == 0, 0.0, 1.0)
    row = lax.broadcasted_iota(jnp.int32, (40, 512), 0)
    col = lax.broadcasted_iota(jnp.int32, (40, 512), 1)
    p = lax.shift_right_logical(row, 3)
    q = row & 7
    o = lax.shift_right_logical(col, 5)
    r = col & 31
    ok = ((p < 2) == (o < 4)) | (i != 0)
    ok = ok & (((q < 2) == (r < 4)) | (j != 0)) & (q < 7)
    ok = ok & ((p < 4) | (i != ni - 1)) & ((q < 6) | (j != nj - 1))
    table = jnp.where(ok, weights(o - 4, p - 2) * weights(r - 4, q - 2), 0.0)
    hi, lo = split2(table)
    wxy_out[...] = jnp.concatenate([hi.astype(f32), lo.astype(f32)], axis=0).astype(bf16)
    lane = lax.broadcasted_iota(jnp.int32, (128, 128), 1)
    sub = lax.broadcasted_iota(jnp.int32, (128, 128), 0)
    spot = lax.rem(lane, 20)
    ok = ((spot < 2) == (sub >= 124)) | (k != 0)
    ok = ok & (spot < 19) & ((spot < 18) | (k != nk - 1))
    voxel = jnp.where(sub >= 124, sub - 128, sub)
    hi, lo = split2(jnp.where(ok, weights(voxel, spot - 2), 0.0))
    wz_out[...] = jnp.concatenate([hi, lo], axis=1)

    src = lax.broadcasted_iota(jnp.int32, (256, 128), 0)
    dst = lax.broadcasted_iota(jnp.int32, (256, 128), 1)
    plane = jnp.where(src < 128, lax.shift_right_logical(src, 3) + 8, lax.shift_right_logical(src - 128, 3) - 8)
    goal = lax.shift_right_logical(dst, 3)
    near = (plane >= goal) & (plane <= goal + 8) & ((src & 7) == (dst & 7)) & (plane >= 0)
    across = (plane < 8) != (goal < 4)
    xsum_out[...] = jnp.where(near, jnp.where(across, ex, 1.0), 0.0).astype(bf16)
    centre = jnp.where(dst < 124, dst, dst - 128)
    below = src >= 128
    place = jnp.where(below, (src & 7) - 8, src)
    gap = place - centre
    inside = (gap <= 4) & (gap >= -4)
    crossing = below != (dst >= 124)
    zsum_out[...] = jnp.where(inside, jnp.where(crossing, ez, 1.0), 0.0)

    pick_q = lax.broadcasted_iota(jnp.int32, (8, 32), 0)
    pick_y = lax.broadcasted_iota(jnp.int32, (8, 32), 1)
    pick = ((pick_y == 4 * j + pick_q - 2) & (pick_q >= 2) & (pick_q < 6)).astype(f32).astype(bf16)
    for side in range(2):
        rows_ref[...] = jnp.zeros((128, 32), f32)
        for c in range(6):
            rows_ref[20 * c + 2 : 20 * c + 18] = vel_ref[c, side]
        turned = jnp.transpose(rows_ref[...])
        total = jnp.zeros((8, 128), f32)
        for piece in split3(turned):
            total = total + dot(pick, piece)
        vel_out[8 * side : 8 * side + 8] = total


def coords():
    return tuple(lax.axis_index(a) for a in AXES)


def split3(v):
    hi = v.astype(bf16)
    r = v - hi.astype(f32)
    mid = r.astype(bf16)
    lo = (r - mid.astype(f32)).astype(bf16)
    return hi, mid, lo


def split2(v):
    hi = v.astype(bf16)
    return hi, (v - hi.astype(f32)).astype(bf16)


def dot(a, b):
    return jnp.dot(a, b, preferred_element_type=f32)


def up_by(v, n, row):
    size = v.shape[0]
    return jnp.where(row < size - n, pltpu.roll(v, size - n, 0), 0.0)


def rows_window(v, head, tail, row8):
    first = v[0:8]
    own = jnp.concatenate([jnp.zeros((8, 128), f32), v[8:40]], axis=0)
    s = first + up_by(first, 1, row8)
    s = s + up_by(s, 2, row8)
    s = s + up_by(s, 4, row8)
    w = own + pltpu.roll(own, 39, 0)
    w = w + pltpu.roll(w, 38, 0)
    w = w + pltpu.roll(w, 36, 0)
    w = w[0:32] + own[8:40]
    top = head * s + tail * w[0:8]
    return jnp.concatenate([top, w[8:32]], axis=0)


def force_kernel(upper, own_ref, zr_ref, yr_ref, yzr_ref, *refs):
    if upper:
        base_ref, *refs = refs
    else:
        xr_ref, xyr_ref, xzr_ref, base_ref, *refs = refs
    wxy_ref, wz_ref, xsum_ref, zsum_ref, out_ref, a_ref, h_ref, v_ref, dz_ref, xs_ref, hs_ref, fh_ref, fl_ref = refs
    first = 8 if upper else 0
    ex, ey, ez = (jnp.where(at == 0, 0.0, 1.0) for at in coords())
    row8 = lax.broadcasted_iota(jnp.int32, (8, 128), 0)
    row32 = lax.broadcasted_iota(jnp.int32, (32, 128), 0)
    lane40 = lax.broadcasted_iota(jnp.int32, (40, 128), 1)
    head = jnp.where(row8 < 4, 1.0, ey)
    tail = jnp.where(row8 < 4, ey, 1.0)

    for h in range(2):
        for n in range(16):
            if upper or n >= 8:
                t = n if upper else n - 8
                a_ref[h, n, 8:40] = own_ref[h, t]
                a_ref[h, n, 0:8] = yr_ref[h, t]
            else:
                a_ref[h, n, 8:40] = xr_ref[h, n]
                a_ref[h, n, 0:8] = xyr_ref[h, n]
        h_ref[h, 0, 8:40] = zr_ref[h]
        h_ref[h, 0, 0:8] = yzr_ref[h, 24:32]
        if not upper:
            h_ref[h, 1, 8:40] = xzr_ref[h]
            h_ref[h, 1, 0:8] = xyr_ref[h, 8]

    plus_z = jnp.where(lane40 == 127, ez, 1.0)
    minus_z = jnp.where(lane40 == 0, ez, 1.0)
    for h in range(2):
        for n in range(3, 13):
            l = n + first
            if l >= 8:
                halo = pltpu.roll(h_ref[h, 0], (120 - 8 * (l - 8)) % 128, 1)
            else:
                halo = pltpu.roll(h_ref[h, 1], (120 - 8 * (l + 8)) % 128, 1)
            v_ref[h, n - 3] = jnp.where(lane40 >= 124, halo, a_ref[h, n])
            if 4 <= n < 12:
                dz_ref[h, n - 4] = halo
    for h in range(2):
        for n in range(4, 12):
            a = a_ref[h, n]
            halo = dz_ref[h, n - 4]
            up = pltpu.roll(jnp.where(lane40 >= 125, halo, a), 127, 1)
            down = pltpu.roll(jnp.where(lane40 >= 123, halo, a), 1, 1)
            dz_ref[h, n - 4] = plus_z * up - minus_z * down

    def x_step(tile, carry):
        rows = pl.ds(pl.multiple_of(tile * 8, 8), 8)
        for q in range(5):
            p = []
            for n in range(16):
                if q == 4:
                    p.append(a_ref[0, n, rows] * a_ref[1, n, rows])
                else:
                    value = a_ref[q % 2, n, rows]
                    p.append(value if q < 2 else value * value)
            if upper:
                b = [p[n] + p[n + 1] for n in range(15)]
                b = [b[n] + b[n + 2] for n in range(13)]
                b = [b[n] + b[n + 4] for n in range(9)]
                for o in range(8):
                    xs_ref[q, o, rows] = b[o] + p[o + 8]
                continue
            left = [None] * 8
            left[7] = p[7]
            for o in range(6, -1, -1):
                left[o] = left[o + 1] + p[o]
            right = p[8]
            for o in range(8):
                if o > 0:
                    right = right + p[o + 8]
                xs_ref[q, o, rows] = left[o] + ex * right if o < 4 else ex * left[o] + right
        return carry

    lax.fori_loop(0, 5, x_step, 0)

    sides = 1 if upper else 2
    x_sum = xsum_ref[0 : 128 * sides]
    for q in range(5):
        parts = []
        for side in range(sides):
            f = h_ref[0, side]
            m = h_ref[1, side]
            value = (f, m, f * f, m * m, f * m)[q]
            parts.append(rows_window(value, head, tail, row8))
        total = jnp.zeros((32, 128), f32)
        for piece in split3(jnp.concatenate(parts, axis=1)):
            total = total + dot(piece, x_sum)
        for n, piece in enumerate(split3(total)):
            hs_ref[q, n] = piece

    from_row = lax.broadcasted_iota(jnp.int32, (256, 128), 0)
    plus_y = jnp.where(row32 == 3, ey, 1.0)
    minus_y = jnp.where(row32 == 4, ey, 1.0)

    def o_step(o, carry):
        mine = (from_row < 128) | (lax.shift_right_logical(from_row - 128, 3) == o + first)
        z_sum = jnp.where(mine, zsum_ref[...], 0.0).astype(bf16)
        pieces = [[], [], []]
        for q in range(5):
            y = rows_window(xs_ref[q, o], head, tail, row8)
            for n, piece in enumerate(split3(y)):
                pieces[n].append(jnp.concatenate([piece, hs_ref[q, n]], axis=1))
        big = dot(jnp.concatenate(pieces[0] + pieces[1] + pieces[2], axis=0), z_sum)
        sums = (big[0:160] + big[160:320]) + big[320:480]
        sums = sums * (1.0 / 729.0)
        mean_f = sums[0:32]
        mean_m = sums[32:64]
        var_f = sums[64:96] - mean_f * mean_f + epsilon_value
        var_m = sums[96:128] - mean_m * mean_m + epsilon_value
        cov = sums[128:160] - mean_f * mean_m
        off_f = v_ref[0, o + 1, 4:36] - mean_f
        off_m = v_ref[1, o + 1, 4:36] - mean_m
        inv = 1.0 / (var_f * var_m)
        factor = cov * inv
        pulls = (
            factor * (off_m - factor * var_m * off_f),
            factor * (off_f - factor * var_f * off_m),
        )
        plus_x = jnp.where(o + first == 3, ex, 1.0)
        minus_x = jnp.where(o + first == 4, ex, 1.0)
        where_to = pl.ds(pl.multiple_of(o * 32, 32), 32)
        for h in range(2):
            dx = plus_x * v_ref[h, o + 2, 4:36] - minus_x * v_ref[h, o, 4:36]
            dy = plus_y * v_ref[h, o + 1, 5:37] - minus_y * v_ref[h, o + 1, 3:35]
            dz = dz_ref[h, o, 4:36]
            for c, d in enumerate((dx, dy, dz)):
                hi, lo = split2(pulls[h] * d)
                fh_ref[3 * h + c, where_to] = hi
                fl_ref[3 * h + c, where_to] = lo
        return carry

    lax.fori_loop(0, 8, o_step, 0, unroll=8)

    cols = slice(32 * first, 32 * first + 256)
    wxy = wxy_ref[:, cols]
    wxy_hi = wxy_ref[0:40, cols]
    planes = []
    for c in range(6):
        one = dot(wxy, fh_ref[c])
        planes.append(one[0:40] + one[40:80] + dot(wxy_hi, fl_ref[c]))
    hi, lo = split2(jnp.concatenate(planes, axis=0))
    along = dot(jnp.concatenate([hi, lo], axis=0), wz_ref[...])
    along = (along[0:240, 0:128] + along[0:240, 128:256]) + along[240:480, 0:128]
    which = lax.div(lax.broadcasted_iota(jnp.int32, (40, 128), 1), 20)
    total = jnp.zeros((40, 128), f32)
    for c in range(6):
        total = total + jnp.where(which == c, along[40 * c : 40 * c + 40], 0.0)
    total = step_size * total
    if upper:
        out_ref[0:16] = total[0:16]
        out_ref[16:32] = total[16:32] + base_ref[...]
        out_ref[32:40] = total[32:40]
    else:
        out_ref[...] = total + base_ref[...]


def fold_kernel(mine_ref, chip_ref, core_ref, out_ref):
    lane = lax.broadcasted_iota(jnp.int32, (40, 128), 1)
    spot = lax.rem(lane, 20)
    live = lane < 120
    odd = (lax.axis_index("gz") & 1) == 1
    chip, core = chip_ref[...], core_ref[...]
    low = pltpu.roll(jnp.where(odd, core, chip), 112, 1)
    high = pltpu.roll(jnp.where(odd, chip, core), 16, 1)
    total = mine_ref[...]
    total = total + jnp.where(live & (spot < 3), low, 0.0)
    out_ref[...] = total + jnp.where(live & (spot >= 16), high, 0.0)


def across_kernel(own_ref, far_ref, one_ref, two_ref, out_ref):
    odd = (lax.axis_index("gx") & 1) == 1
    tiles = lambda ref: [ref[8 * p : 8 * p + 8] for p in range(5)]
    own, one, two, far = tiles(own_ref), tiles(one_ref), tiles(two_ref), tiles(far_ref)
    below = [jnp.where(odd, a, b) for a, b in zip(one, two)]
    above = [jnp.where(odd, b, a) for a, b in zip(one, two)]
    window = [
        own[0] + below[2] + far[4],
        own[1] + below[3],
        own[2] + below[4] + above[0],
        own[3] + above[1],
        own[4] + above[2] + far[0],
        above[3] + far[1],
    ]
    for n in range(8):
        for w in range(6):
            out_ref[n, 8 * w : 8 * w + 8] = window[w]


def field_kernel(g_ref, wxy_ref, wz_ref, nv_ref, field_ref, rows_ref, buf_ref, sems):
    me_i, me_j, me_k = coords()
    ni, nj, nk = (lax.axis_size(a) for a in AXES)
    row8 = lax.broadcasted_iota(jnp.int32, (8, 128), 0)

    window = []
    js = [lax.rem(me_j + 7, 8), me_j, lax.rem(me_j + 1, 8)]
    for w in range(6):
        before, own, after = (g_ref[j, 8 * w : 8 * w + 8] for j in js)
        window.append(own + jnp.where(row8 < 4, pltpu.roll(before, 4, 0), pltpu.roll(after, 4, 0)))
    coefs = jnp.concatenate(window, axis=0)
    row = lax.broadcasted_iota(jnp.int32, (48, 128), 0)
    lane = lax.broadcasted_iota(jnp.int32, (48, 128), 1)
    at_x = 2 * me_i - 2 + lax.shift_right_logical(row, 3)
    at_y = 4 * me_j - 2 + (row & 7)
    at_z = 16 * me_k - 2 + lax.rem(lane, 20)
    real = (at_x >= 0) & (at_x < 2 * ni) & (at_y >= 0) & (at_y < 4 * nj)
    real = real & (at_z >= 0) & (at_z < 16 * nk) & (lane < 120)
    part = lax.div(lane, 20)
    coefs = jnp.where(real, coefs, 0.0)
    hi, lo = split2(jnp.concatenate([jnp.where(part == c, coefs, 0.0) for c in range(6)], axis=0))
    along = dot(jnp.concatenate([hi, lo], axis=0), wz_ref[...])
    along = (along[0:288, 0:128] + along[0:288, 128:256]) + along[288:576, 0:128]
    ch, cl = split2(along)
    copies = []
    for pair in range(3):
        rhs = []
        for c in (2 * pair, 2 * pair + 1):
            rows = slice(48 * c, 48 * c + 48)
            rhs.append(jnp.concatenate([ch[rows], cl[rows], ch[rows]], axis=0))
        both = dot(wxy_ref[...], jnp.concatenate(rhs, axis=1)).astype(bf16)
        for n in range(2):
            buf_ref[2 * pair + n] = both[:, 128 * n : 128 * n + 128]
        there = pl.ds(2 * pair, 2)
        copy = pltpu.make_async_copy(buf_ref.at[there], field_ref.at[there], sems.at[pair])
        copy.start()
        copies.append(copy)

    for side in range(2):
        cols = [g_ref[j, 16 + 8 * side : 24 + 8 * side] for j in range(8)]
        turned = [pltpu.roll(c, 4, 0) for c in cols]
        tiles = []
        zero = jnp.zeros((8, 128), f32)
        for n in range(5):
            even = cols[2 * n] if n < 4 else zero
            high = turned[2 * n + 1] if n < 4 else zero
            low = turned[2 * n - 1] if n > 0 else zero
            tiles.append(even + jnp.where(row8 < 4, low, high))
        tiles[4] = tiles[4] + tiles[0]
        for n in range(5):
            rows_ref[side, 8 * n : 8 * n + 8] = tiles[n]
        block = jnp.transpose(rows_ref[side, 2:34])
        for c in range(6):
            nv_ref[c, side] = block[20 * c + 2 : 20 * c + 18]
    for copy in copies:
        copy.wait()


VMEM = pl.BlockSpec(memory_space=pltpu.VMEM)


HBM = pl.BlockSpec(memory_space=pltpu.HBM)


def call(body, out_shape, in_specs, scratch=(), out_specs=None, flops=0, bytes_accessed=0):
    return pl.pallas_call(
        body,
        out_shape=[jax.ShapeDtypeStruct(shape, dtype) for shape, dtype in out_shape],
        in_specs=in_specs,
        out_specs=out_specs or [VMEM] * len(out_shape),
        scratch_shapes=list(scratch),
        compiler_params=pltpu.CompilerParams(vmem_limit_bytes=48 << 20),
        cost_estimate=pl.CostEstimate(flops=flops, bytes_accessed=bytes_accessed, transcendentals=0),
    )


def pairs(mesh_sizes, di, dj, dk):
    ni, nj, nk = mesh_sizes
    out = []
    for i in range(ni):
        for j in range(nj):
            for k in range(nk):
                to = (((i + di) % ni) * nj + (j + dj) % nj) * nk + (k + dk) % nk
                out.append(((i * nj + j) * nk + k, to))
    return out


def fixed_tables():
    weight = lambda n, points: spline((np.arange(n)[None, :] - 8.0 * (np.arange(points) - 2)[:, None] - 3.5) / 8.0)
    ex, ey, ez = (weight(n, points) for n, points in ((16, 6), (32, 8), (128, 20)))
    hi, lo = split_two(np.einsum("px,qy->xypq", ex, ey).reshape(512, 48))
    exy = np.concatenate([hi, hi, lo], axis=1)
    padded = lambda part: np.concatenate([np.tile(part, (6, 1)), np.zeros((8, 128), part.dtype)])
    return exy, np.concatenate([padded(part) for part in split_two(ez)], axis=1)


def shards(images, velocity):
    sizes = tuple(lax.axis_size(a) for a in AXES)
    nk = sizes[2]
    exy, ezs = fixed_tables()

    def send(v, di, dj, dk):
        return lax.ppermute(v, AXES, pairs(sizes, di, dj, dk))

    (pack,) = call(pack_kernel, [((2, 32, 128), f32)], [VMEM], bytes_accessed=6 * 10**5)(images)
    to_x, to_y, to_xy = call(
        slab_kernel,
        [((2, 8, 32, 128), f32), ((2, 16, 8, 128), f32), ((2, 9, 8, 128), f32)],
        [pl.BlockSpec(memory_space=pl.ANY), VMEM],
        bytes_accessed=10**6,
    )(pack, images)
    zr = lax.ppermute(pack, "gz", [(n, (n + 1) % nk) for n in range(nk)])
    yr = send(to_y, 0, 1, 0)
    xr = send(to_x, 1, 0, 0)

    velocity = jnp.swapaxes(velocity, 3, 4).reshape(6, 2, 16, 32)
    vel, wxy, wzs, xsum, zsum = call(
        prep_kernel,
        [((16, 128), f32), ((80, 512), bf16), ((128, 256), bf16), ((256, 128), bf16), ((256, 128), f32)],
        [VMEM],
        [pltpu.VMEM((128, 32), f32)],
        bytes_accessed=10**6,
    )(velocity)
    zr, vel = lax.optimization_barrier((zr, vel))
    top = zr[:, 24:]
    yzr = send(zr, 0, 1, 0)
    xyr = send(to_xy.at[:, 8].set(top), 1, 1, 0)
    xzr = send(zr, 1, 0, 0)

    def forces(upper, *arrays):
        return call(
            functools.partial(force_kernel, upper),
            [((40, 128), f32)],
            [VMEM] * (len(arrays) + 4),
            [
                pltpu.VMEM((2, 16, 40, 128), f32),
                pltpu.VMEM((2, 2, 40, 128), f32),
                pltpu.VMEM((2, 10, 40, 128), f32),
                pltpu.VMEM((2, 8, 40, 128), f32),
                pltpu.VMEM((5, 8, 40, 128), f32),
                pltpu.VMEM((5, 3, 32, 128), bf16),
                pltpu.VMEM((6, 256, 128), bf16),
                pltpu.VMEM((6, 256, 128), bf16),
            ],
            flops=5 * 10**8,
            bytes_accessed=10**6,
        )(*arrays, wxy, wzs, xsum, zsum)[0]

    part = forces(True, images, zr, yr, yzr, vel)
    part = forces(False, images, zr, yr, yzr, xr, xyr, xzr, part)

    swap = lambda v, axis, couples: lax.ppermute(v, axis, couples + [(b, a) for a, b in couples])
    chip = swap(part, "gz", [(1, 2), (3, 0)])
    core = swap(part, "gz", [(0, 1), (2, 3)])
    (own,) = call(fold_kernel, [((40, 128), f32)], [VMEM] * 3)(part, chip, core)
    far = swap(own, "gx", [(0, 2), (1, 3)])
    one = swap(own, "gx", [(0, 1), (2, 3)])
    two = swap(own, "gx", [(1, 2), (3, 0)])
    (copies,) = call(across_kernel, [((8, 48, 128), f32)], [VMEM] * 4)(own, far, one, two)
    everything = lax.all_to_all(copies, "gy", 0, 0, tiled=True)

    nv, field = call(
        field_kernel,
        [((6, 2, 16, 32), f32), ((6, 512, 128), bf16)],
        [VMEM] * 3,
        [pltpu.VMEM((2, 40, 128), f32), pltpu.VMEM((6, 512, 128), bf16), pltpu.SemaphoreType.DMA((3,))],
        out_specs=[VMEM, HBM],
        flops=10**8,
        bytes_accessed=10**6,
    )(everything, exy, ezs)
    nv = jnp.swapaxes(nv.reshape(2, 3, 2, 16, 32), 3, 4)
    return nv, field.reshape(2, 3, 16, 32, 128)


def solution(mesh):
    placed = (P(None, "gx", "gy", "gz"), P(None, None, "gx", None, "gz"))
    return jax.shard_map(
        shards,
        mesh=mesh,
        in_specs=placed,
        out_specs=(P(None, None, "gx", None, "gz"), P(None, None, "gx", "gy", "gz")),
        check_vma=False,
    )
```

```python
import functools

import jax
import jax.numpy as jnp
import numpy as np
from jax import lax
from jax.experimental import pallas as pl
from jax.experimental.pallas import tpu as pltpu
from jax.sharding import PartitionSpec as P

epsilon_value = 1e-05
step_size = 0.5
AXES = ("gx", "gy", "gz")
f32 = jnp.float32
bf16 = jnp.bfloat16


def spline(t):
    m = np.abs(t)
    inside = 2.0 / 3.0 - m * m + 0.5 * m * m * m
    out = np.maximum(2.0 - m, 0.0)
    return np.where(m < 1.0, inside, out * out * out / 6.0)


def split_two(w):
    hi = w.astype(np.float32).astype(jnp.bfloat16)
    lo = (w - hi.astype(np.float64)).astype(np.float32).astype(jnp.bfloat16)
    return hi, lo


def pack_kernel(img_ref, out_ref):
    lane = lax.broadcasted_iota(jnp.int32, (32, 128), 1)
    for h in range(2):
        packed = jnp.zeros((32, 128), f32)
        for t in range(16):
            moved = pltpu.roll(img_ref[h, t], (8 * t + 8) % 128, 1)
            packed = jnp.where((lane >= 8 * t) & (lane < 8 * t + 8), moved, packed)
        out_ref[h] = packed


def slab_kernel(after_ref, img_ref, x_ref, y_ref, xy_ref):
    for h in range(2):
        for t in range(16):
            y_ref[h, t] = img_ref[h, t, 24:32]
            if t >= 8:
                x_ref[h, t - 8] = img_ref[h, t]
                xy_ref[h, t - 8] = img_ref[h, t, 24:32]
        xy_ref[h, 8] = jnp.zeros((8, 128), f32)


def spline_at(t):
    m = jnp.abs(t)
    inside = 2.0 / 3.0 - m * m + 0.5 * m * m * m
    out = jnp.maximum(2.0 - m, 0.0)
    return jnp.where(m < 1.0, inside, out * out * out / 6.0)


def weights(voxel, point):
    return spline_at((voxel.astype(f32) - 8.0 * point.astype(f32) - 3.5) * 0.125)


def prep_kernel(vel_ref, vel_out, wxy_out, wz_out, xsum_out, zsum_out, rows_ref):
    i, j, k = coords()
    ni, nj, nk = (lax.axis_size(a) for a in AXES)
    ex = jnp.where(i == 0, 0.0, 1.0)
    ez = jnp.where(k == 0, 0.0, 1.0)
    row = lax.broadcasted_iota(jnp.int32, (40, 512), 0)
    col = lax.broadcasted_iota(jnp.int32, (40, 512), 1)
    p = lax.shift_right_logical(row, 3)
    q = row & 7
    o = lax.shift_right_logical(col, 5)
    r = col & 31
    ok = ((p < 2) == (o < 4)) | (i != 0)
    ok = ok & (((q < 2) == (r < 4)) | (j != 0)) & (q < 7)
    ok = ok & ((p < 4) | (i != ni - 1)) & ((q < 6) | (j != nj - 1))
    table = jnp.where(ok, weights(o - 4, p - 2) * weights(r - 4, q - 2), 0.0)
    hi, lo = split2(table)
    wxy_out[...] = jnp.concatenate([hi.astype(f32), lo.astype(f32)], axis=0).astype(bf16)
    lane = lax.broadcasted_iota(jnp.int32, (128, 128), 1)
    sub = lax.broadcasted_iota(jnp.int32, (128, 128), 0)
    spot = lax.rem(lane, 20)
    ok = ((spot < 2) == (sub >= 124)) | (k != 0)
    ok = ok & (spot < 19) & ((spot < 18) | (k != nk - 1))
    voxel = jnp.where(sub >= 124, sub - 128, sub)
    hi, lo = split2(jnp.where(ok, weights(voxel, spot - 2), 0.0))
    wz_out[...] = jnp.concatenate([hi, lo], axis=1)

    src = lax.broadcasted_iota(jnp.int32, (256, 128), 0)
    dst = lax.broadcasted_iota(jnp.int32, (256, 128), 1)
    plane = jnp.where(src < 128, lax.shift_right_logical(src, 3) + 8, lax.shift_right_logical(src - 128, 3) - 8)
    goal = lax.shift_right_logical(dst, 3)
    near = (plane >= goal) & (plane <= goal + 8) & ((src & 7) == (dst & 7)) & (plane >= 0)
    across = (plane < 8) != (goal < 4)
    xsum_out[...] = jnp.where(near, jnp.where(across, ex, 1.0), 0.0).astype(bf16)
    centre = jnp.where(dst < 124, dst, dst - 128)
    below = src >= 128
    place = jnp.where(below, (src & 7) - 8, src)
    gap = place - centre
    inside = (gap <= 4) & (gap >= -4)
    crossing = below != (dst >= 124)
    zsum_out[...] = jnp.where(inside, jnp.where(crossing, ez, 1.0), 0.0)

    pick_q = lax.broadcasted_iota(jnp.int32, (8, 32), 0)
    pick_y = lax.broadcasted_iota(jnp.int32, (8, 32), 1)
    pick = ((pick_y == 4 * j + pick_q - 2) & (pick_q >= 2) & (pick_q < 6)).astype(f32).astype(bf16)
    for side in range(2):
        rows_ref[...] = jnp.zeros((128, 32), f32)
        for c in range(6):
            rows_ref[20 * c + 2 : 20 * c + 18] = vel_ref[c, side]
        turned = jnp.transpose(rows_ref[...])
        total = jnp.zeros((8, 128), f32)
        for piece in split3(turned):
            total = total + dot(pick, piece)
        vel_out[8 * side : 8 * side + 8] = total


def coords():
    return tuple(lax.axis_index(a) for a in AXES)


def split3(v):
    hi = v.astype(bf16)
    r = v - hi.astype(f32)
    mid = r.astype(bf16)
    lo = (r - mid.astype(f32)).astype(bf16)
    return hi, mid, lo


def split2(v):
    hi = v.astype(bf16)
    return hi, (v - hi.astype(f32)).astype(bf16)


def dot(a, b):
    return jnp.dot(a, b, preferred_element_type=f32)


def up_by(v, n, row):
    size = v.shape[0]
    return jnp.where(row < size - n, pltpu.roll(v, size - n, 0), 0.0)


def rows_window(v, head, tail, row8):
    first = v[0:8]
    own = jnp.concatenate([jnp.zeros((8, 128), f32), v[8:40]], axis=0)
    s = first + up_by(first, 1, row8)
    s = s + up_by(s, 2, row8)
    s = s + up_by(s, 4, row8)
    w = own + pltpu.roll(own, 39, 0)
    w = w + pltpu.roll(w, 38, 0)
    w = w + pltpu.roll(w, 36, 0)
    w = w[0:32] + own[8:40]
    top = head * s + tail * w[0:8]
    return jnp.concatenate([top, w[8:32]], axis=0)


def force_kernel(upper, own_ref, zr_ref, yr_ref, yzr_ref, *refs):
    if upper:
        base_ref, *refs = refs
    else:
        xr_ref, xyr_ref, xzr_ref, base_ref, *refs = refs
    wxy_ref, wz_ref, xsum_ref, zsum_ref, out_ref, a_ref, h_ref, v_ref, dz_ref, xs_ref, hs_ref, fh_ref, fl_ref = refs
    first = 8 if upper else 0
    ex, ey, ez = (jnp.where(at == 0, 0.0, 1.0) for at in coords())
    row8 = lax.broadcasted_iota(jnp.int32, (8, 128), 0)
    row32 = lax.broadcasted_iota(jnp.int32, (32, 128), 0)
    lane40 = lax.broadcasted_iota(jnp.int32, (40, 128), 1)
    head = jnp.where(row8 < 4, 1.0, ey)
    tail = jnp.where(row8 < 4, ey, 1.0)

    for h in range(2):
        for n in range(16):
            if upper or n >= 8:
                t = n if upper else n - 8
                a_ref[h, n, 8:40] = own_ref[h, t]
                a_ref[h, n, 0:8] = yr_ref[h, t]
            else:
                a_ref[h, n, 8:40] = xr_ref[h, n]
                a_ref[h, n, 0:8] = xyr_ref[h, n]
        h_ref[h, 0, 8:40] = zr_ref[h]
        h_ref[h, 0, 0:8] = yzr_ref[h, 24:32]
        if not upper:
            h_ref[h, 1, 8:40] = xzr_ref[h]
            h_ref[h, 1, 0:8] = xyr_ref[h, 8]

    plus_z = jnp.where(lane40 == 127, ez, 1.0)
    minus_z = jnp.where(lane40 == 0, ez, 1.0)
    for h in range(2):
        for n in range(3, 13):
            l = n + first
            if l >= 8:
                halo = pltpu.roll(h_ref[h, 0], (120 - 8 * (l - 8)) % 128, 1)
            else:
                halo = pltpu.roll(h_ref[h, 1], (120 - 8 * (l + 8)) % 128, 1)
            v_ref[h, n - 3] = jnp.where(lane40 >= 124, halo, a_ref[h, n])
            if 4 <= n < 12:
                dz_ref[h, n - 4] = halo
    for h in range(2):
        for n in range(4, 12):
            a = a_ref[h, n]
            halo = dz_ref[h, n - 4]
            up = pltpu.roll(jnp.where(lane40 >= 125, halo, a), 127, 1)
            down = pltpu.roll(jnp.where(lane40 >= 123, halo, a), 1, 1)
            dz_ref[h, n - 4] = plus_z * up - minus_z * down

    def x_step(tile, carry):
        rows = pl.ds(pl.multiple_of(tile * 8, 8), 8)
        for q in range(5):
            p = []
            for n in range(16):
                if q == 4:
                    p.append(a_ref[0, n, rows] * a_ref[1, n, rows])
                else:
                    value = a_ref[q % 2, n, rows]
                    p.append(value if q < 2 else value * value)
            if upper:
                b = [p[n] + p[n + 1] for n in range(15)]
                b = [b[n] + b[n + 2] for n in range(13)]
                b = [b[n] + b[n + 4] for n in range(9)]
                for o in range(8):
                    xs_ref[q, o, rows] = b[o] + p[o + 8]
                continue
            left = [None] * 8
            left[7] = p[7]
            for o in range(6, -1, -1):
                left[o] = left[o + 1] + p[o]
            right = p[8]
            for o in range(8):
                if o > 0:
                    right = right + p[o + 8]
                xs_ref[q, o, rows] = left[o] + ex * right if o < 4 else ex * left[o] + right
        return carry

    lax.fori_loop(0, 5, x_step, 0)

    sides = 1 if upper else 2
    x_sum = xsum_ref[0 : 128 * sides]
    for q in range(5):
        parts = []
        for side in range(sides):
            f = h_ref[0, side]
            m = h_ref[1, side]
            value = (f, m, f * f, m * m, f * m)[q]
            parts.append(rows_window(value, head, tail, row8))
        total = jnp.zeros((32, 128), f32)
        for piece in split3(jnp.concatenate(parts, axis=1)):
            total = total + dot(piece, x_sum)
        for n, piece in enumerate(split3(total)):
            hs_ref[q, n] = piece

    from_row = lax.broadcasted_iota(jnp.int32, (256, 128), 0)
    plus_y = jnp.where(row32 == 3, ey, 1.0)
    minus_y = jnp.where(row32 == 4, ey, 1.0)

    def o_step(o, carry):
        mine = (from_row < 128) | (lax.shift_right_logical(from_row - 128, 3) == o + first)
        z_sum = jnp.where(mine, zsum_ref[...], 0.0).astype(bf16)
        pieces = [[], [], []]
        for q in range(5):
            y = rows_window(xs_ref[q, o], head, tail, row8)
            for n, piece in enumerate(split3(y)):
                pieces[n].append(jnp.concatenate([piece, hs_ref[q, n]], axis=1))
        big = dot(jnp.concatenate(pieces[0] + pieces[1] + pieces[2], axis=0), z_sum)
        sums = (big[0:160] + big[160:320]) + big[320:480]
        sums = sums * (1.0 / 729.0)
        mean_f = sums[0:32]
        mean_m = sums[32:64]
        var_f = sums[64:96] - mean_f * mean_f + epsilon_value
        var_m = sums[96:128] - mean_m * mean_m + epsilon_value
        cov = sums[128:160] - mean_f * mean_m
        off_f = v_ref[0, o + 1, 4:36] - mean_f
        off_m = v_ref[1, o + 1, 4:36] - mean_m
        inv = 1.0 / (var_f * var_m)
        factor = cov * inv
        pulls = (
            factor * (off_m - factor * var_m * off_f),
            factor * (off_f - factor * var_f * off_m),
        )
        plus_x = jnp.where(o + first == 3, ex, 1.0)
        minus_x = jnp.where(o + first == 4, ex, 1.0)
        where_to = pl.ds(pl.multiple_of(o * 32, 32), 32)
        for h in range(2):
            dx = plus_x * v_ref[h, o + 2, 4:36] - minus_x * v_ref[h, o, 4:36]
            dy = plus_y * v_ref[h, o + 1, 5:37] - minus_y * v_ref[h, o + 1, 3:35]
            dz = dz_ref[h, o, 4:36]
            for c, d in enumerate((dx, dy, dz)):
                hi, lo = split2(pulls[h] * d)
                fh_ref[3 * h + c, where_to] = hi
                fl_ref[3 * h + c, where_to] = lo
        return carry

    lax.fori_loop(0, 8, o_step, 0, unroll=8)

    cols = slice(32 * first, 32 * first + 256)
    wxy = wxy_ref[:, cols]
    wxy_hi = wxy_ref[0:40, cols]
    planes = []
    for c in range(6):
        one = dot(wxy, fh_ref[c])
        planes.append(one[0:40] + one[40:80] + dot(wxy_hi, fl_ref[c]))
    hi, lo = split2(jnp.concatenate(planes, axis=0))
    along = dot(jnp.concatenate([hi, lo], axis=0), wz_ref[...])
    along = (along[0:240, 0:128] + along[0:240, 128:256]) + along[240:480, 0:128]
    which = lax.div(lax.broadcasted_iota(jnp.int32, (40, 128), 1), 20)
    total = jnp.zeros((40, 128), f32)
    for c in range(6):
        total = total + jnp.where(which == c, along[40 * c : 40 * c + 40], 0.0)
    total = step_size * total
    if upper:
        out_ref[0:16] = total[0:16]
        out_ref[16:32] = total[16:32] + base_ref[...]
        out_ref[32:40] = total[32:40]
    else:
        out_ref[...] = total + base_ref[...]


def fold_kernel(mine_ref, chip_ref, core_ref, out_ref):
    lane = lax.broadcasted_iota(jnp.int32, (40, 128), 1)
    spot = lax.rem(lane, 20)
    live = lane < 120
    odd = (lax.axis_index("gz") & 1) == 1
    chip, core = chip_ref[...], core_ref[...]
    low = pltpu.roll(jnp.where(odd, core, chip), 112, 1)
    high = pltpu.roll(jnp.where(odd, chip, core), 16, 1)
    total = mine_ref[...]
    total = total + jnp.where(live & (spot < 3), low, 0.0)
    out_ref[...] = total + jnp.where(live & (spot >= 16), high, 0.0)


def across_kernel(own_ref, far_ref, one_ref, two_ref, out_ref, mine_ref):
    odd = (lax.axis_index("gx") & 1) == 1
    tiles = lambda ref: [ref[8 * p : 8 * p + 8] for p in range(5)]
    own, one, two, far = tiles(own_ref), tiles(one_ref), tiles(two_ref), tiles(far_ref)
    below = [jnp.where(odd, a, b) for a, b in zip(one, two)]
    above = [jnp.where(odd, b, a) for a, b in zip(one, two)]
    window = [
        own[0] + below[2] + far[4],
        own[1] + below[3],
        own[2] + below[4] + above[0],
        own[3] + above[1],
        own[4] + above[2] + far[0],
        above[3] + far[1],
    ]
    for w in range(6):
        mine_ref[8 * w : 8 * w + 8] = window[w]
    low_half = lax.broadcasted_iota(jnp.int32, (8, 128), 0) < 4
    upper, lower = [], []
    for w in (0, 4):
        upper.append(jnp.where(low_half, pltpu.roll(window[w], 4, 0), window[w + 1]))
        lower.append(jnp.where(low_half, window[w], pltpu.roll(window[w + 1], 4, 0)))
    following = lax.rem(lax.axis_index("gy") + 1, 8)
    for n in range(8):
        out_ref[n, 0:8] = window[2]
        out_ref[n, 8:16] = window[3]
        for m in range(2):
            out_ref[n, 16 + 8 * m : 24 + 8 * m] = jnp.where(following == n, upper[m], lower[m])


def field_kernel(g_ref, mine_ref, wxy_ref, wz_ref, nv_ref, field_ref, rows_ref, buf_ref, sems):
    me_i, me_j, me_k = coords()
    ni, nj, nk = (lax.axis_size(a) for a in AXES)
    row8 = lax.broadcasted_iota(jnp.int32, (8, 128), 0)

    window = []
    before, after = lax.rem(me_j + 7, 8), lax.rem(me_j + 1, 8)
    for w in range(6):
        at = 8 * (w - 2) if 2 <= w <= 3 else 16 + 8 * (w // 4)
        lows, highs = g_ref[before, at : at + 8], g_ref[after, at : at + 8]
        if w not in (0, 4):
            lows = pltpu.roll(lows, 4, 0)
        if w not in (1, 5):
            highs = pltpu.roll(highs, 4, 0)
        window.append(mine_ref[8 * w : 8 * w + 8] + jnp.where(row8 < 4, lows, highs))
    coefs = jnp.concatenate(window, axis=0)
    row = lax.broadcasted_iota(jnp.int32, (48, 128), 0)
    lane = lax.broadcasted_iota(jnp.int32, (48, 128), 1)
    at_x = 2 * me_i - 2 + lax.shift_right_logical(row, 3)
    at_y = 4 * me_j - 2 + (row & 7)
    at_z = 16 * me_k - 2 + lax.rem(lane, 20)
    real = (at_x >= 0) & (at_x < 2 * ni) & (at_y >= 0) & (at_y < 4 * nj)
    real = real & (at_z >= 0) & (at_z < 16 * nk) & (lane < 120)
    part = lax.div(lane, 20)
    coefs = jnp.where(real, coefs, 0.0)
    hi, lo = split2(jnp.concatenate([jnp.where(part == c, coefs, 0.0) for c in range(6)], axis=0))
    along = dot(jnp.concatenate([hi, lo], axis=0), wz_ref[...])
    along = (along[0:288, 0:128] + along[0:288, 128:256]) + along[288:576, 0:128]
    ch, cl = split2(along)
    copies = []
    for pair in range(3):
        rhs = []
        for c in (2 * pair, 2 * pair + 1):
            rows = slice(48 * c, 48 * c + 48)
            rhs.append(jnp.concatenate([ch[rows], cl[rows], ch[rows]], axis=0))
        both = dot(wxy_ref[...], jnp.concatenate(rhs, axis=1)).astype(bf16)
        for n in range(2):
            buf_ref[2 * pair + n] = both[:, 128 * n : 128 * n + 128]
        there = pl.ds(2 * pair, 2)
        copy = pltpu.make_async_copy(buf_ref.at[there], field_ref.at[there], sems.at[pair])
        copy.start()
        copies.append(copy)

    for side in range(2):
        cols = [g_ref[j, 8 * side : 8 * side + 8] for j in range(8)]
        turned = [pltpu.roll(c, 4, 0) for c in cols]
        tiles = []
        zero = jnp.zeros((8, 128), f32)
        for n in range(5):
            even = cols[2 * n] if n < 4 else zero
            high = turned[2 * n + 1] if n < 4 else zero
            low = turned[2 * n - 1] if n > 0 else zero
            tiles.append(even + jnp.where(row8 < 4, low, high))
        tiles[4] = tiles[4] + tiles[0]
        for n in range(5):
            rows_ref[side, 8 * n : 8 * n + 8] = tiles[n]
        block = jnp.transpose(rows_ref[side, 2:34])
        for c in range(6):
            nv_ref[c, side] = block[20 * c + 2 : 20 * c + 18]
    for copy in copies:
        copy.wait()


VMEM = pl.BlockSpec(memory_space=pltpu.VMEM)


HBM = pl.BlockSpec(memory_space=pltpu.HBM)


def call(body, out_shape, in_specs, scratch=(), out_specs=None, flops=0, bytes_accessed=0):
    return pl.pallas_call(
        body,
        out_shape=[jax.ShapeDtypeStruct(shape, dtype) for shape, dtype in out_shape],
        in_specs=in_specs,
        out_specs=out_specs or [VMEM] * len(out_shape),
        scratch_shapes=list(scratch),
        compiler_params=pltpu.CompilerParams(vmem_limit_bytes=48 << 20),
        cost_estimate=pl.CostEstimate(flops=flops, bytes_accessed=bytes_accessed, transcendentals=0),
    )


def pairs(mesh_sizes, di, dj, dk):
    ni, nj, nk = mesh_sizes
    out = []
    for i in range(ni):
        for j in range(nj):
            for k in range(nk):
                to = (((i + di) % ni) * nj + (j + dj) % nj) * nk + (k + dk) % nk
                out.append(((i * nj + j) * nk + k, to))
    return out


def fixed_tables():
    weight = lambda n, points: spline((np.arange(n)[None, :] - 8.0 * (np.arange(points) - 2)[:, None] - 3.5) / 8.0)
    ex, ey, ez = (weight(n, points) for n, points in ((16, 6), (32, 8), (128, 20)))
    hi, lo = split_two(np.einsum("px,qy->xypq", ex, ey).reshape(512, 48))
    exy = np.concatenate([hi, hi, lo], axis=1)
    padded = lambda part: np.concatenate([np.tile(part, (6, 1)), np.zeros((8, 128), part.dtype)])
    return exy, np.concatenate([padded(part) for part in split_two(ez)], axis=1)


def shards(images, velocity):
    sizes = tuple(lax.axis_size(a) for a in AXES)
    nk = sizes[2]
    exy, ezs = fixed_tables()

    def send(v, di, dj, dk):
        return lax.ppermute(v, AXES, pairs(sizes, di, dj, dk))

    (pack,) = call(pack_kernel, [((2, 32, 128), f32)], [VMEM], bytes_accessed=6 * 10**5)(images)
    to_x, to_y, to_xy = call(
        slab_kernel,
        [((2, 8, 32, 128), f32), ((2, 16, 8, 128), f32), ((2, 9, 8, 128), f32)],
        [pl.BlockSpec(memory_space=pl.ANY), VMEM],
        bytes_accessed=10**6,
    )(pack, images)
    zr = lax.ppermute(pack, "gz", [(n, (n + 1) % nk) for n in range(nk)])
    yr = send(to_y, 0, 1, 0)
    xr = send(to_x, 1, 0, 0)

    velocity = jnp.swapaxes(velocity, 3, 4).reshape(6, 2, 16, 32)
    vel, wxy, wzs, xsum, zsum = call(
        prep_kernel,
        [((16, 128), f32), ((80, 512), bf16), ((128, 256), bf16), ((256, 128), bf16), ((256, 128), f32)],
        [VMEM],
        [pltpu.VMEM((128, 32), f32)],
        bytes_accessed=10**6,
    )(velocity)
    zr, vel = lax.optimization_barrier((zr, vel))
    top = zr[:, 24:]
    yzr = send(zr, 0, 1, 0)
    xyr = send(to_xy.at[:, 8].set(top), 1, 1, 0)
    xzr = send(zr, 1, 0, 0)

    def forces(upper, *arrays):
        return call(
            functools.partial(force_kernel, upper),
            [((40, 128), f32)],
            [VMEM] * (len(arrays) + 4),
            [
                pltpu.VMEM((2, 16, 40, 128), f32),
                pltpu.VMEM((2, 2, 40, 128), f32),
                pltpu.VMEM((2, 10, 40, 128), f32),
                pltpu.VMEM((2, 8, 40, 128), f32),
                pltpu.VMEM((5, 8, 40, 128), f32),
                pltpu.VMEM((5, 3, 32, 128), bf16),
                pltpu.VMEM((6, 256, 128), bf16),
                pltpu.VMEM((6, 256, 128), bf16),
            ],
            flops=5 * 10**8,
            bytes_accessed=10**6,
        )(*arrays, wxy, wzs, xsum, zsum)[0]

    part = forces(True, images, zr, yr, yzr, vel)
    part = forces(False, images, zr, yr, yzr, xr, xyr, xzr, part)

    swap = lambda v, axis, couples: lax.ppermute(v, axis, couples + [(b, a) for a, b in couples])
    chip = swap(part, "gz", [(1, 2), (3, 0)])
    core = swap(part, "gz", [(0, 1), (2, 3)])
    (own,) = call(fold_kernel, [((40, 128), f32)], [VMEM] * 3)(part, chip, core)
    far = swap(own, "gx", [(0, 2), (1, 3)])
    one = swap(own, "gx", [(0, 1), (2, 3)])
    two = swap(own, "gx", [(1, 2), (3, 0)])
    copies, mine = call(across_kernel, [((8, 32, 128), f32), ((48, 128), f32)], [VMEM] * 4)(own, far, one, two)
    everything = lax.all_to_all(copies, "gy", 0, 0, tiled=True)

    nv, field = call(
        field_kernel,
        [((6, 2, 16, 32), f32), ((6, 512, 128), bf16)],
        [VMEM] * 4,
        [pltpu.VMEM((2, 40, 128), f32), pltpu.VMEM((6, 512, 128), bf16), pltpu.SemaphoreType.DMA((3,))],
        out_specs=[VMEM, HBM],
        flops=10**8,
        bytes_accessed=10**6,
    )(everything, mine, exy, ezs)
    nv = jnp.swapaxes(nv.reshape(2, 3, 2, 16, 32), 3, 4)
    return nv, field.reshape(2, 3, 16, 32, 128)


def solution(mesh):
    placed = (P(None, "gx", "gy", "gz"), P(None, None, "gx", None, "gz"))
    return jax.shard_map(
        shards,
        mesh=mesh,
        in_specs=placed,
        out_specs=(P(None, None, "gx", None, "gz"), P(None, None, "gx", "gy", "gz")),
        check_vma=False,
    )
```

```python
import functools

import jax
import jax.numpy as jnp
import numpy as np
from jax import lax
from jax.experimental import pallas as pl
from jax.experimental.pallas import tpu as pltpu
from jax.sharding import PartitionSpec as P

epsilon_value = 1e-05
step_size = 0.5
AXES = ("gx", "gy", "gz")
f32 = jnp.float32
bf16 = jnp.bfloat16


def spline(t):
    m = np.abs(t)
    inside = 2.0 / 3.0 - m * m + 0.5 * m * m * m
    out = np.maximum(2.0 - m, 0.0)
    return np.where(m < 1.0, inside, out * out * out / 6.0)


def split_two(w):
    hi = w.astype(np.float32).astype(jnp.bfloat16)
    lo = (w - hi.astype(np.float64)).astype(np.float32).astype(jnp.bfloat16)
    return hi, lo


def pack_kernel(img_ref, out_ref):
    lane = lax.broadcasted_iota(jnp.int32, (32, 128), 1)
    for h in range(2):
        packed = jnp.zeros((32, 128), f32)
        for t in range(16):
            moved = pltpu.roll(img_ref[h, t], (8 * t + 8) % 128, 1)
            packed = jnp.where((lane >= 8 * t) & (lane < 8 * t + 8), moved, packed)
        out_ref[h] = packed


def slab_kernel(after_ref, img_ref, x_ref, y_ref, xy_ref):
    for h in range(2):
        for t in range(16):
            y_ref[h, t] = img_ref[h, t, 24:32]
            if t >= 8:
                x_ref[h, t - 8] = img_ref[h, t]
                xy_ref[h, t - 8] = img_ref[h, t, 24:32]
        xy_ref[h, 8] = jnp.zeros((8, 128), f32)


def spline_at(t):
    m = jnp.abs(t)
    inside = 2.0 / 3.0 - m * m + 0.5 * m * m * m
    out = jnp.maximum(2.0 - m, 0.0)
    return jnp.where(m < 1.0, inside, out * out * out / 6.0)


def weights(voxel, point):
    return spline_at((voxel.astype(f32) - 8.0 * point.astype(f32) - 3.5) * 0.125)


def prep_kernel(vel_ref, vel_out, wxy_out, wz_out, xsum_out, zsum_out, rows_ref):
    i, j, k = coords()
    ni, nj, nk = (lax.axis_size(a) for a in AXES)
    ex = jnp.where(i == 0, 0.0, 1.0)
    ez = jnp.where(k == 0, 0.0, 1.0)
    row = lax.broadcasted_iota(jnp.int32, (40, 512), 0)
    col = lax.broadcasted_iota(jnp.int32, (40, 512), 1)
    p = lax.shift_right_logical(row, 3)
    q = row & 7
    o = lax.shift_right_logical(col, 5)
    r = col & 31
    ok = ((p < 2) == (o < 4)) | (i != 0)
    ok = ok & (((q < 2) == (r < 4)) | (j != 0)) & (q < 7)
    ok = ok & ((p < 4) | (i != ni - 1)) & ((q < 6) | (j != nj - 1))
    table = jnp.where(ok, weights(o - 4, p - 2) * weights(r - 4, q - 2), 0.0)
    hi, lo = split2(table)
    wxy_out[...] = jnp.concatenate([hi.astype(f32), lo.astype(f32)], axis=0).astype(bf16)
    lane = lax.broadcasted_iota(jnp.int32, (128, 128), 1)
    sub = lax.broadcasted_iota(jnp.int32, (128, 128), 0)
    spot = lax.rem(lane, 20)
    ok = ((spot < 2) == (sub >= 124)) | (k != 0)
    ok = ok & (spot < 19) & ((spot < 18) | (k != nk - 1))
    voxel = jnp.where(sub >= 124, sub - 128, sub)
    hi, lo = split2(jnp.where(ok, weights(voxel, spot - 2), 0.0))
    wz_out[...] = jnp.concatenate([hi, lo], axis=1)

    src = lax.broadcasted_iota(jnp.int32, (256, 128), 0)
    dst = lax.broadcasted_iota(jnp.int32, (256, 128), 1)
    plane = jnp.where(src < 128, lax.shift_right_logical(src, 3) + 8, lax.shift_right_logical(src - 128, 3) - 8)
    goal = lax.shift_right_logical(dst, 3)
    near = (plane >= goal) & (plane <= goal + 8) & ((src & 7) == (dst & 7)) & (plane >= 0)
    across = (plane < 8) != (goal < 4)
    xsum_out[...] = jnp.where(near, jnp.where(across, ex, 1.0), 0.0).astype(bf16)
    centre = jnp.where(dst < 124, dst, dst - 128)
    below = src >= 128
    place = jnp.where(below, (src & 7) - 8, src)
    gap = place - centre
    inside = (gap <= 4) & (gap >= -4)
    crossing = below != (dst >= 124)
    zsum_out[...] = jnp.where(inside, jnp.where(crossing, ez, 1.0), 0.0)

    pick_q = lax.broadcasted_iota(jnp.int32, (8, 32), 0)
    pick_y = lax.broadcasted_iota(jnp.int32, (8, 32), 1)
    pick = ((pick_y == 4 * j + pick_q - 2) & (pick_q >= 2) & (pick_q < 6)).astype(f32).astype(bf16)
    for side in range(2):
        rows_ref[...] = jnp.zeros((128, 32), f32)
        for c in range(6):
            rows_ref[20 * c + 2 : 20 * c + 18] = vel_ref[c, side]
        turned = jnp.transpose(rows_ref[...])
        total = jnp.zeros((8, 128), f32)
        for piece in split3(turned):
            total = total + dot(pick, piece)
        vel_out[8 * side : 8 * side + 8] = total


def coords():
    return tuple(lax.axis_index(a) for a in AXES)


def split3(v):
    hi = v.astype(bf16)
    r = v - hi.astype(f32)
    mid = r.astype(bf16)
    lo = (r - mid.astype(f32)).astype(bf16)
    return hi, mid, lo


def split2(v):
    hi = v.astype(bf16)
    return hi, (v - hi.astype(f32)).astype(bf16)


def dot(a, b):
    return jnp.dot(a, b, preferred_element_type=f32)


def up_by(v, n, row):
    size = v.shape[0]
    return jnp.where(row < size - n, pltpu.roll(v, size - n, 0), 0.0)


def rows_window(v, head, tail, row8):
    first = v[0:8]
    own = jnp.concatenate([jnp.zeros((8, 128), f32), v[8:40]], axis=0)
    s = first + up_by(first, 1, row8)
    s = s + up_by(s, 2, row8)
    s = s + up_by(s, 4, row8)
    w = own + pltpu.roll(own, 39, 0)
    w = w + pltpu.roll(w, 38, 0)
    w = w + pltpu.roll(w, 36, 0)
    w = w[0:32] + own[8:40]
    top = head * s + tail * w[0:8]
    return jnp.concatenate([top, w[8:32]], axis=0)


def force_kernel(upper, own_ref, zr_ref, yr_ref, yzr_ref, *refs):
    if upper:
        base_ref, *refs = refs
    else:
        xr_ref, xyr_ref, xzr_ref, base_ref, *refs = refs
    wxy_ref, wz_ref, xsum_ref, zsum_ref, out_ref, a_ref, h_ref, v_ref, dz_ref, xs_ref, hs_ref, fh_ref, fl_ref = refs
    first = 8 if upper else 0
    ex, ey, ez = (jnp.where(at == 0, 0.0, 1.0) for at in coords())
    row8 = lax.broadcasted_iota(jnp.int32, (8, 128), 0)
    row32 = lax.broadcasted_iota(jnp.int32, (32, 128), 0)
    lane40 = lax.broadcasted_iota(jnp.int32, (40, 128), 1)
    head = jnp.where(row8 < 4, 1.0, ey)
    tail = jnp.where(row8 < 4, ey, 1.0)

    for h in range(2):
        for n in range(16):
            if upper or n >= 8:
                t = n if upper else n - 8
                a_ref[h, n, 8:40] = own_ref[h, t]
                a_ref[h, n, 0:8] = yr_ref[h, t]
            else:
                a_ref[h, n, 8:40] = xr_ref[h, n]
                a_ref[h, n, 0:8] = xyr_ref[h, n]
        h_ref[h, 0, 8:40] = zr_ref[h]
        h_ref[h, 0, 0:8] = yzr_ref[h, 24:32]
        if not upper:
            h_ref[h, 1, 8:40] = xzr_ref[h]
            h_ref[h, 1, 0:8] = xyr_ref[h, 8]

    plus_z = jnp.where(lane40 == 127, ez, 1.0)
    minus_z = jnp.where(lane40 == 0, ez, 1.0)
    for h in range(2):
        for n in range(3, 13):
            l = n + first
            if l >= 8:
                halo = pltpu.roll(h_ref[h, 0], (120 - 8 * (l - 8)) % 128, 1)
            else:
                halo = pltpu.roll(h_ref[h, 1], (120 - 8 * (l + 8)) % 128, 1)
            v_ref[h, n - 3] = jnp.where(lane40 >= 124, halo, a_ref[h, n])
            if 4 <= n < 12:
                dz_ref[h, n - 4] = halo
    for h in range(2):
        for n in range(4, 12):
            a = a_ref[h, n]
            halo = dz_ref[h, n - 4]
            up = pltpu.roll(jnp.where(lane40 >= 125, halo, a), 127, 1)
            down = pltpu.roll(jnp.where(lane40 >= 123, halo, a), 1, 1)
            dz_ref[h, n - 4] = plus_z * up - minus_z * down

    def x_step(tile, carry):
        rows = pl.ds(pl.multiple_of(tile * 8, 8), 8)
        for q in range(5):
            p = []
            for n in range(16):
                if q == 4:
                    p.append(a_ref[0, n, rows] * a_ref[1, n, rows])
                else:
                    value = a_ref[q % 2, n, rows]
                    p.append(value if q < 2 else value * value)
            if upper:
                b = [p[n] + p[n + 1] for n in range(15)]
                b = [b[n] + b[n + 2] for n in range(13)]
                b = [b[n] + b[n + 4] for n in range(9)]
                for o in range(8):
                    xs_ref[q, o, rows] = b[o] + p[o + 8]
                continue
            left = [None] * 8
            left[7] = p[7]
            for o in range(6, -1, -1):
                left[o] = left[o + 1] + p[o]
            right = p[8]
            for o in range(8):
                if o > 0:
                    right = right + p[o + 8]
                xs_ref[q, o, rows] = left[o] + ex * right if o < 4 else ex * left[o] + right
        return carry

    lax.fori_loop(0, 5, x_step, 0)

    sides = 1 if upper else 2
    x_sum = xsum_ref[0 : 128 * sides]
    for q in range(5):
        parts = []
        for side in range(sides):
            f = h_ref[0, side]
            m = h_ref[1, side]
            value = (f, m, f * f, m * m, f * m)[q]
            parts.append(rows_window(value, head, tail, row8))
        total = jnp.zeros((32, 128), f32)
        for piece in split3(jnp.concatenate(parts, axis=1)):
            total = total + dot(piece, x_sum)
        for n, piece in enumerate(split3(total)):
            hs_ref[q, n] = piece

    from_row = lax.broadcasted_iota(jnp.int32, (256, 128), 0)
    plus_y = jnp.where(row32 == 3, ey, 1.0)
    minus_y = jnp.where(row32 == 4, ey, 1.0)

    def o_step(o, carry):
        mine = (from_row < 128) | (lax.shift_right_logical(from_row - 128, 3) == o + first)
        z_sum = jnp.where(mine, zsum_ref[...], 0.0).astype(bf16)
        pieces = [[], [], []]
        for q in range(5):
            y = rows_window(xs_ref[q, o], head, tail, row8)
            for n, piece in enumerate(split3(y)):
                pieces[n].append(jnp.concatenate([piece, hs_ref[q, n]], axis=1))
        big = dot(jnp.concatenate(pieces[0] + pieces[1] + pieces[2], axis=0), z_sum)
        sums = (big[0:160] + big[160:320]) + big[320:480]
        sums = sums * (1.0 / 729.0)
        mean_f = sums[0:32]
        mean_m = sums[32:64]
        var_f = sums[64:96] - mean_f * mean_f + epsilon_value
        var_m = sums[96:128] - mean_m * mean_m + epsilon_value
        cov = sums[128:160] - mean_f * mean_m
        off_f = v_ref[0, o + 1, 4:36] - mean_f
        off_m = v_ref[1, o + 1, 4:36] - mean_m
        inv = 1.0 / (var_f * var_m)
        factor = cov * inv
        pulls = (
            factor * (off_m - factor * var_m * off_f),
            factor * (off_f - factor * var_f * off_m),
        )
        plus_x = jnp.where(o + first == 3, ex, 1.0)
        minus_x = jnp.where(o + first == 4, ex, 1.0)
        where_to = pl.ds(pl.multiple_of(o * 32, 32), 32)
        for h in range(2):
            dx = plus_x * v_ref[h, o + 2, 4:36] - minus_x * v_ref[h, o, 4:36]
            dy = plus_y * v_ref[h, o + 1, 5:37] - minus_y * v_ref[h, o + 1, 3:35]
            dz = dz_ref[h, o, 4:36]
            for c, d in enumerate((dx, dy, dz)):
                hi, lo = split2(pulls[h] * d)
                fh_ref[3 * h + c, where_to] = hi
                fl_ref[3 * h + c, where_to] = lo
        return carry

    lax.fori_loop(0, 8, o_step, 0, unroll=8)

    cols = slice(32 * first, 32 * first + 256)
    wxy = wxy_ref[:, cols]
    wxy_hi = wxy_ref[0:40, cols]
    planes = []
    for c in range(6):
        one = dot(wxy, fh_ref[c])
        planes.append(one[0:40] + one[40:80] + dot(wxy_hi, fl_ref[c]))
    hi, lo = split2(jnp.concatenate(planes, axis=0))
    along = dot(jnp.concatenate([hi, lo], axis=0), wz_ref[...])
    along = (along[0:240, 0:128] + along[0:240, 128:256]) + along[240:480, 0:128]
    which = lax.div(lax.broadcasted_iota(jnp.int32, (40, 128), 1), 20)
    total = jnp.zeros((40, 128), f32)
    for c in range(6):
        total = total + jnp.where(which == c, along[40 * c : 40 * c + 40], 0.0)
    total = step_size * total
    if upper:
        out_ref[0:16] = total[0:16]
        out_ref[16:32] = total[16:32] + base_ref[...]
        out_ref[32:40] = total[32:40]
    else:
        out_ref[...] = total + base_ref[...]


def fold_kernel(mine_ref, chip_ref, core_ref, out_ref):
    lane = lax.broadcasted_iota(jnp.int32, (40, 128), 1)
    spot = lax.rem(lane, 20)
    live = lane < 120
    odd = (lax.axis_index("gz") & 1) == 1
    chip, core = chip_ref[...], core_ref[...]
    low = pltpu.roll(jnp.where(odd, core, chip), 112, 1)
    high = pltpu.roll(jnp.where(odd, chip, core), 16, 1)
    total = mine_ref[...]
    total = total + jnp.where(live & (spot < 3), low, 0.0)
    out_ref[...] = total + jnp.where(live & (spot >= 16), high, 0.0)


def across_kernel(own_ref, far_ref, one_ref, two_ref, out_ref, mine_ref):
    odd = (lax.axis_index("gx") & 1) == 1
    tiles = lambda ref: [ref[8 * p : 8 * p + 8] for p in range(5)]
    own, one, two, far = tiles(own_ref), tiles(one_ref), tiles(two_ref), tiles(far_ref)
    below = [jnp.where(odd, a, b) for a, b in zip(one, two)]
    above = [jnp.where(odd, b, a) for a, b in zip(one, two)]
    window = [
        own[0] + below[2] + far[4],
        own[1] + below[3],
        own[2] + below[4] + above[0],
        own[3] + above[1],
        own[4] + above[2] + far[0],
        above[3] + far[1],
    ]
    for w in range(6):
        mine_ref[8 * w : 8 * w + 8] = window[w]
    low_half = lax.broadcasted_iota(jnp.int32, (8, 128), 0) < 4
    upper, lower = [], []
    for w in (0, 4):
        upper.append(jnp.where(low_half, pltpu.roll(window[w], 4, 0), window[w + 1]))
        lower.append(jnp.where(low_half, window[w], pltpu.roll(window[w + 1], 4, 0)))
    following = lax.rem(lax.axis_index("gy") + 1, 8)
    for n in range(8):
        out_ref[n, 0:8] = window[2]
        out_ref[n, 8:16] = window[3]
        for m in range(2):
            out_ref[n, 16 + 8 * m : 24 + 8 * m] = jnp.where(following == n, upper[m], lower[m])


def field_kernel(g_ref, mine_ref, wxy_ref, wz_ref, nv_ref, field_ref, rows_ref, buf_ref, own_ref, sems):
    me_i, me_j, me_k = coords()
    ni, nj, nk = (lax.axis_size(a) for a in AXES)
    row8 = lax.broadcasted_iota(jnp.int32, (8, 128), 0)

    window = []
    before, after = lax.rem(me_j + 7, 8), lax.rem(me_j + 1, 8)
    for w in range(6):
        at = 8 * (w - 2) if 2 <= w <= 3 else 16 + 8 * (w // 4)
        lows, highs = g_ref[before, at : at + 8], g_ref[after, at : at + 8]
        if w not in (0, 4):
            lows = pltpu.roll(lows, 4, 0)
        if w not in (1, 5):
            highs = pltpu.roll(highs, 4, 0)
        window.append(mine_ref[8 * w : 8 * w + 8] + jnp.where(row8 < 4, lows, highs))
    coefs = jnp.concatenate(window, axis=0)
    row = lax.broadcasted_iota(jnp.int32, (48, 128), 0)
    lane = lax.broadcasted_iota(jnp.int32, (48, 128), 1)
    at_x = 2 * me_i - 2 + lax.shift_right_logical(row, 3)
    at_y = 4 * me_j - 2 + (row & 7)
    at_z = 16 * me_k - 2 + lax.rem(lane, 20)
    real = (at_x >= 0) & (at_x < 2 * ni) & (at_y >= 0) & (at_y < 4 * nj)
    real = real & (at_z >= 0) & (at_z < 16 * nk) & (lane < 120)
    part = lax.div(lane, 20)
    coefs = jnp.where(real, coefs, 0.0)
    hi, lo = split2(jnp.concatenate([jnp.where(part == c, coefs, 0.0) for c in range(6)], axis=0))
    along = dot(jnp.concatenate([hi, lo], axis=0), wz_ref[...])
    along = (along[0:288, 0:128] + along[0:288, 128:256]) + along[288:576, 0:128]
    ch, cl = split2(along)
    copies = []
    for pair in range(3):
        rhs = []
        for c in (2 * pair, 2 * pair + 1):
            rows = slice(48 * c, 48 * c + 48)
            rhs.append(jnp.concatenate([ch[rows], cl[rows], ch[rows]], axis=0))
        both = dot(wxy_ref[...], jnp.concatenate(rhs, axis=1)).astype(bf16)
        for n in range(2):
            buf_ref[2 * pair + n] = both[:, 128 * n : 128 * n + 128]
        there = pl.ds(2 * pair, 2)
        copy = pltpu.make_async_copy(buf_ref.at[there], field_ref.at[there], sems.at[pair])
        copy.start()
        copies.append(copy)

    for side in range(2):
        cols = [g_ref[j, 8 * side : 8 * side + 8] for j in range(8)]
        turned = [pltpu.roll(c, 4, 0) for c in cols]
        tiles = []
        zero = jnp.zeros((8, 128), f32)
        for n in range(5):
            even = cols[2 * n] if n < 4 else zero
            high = turned[2 * n + 1] if n < 4 else zero
            low = turned[2 * n - 1] if n > 0 else zero
            tiles.append(even + jnp.where(row8 < 4, low, high))
        tiles[4] = tiles[4] + tiles[0]
        for n in range(5):
            rows_ref[side, 8 * n : 8 * n + 8] = tiles[n]
        block = jnp.transpose(rows_ref[side, 2:34])
        for c in range(6):
            own_ref[c, side] = block[20 * c + 2 : 20 * c + 18]
    copy = pltpu.make_async_copy(own_ref, nv_ref, sems.at[3])
    copy.start()
    copies.append(copy)
    for copy in copies:
        copy.wait()


VMEM = pl.BlockSpec(memory_space=pltpu.VMEM)


HBM = pl.BlockSpec(memory_space=pltpu.HBM)


def call(body, out_shape, in_specs, scratch=(), out_specs=None, flops=0, bytes_accessed=0):
    return pl.pallas_call(
        body,
        out_shape=[jax.ShapeDtypeStruct(shape, dtype) for shape, dtype in out_shape],
        in_specs=in_specs,
        out_specs=out_specs or [VMEM] * len(out_shape),
        scratch_shapes=list(scratch),
        compiler_params=pltpu.CompilerParams(vmem_limit_bytes=48 << 20),
        cost_estimate=pl.CostEstimate(flops=flops, bytes_accessed=bytes_accessed, transcendentals=0),
    )


def pairs(mesh_sizes, di, dj, dk):
    ni, nj, nk = mesh_sizes
    out = []
    for i in range(ni):
        for j in range(nj):
            for k in range(nk):
                to = (((i + di) % ni) * nj + (j + dj) % nj) * nk + (k + dk) % nk
                out.append(((i * nj + j) * nk + k, to))
    return out


def fixed_tables():
    weight = lambda n, points: spline((np.arange(n)[None, :] - 8.0 * (np.arange(points) - 2)[:, None] - 3.5) / 8.0)
    ex, ey, ez = (weight(n, points) for n, points in ((16, 6), (32, 8), (128, 20)))
    hi, lo = split_two(np.einsum("px,qy->xypq", ex, ey).reshape(512, 48))
    exy = np.concatenate([hi, hi, lo], axis=1)
    padded = lambda part: np.concatenate([np.tile(part, (6, 1)), np.zeros((8, 128), part.dtype)])
    return exy, np.concatenate([padded(part) for part in split_two(ez)], axis=1)


def shards(images, velocity):
    sizes = tuple(lax.axis_size(a) for a in AXES)
    nk = sizes[2]
    exy, ezs = fixed_tables()

    def send(v, di, dj, dk):
        return lax.ppermute(v, AXES, pairs(sizes, di, dj, dk))

    (pack,) = call(pack_kernel, [((2, 32, 128), f32)], [VMEM], bytes_accessed=6 * 10**5)(images)
    to_x, to_y, to_xy = call(
        slab_kernel,
        [((2, 8, 32, 128), f32), ((2, 16, 8, 128), f32), ((2, 9, 8, 128), f32)],
        [pl.BlockSpec(memory_space=pl.ANY), VMEM],
        bytes_accessed=10**6,
    )(pack, images)
    zr = lax.ppermute(pack, "gz", [(n, (n + 1) % nk) for n in range(nk)])
    yr = send(to_y, 0, 1, 0)
    xr = send(to_x, 1, 0, 0)

    velocity = jnp.swapaxes(velocity, 3, 4).reshape(6, 2, 16, 32)
    vel, wxy, wzs, xsum, zsum = call(
        prep_kernel,
        [((16, 128), f32), ((80, 512), bf16), ((128, 256), bf16), ((256, 128), bf16), ((256, 128), f32)],
        [VMEM],
        [pltpu.VMEM((128, 32), f32)],
        bytes_accessed=10**6,
    )(velocity)
    zr, vel = lax.optimization_barrier((zr, vel))
    top = zr[:, 24:]
    yzr = send(zr, 0, 1, 0)
    xyr = send(to_xy.at[:, 8].set(top), 1, 1, 0)
    xzr = send(zr, 1, 0, 0)

    def forces(upper, *arrays):
        return call(
            functools.partial(force_kernel, upper),
            [((40, 128), f32)],
            [VMEM] * (len(arrays) + 4),
            [
                pltpu.VMEM((2, 16, 40, 128), f32),
                pltpu.VMEM((2, 2, 40, 128), f32),
                pltpu.VMEM((2, 10, 40, 128), f32),
                pltpu.VMEM((2, 8, 40, 128), f32),
                pltpu.VMEM((5, 8, 40, 128), f32),
                pltpu.VMEM((5, 3, 32, 128), bf16),
                pltpu.VMEM((6, 256, 128), bf16),
                pltpu.VMEM((6, 256, 128), bf16),
            ],
            flops=5 * 10**8,
            bytes_accessed=10**6,
        )(*arrays, wxy, wzs, xsum, zsum)[0]

    part = forces(True, images, zr, yr, yzr, vel)
    part = forces(False, images, zr, yr, yzr, xr, xyr, xzr, part)

    swap = lambda v, axis, couples: lax.ppermute(v, axis, couples + [(b, a) for a, b in couples])
    chip = swap(part, "gz", [(1, 2), (3, 0)])
    core = swap(part, "gz", [(0, 1), (2, 3)])
    (own,) = call(fold_kernel, [((40, 128), f32)], [VMEM] * 3)(part, chip, core)
    far = swap(own, "gx", [(0, 2), (1, 3)])
    one = swap(own, "gx", [(0, 1), (2, 3)])
    two = swap(own, "gx", [(1, 2), (3, 0)])
    copies, mine = call(across_kernel, [((8, 32, 128), f32), ((48, 128), f32)], [VMEM] * 4)(own, far, one, two)
    everything = lax.all_to_all(copies, "gy", 0, 0, tiled=True)

    nv, field = call(
        field_kernel,
        [((6, 2, 16, 32), f32), ((6, 512, 128), bf16)],
        [VMEM] * 4,
        [pltpu.VMEM((2, 40, 128), f32), pltpu.VMEM((6, 512, 128), bf16), pltpu.VMEM((6, 2, 16, 32), f32), pltpu.SemaphoreType.DMA((4,))],
        out_specs=[HBM, HBM],
        flops=10**8,
        bytes_accessed=10**6,
    )(everything, mine, exy, ezs)
    nv = jnp.swapaxes(nv.reshape(2, 3, 2, 16, 32), 3, 4)
    return nv, field.reshape(2, 3, 16, 32, 128)


def solution(mesh):
    placed = (P(None, "gx", "gy", "gz"), P(None, None, "gx", None, "gz"))
    return jax.shard_map(
        shards,
        mesh=mesh,
        in_specs=placed,
        out_specs=(P(None, None, "gx", None, "gz"), P(None, None, "gx", "gy", "gz")),
        check_vma=False,
    )
```

```python
import functools

import jax
import jax.numpy as jnp
import numpy as np
from jax import lax
from jax.experimental import pallas as pl
from jax.experimental.pallas import tpu as pltpu
from jax.sharding import PartitionSpec as P

epsilon_value = 1e-05
step_size = 0.5
AXES = ("gx", "gy", "gz")
f32 = jnp.float32
bf16 = jnp.bfloat16


def spline(t):
    m = np.abs(t)
    inside = 2.0 / 3.0 - m * m + 0.5 * m * m * m
    out = np.maximum(2.0 - m, 0.0)
    return np.where(m < 1.0, inside, out * out * out / 6.0)


def split_two(w):
    hi = w.astype(np.float32).astype(jnp.bfloat16)
    lo = (w - hi.astype(np.float64)).astype(np.float32).astype(jnp.bfloat16)
    return hi, lo


def pack_kernel(img_ref, out_ref):
    lane = lax.broadcasted_iota(jnp.int32, (32, 128), 1)
    for h in range(2):
        packed = jnp.zeros((32, 128), f32)
        for t in range(16):
            moved = pltpu.roll(img_ref[h, t], (8 * t + 8) % 128, 1)
            packed = jnp.where((lane >= 8 * t) & (lane < 8 * t + 8), moved, packed)
        out_ref[h] = packed


def slab_kernel(after_ref, img_ref, x_ref, y_ref, xy_ref):
    for h in range(2):
        for t in range(16):
            y_ref[h, t] = img_ref[h, t, 24:32]
            if t >= 8:
                x_ref[h, t - 8] = img_ref[h, t]
                xy_ref[h, t - 8] = img_ref[h, t, 24:32]
        xy_ref[h, 8] = jnp.zeros((8, 128), f32)


def spline_at(t):
    m = jnp.abs(t)
    inside = 2.0 / 3.0 - m * m + 0.5 * m * m * m
    out = jnp.maximum(2.0 - m, 0.0)
    return jnp.where(m < 1.0, inside, out * out * out / 6.0)


def weights(voxel, point):
    return spline_at((voxel.astype(f32) - 8.0 * point.astype(f32) - 3.5) * 0.125)


def prep_kernel(vel_ref, vel_out, wxy_out, wz_out, xsum_out, zsum_out, rows_ref):
    i, j, k = coords()
    ni, nj, nk = (lax.axis_size(a) for a in AXES)
    ex = jnp.where(i == 0, 0.0, 1.0)
    ez = jnp.where(k == 0, 0.0, 1.0)
    row = lax.broadcasted_iota(jnp.int32, (40, 512), 0)
    col = lax.broadcasted_iota(jnp.int32, (40, 512), 1)
    p = lax.shift_right_logical(row, 3)
    q = row & 7
    o = lax.shift_right_logical(col, 5)
    r = col & 31
    ok = ((p < 2) == (o < 4)) | (i != 0)
    ok = ok & (((q < 2) == (r < 4)) | (j != 0)) & (q < 7)
    ok = ok & ((p < 4) | (i != ni - 1)) & ((q < 6) | (j != nj - 1))
    table = jnp.where(ok, weights(o - 4, p - 2) * weights(r - 4, q - 2), 0.0)
    hi, lo = split2(table)
    wxy_out[...] = jnp.concatenate([hi.astype(f32), lo.astype(f32)], axis=0).astype(bf16)
    lane = lax.broadcasted_iota(jnp.int32, (128, 128), 1)
    sub = lax.broadcasted_iota(jnp.int32, (128, 128), 0)
    spot = lax.rem(lane, 20)
    ok = ((spot < 2) == (sub >= 124)) | (k != 0)
    ok = ok & (spot < 19) & ((spot < 18) | (k != nk - 1))
    voxel = jnp.where(sub >= 124, sub - 128, sub)
    hi, lo = split2(jnp.where(ok, weights(voxel, spot - 2), 0.0))
    wz_out[...] = jnp.concatenate([hi, lo], axis=1)

    src = lax.broadcasted_iota(jnp.int32, (256, 128), 0)
    dst = lax.broadcasted_iota(jnp.int32, (256, 128), 1)
    plane = jnp.where(src < 128, lax.shift_right_logical(src, 3) + 8, lax.shift_right_logical(src - 128, 3) - 8)
    goal = lax.shift_right_logical(dst, 3)
    near = (plane >= goal) & (plane <= goal + 8) & ((src & 7) == (dst & 7)) & (plane >= 0)
    across = (plane < 8) != (goal < 4)
    xsum_out[...] = jnp.where(near, jnp.where(across, ex, 1.0), 0.0).astype(bf16)
    centre = jnp.where(dst < 124, dst, dst - 128)
    below = src >= 128
    place = jnp.where(below, (src & 7) - 8, src)
    gap = place - centre
    inside = (gap <= 4) & (gap >= -4)
    crossing = below != (dst >= 124)
    zsum_out[...] = jnp.where(inside, jnp.where(crossing, ez, 1.0), 0.0)

    pick_q = lax.broadcasted_iota(jnp.int32, (8, 32), 0)
    pick_y = lax.broadcasted_iota(jnp.int32, (8, 32), 1)
    pick = ((pick_y == 4 * j + pick_q - 2) & (pick_q >= 2) & (pick_q < 6)).astype(f32).astype(bf16)
    for side in range(2):
        rows_ref[...] = jnp.zeros((128, 32), f32)
        for c in range(6):
            rows_ref[20 * c + 2 : 20 * c + 18] = vel_ref[c, side]
        turned = jnp.transpose(rows_ref[...])
        total = jnp.zeros((8, 128), f32)
        for piece in split3(turned):
            total = total + dot(pick, piece)
        vel_out[8 * side : 8 * side + 8] = total


def coords():
    return tuple(lax.axis_index(a) for a in AXES)


def split3(v):
    hi = v.astype(bf16)
    r = v - hi.astype(f32)
    mid = r.astype(bf16)
    lo = (r - mid.astype(f32)).astype(bf16)
    return hi, mid, lo


def split2(v):
    hi = v.astype(bf16)
    return hi, (v - hi.astype(f32)).astype(bf16)


def dot(a, b):
    return jnp.dot(a, b, preferred_element_type=f32)


def up_by(v, n, row):
    size = v.shape[0]
    return jnp.where(row < size - n, pltpu.roll(v, size - n, 0), 0.0)


def rows_window(v, head, tail, row8):
    first = v[0:8]
    own = jnp.concatenate([jnp.zeros((8, 128), f32), v[8:40]], axis=0)
    s = first + up_by(first, 1, row8)
    s = s + up_by(s, 2, row8)
    s = s + up_by(s, 4, row8)
    w = own + pltpu.roll(own, 39, 0)
    w = w + pltpu.roll(w, 38, 0)
    w = w + pltpu.roll(w, 36, 0)
    w = w[0:32] + own[8:40]
    top = head * s + tail * w[0:8]
    return jnp.concatenate([top, w[8:32]], axis=0)


def force_kernel(upper, own_ref, zr_ref, yr_ref, yzr_ref, *refs):
    if upper:
        base_ref, *refs = refs
        wxy_ref, wz_ref, xsum_ref, zsum_ref, out_ref, vown_ref, dzown_ref, xown_ref, hown_ref, *refs = refs
    else:
        xr_ref, xyr_ref, xzr_ref, base_ref, vown_ref, dzown_ref, xown_ref, hown_ref, *refs = refs
        wxy_ref, wz_ref, xsum_ref, zsum_ref, out_ref, *refs = refs
    a_ref, h_ref, v_ref, dz_ref, xs_ref, hs_ref, fh_ref, fl_ref = refs
    first = 8 if upper else 0
    ex, ey, ez = (jnp.where(at == 0, 0.0, 1.0) for at in coords())
    row8 = lax.broadcasted_iota(jnp.int32, (8, 128), 0)
    row32 = lax.broadcasted_iota(jnp.int32, (32, 128), 0)
    lane40 = lax.broadcasted_iota(jnp.int32, (40, 128), 1)
    head = jnp.where(row8 < 4, 1.0, ey)
    tail = jnp.where(row8 < 4, ey, 1.0)

    for h in range(2):
        for n in range(16 if upper else 8):
            a_ref[h, n, 8:40] = own_ref[h, n] if upper else xr_ref[h, n]
            a_ref[h, n, 0:8] = yr_ref[h, n] if upper else xyr_ref[h, n]
        if upper:
            h_ref[h, 0, 8:40] = zr_ref[h]
            h_ref[h, 0, 0:8] = yzr_ref[h, 24:32]
        else:
            h_ref[h, 1, 8:40] = xzr_ref[h]
            h_ref[h, 1, 0:8] = xyr_ref[h, 8]

    plus_z = jnp.where(lane40 == 127, ez, 1.0)
    minus_z = jnp.where(lane40 == 0, ez, 1.0)
    def centre(h, n):
        if upper:
            return v_ref.at[h, n - 3]
        return v_ref.at[h, n - 3] if n < 8 else vown_ref.at[h, n - 8]

    def slope(h, n):
        if upper:
            return dz_ref.at[h, n - 4] if n >= 4 else dzown_ref.at[h, n]
        return dz_ref.at[h, n - 4] if n < 8 else dzown_ref.at[h, n - 8]

    planes = range(0, 13) if upper else range(3, 8)
    sloped = range(0, 12) if upper else range(4, 8)
    for h in range(2):
        for n in planes:
            if upper:
                halo = pltpu.roll(h_ref[h, 0], (120 - 8 * n) % 128, 1)
            else:
                halo = pltpu.roll(h_ref[h, 1], (120 - 8 * (n + 8)) % 128, 1)
            value = jnp.where(lane40 >= 124, halo, a_ref[h, n])
            if upper and n < 5:
                vown_ref[h, n] = value
            if not upper or n >= 3:
                v_ref[h, n - 3] = value
            if n in sloped:
                slope(h, n)[...] = halo
    for h in range(2):
        for n in sloped:
            a = a_ref[h, n]
            halo = slope(h, n)[...]
            up = pltpu.roll(jnp.where(lane40 >= 125, halo, a), 127, 1)
            down = pltpu.roll(jnp.where(lane40 >= 123, halo, a), 1, 1)
            slope(h, n)[...] = plus_z * up - minus_z * down

    def x_step(tile, carry):
        rows = pl.ds(pl.multiple_of(tile * 8, 8), 8)
        for q in range(5):
            p = []
            for n in range(16 if upper else 8):
                if q == 4:
                    p.append(a_ref[0, n, rows] * a_ref[1, n, rows])
                else:
                    value = a_ref[q % 2, n, rows]
                    p.append(value if q < 2 else value * value)
            if upper:
                b = [p[n] + p[n + 1] for n in range(15)]
                b = [b[n] + b[n + 2] for n in range(13)]
                b = [b[n] + b[n + 4] for n in range(9)]
                right = p[0]
                for o in range(8):
                    xs_ref[q, o, rows] = b[o] + p[o + 8]
                    if o > 0:
                        right = right + p[o]
                    xown_ref[q, o, rows] = right
                continue
            left = [None] * 8
            left[7] = p[7]
            for o in range(6, -1, -1):
                left[o] = left[o + 1] + p[o]
            for o in range(8):
                right = xown_ref[q, o, rows]
                xs_ref[q, o, rows] = left[o] + ex * right if o < 4 else ex * left[o] + right
        return carry

    lax.fori_loop(0, 5, x_step, 0)

    side = 0 if upper else 1
    x_sum = xsum_ref[128 * side : 128 * side + 128]
    for q in range(5):
        f = h_ref[0, side]
        m = h_ref[1, side]
        value = (f, m, f * f, m * m, f * m)[q]
        total = jnp.zeros((32, 128), f32) if upper else hown_ref[q]
        for piece in split3(rows_window(value, head, tail, row8)):
            total = total + dot(piece, x_sum)
        if upper:
            hown_ref[q] = total
        for n, piece in enumerate(split3(total)):
            hs_ref[q, n] = piece

    from_row = lax.broadcasted_iota(jnp.int32, (256, 128), 0)
    plus_y = jnp.where(row32 == 3, ey, 1.0)
    minus_y = jnp.where(row32 == 4, ey, 1.0)

    for o in range(8):
        mine = (from_row < 128) | (lax.shift_right_logical(from_row - 128, 3) == o + first)
        z_sum = jnp.where(mine, zsum_ref[...], 0.0).astype(bf16)
        pieces = [[], [], []]
        for q in range(5):
            y = rows_window(xs_ref[q, o], head, tail, row8)
            for n, piece in enumerate(split3(y)):
                pieces[n].append(jnp.concatenate([piece, hs_ref[q, n]], axis=1))
        big = dot(jnp.concatenate(pieces[0] + pieces[1] + pieces[2], axis=0), z_sum)
        sums = (big[0:160] + big[160:320]) + big[320:480]
        sums = sums * (1.0 / 729.0)
        mean_f = sums[0:32]
        mean_m = sums[32:64]
        var_f = sums[64:96] - mean_f * mean_f + epsilon_value
        var_m = sums[96:128] - mean_m * mean_m + epsilon_value
        cov = sums[128:160] - mean_f * mean_m
        off_f = centre(0, o + 4)[4:36] - mean_f
        off_m = centre(1, o + 4)[4:36] - mean_m
        inv = 1.0 / (var_f * var_m)
        factor = cov * inv
        pulls = (
            factor * (off_m - factor * var_m * off_f),
            factor * (off_f - factor * var_f * off_m),
        )
        plus_x = ex if o + first == 3 else 1.0
        minus_x = ex if o + first == 4 else 1.0
        where_to = slice(32 * o, 32 * o + 32)
        for h in range(2):
            dx = plus_x * centre(h, o + 5)[4:36] - minus_x * centre(h, o + 3)[4:36]
            dy = plus_y * centre(h, o + 4)[5:37] - minus_y * centre(h, o + 4)[3:35]
            dz = slope(h, o + 4)[4:36]
            for c, d in enumerate((dx, dy, dz)):
                hi, lo = split2(pulls[h] * d)
                fh_ref[3 * h + c, where_to] = hi
                fl_ref[3 * h + c, where_to] = lo

    cols = slice(32 * first, 32 * first + 256)
    wxy = wxy_ref[:, cols]
    wxy_hi = wxy_ref[0:40, cols]
    lattice = []
    for c in range(6):
        one = dot(wxy, fh_ref[c])
        lattice.append(one[0:40] + one[40:80] + dot(wxy_hi, fl_ref[c]))
    hi, lo = split2(jnp.concatenate(lattice, axis=0))
    along = dot(jnp.concatenate([hi, lo], axis=0), wz_ref[...])
    along = (along[0:240, 0:128] + along[0:240, 128:256]) + along[240:480, 0:128]
    which = lax.div(lax.broadcasted_iota(jnp.int32, (40, 128), 1), 20)
    total = jnp.zeros((40, 128), f32)
    for c in range(6):
        total = total + jnp.where(which == c, along[40 * c : 40 * c + 40], 0.0)
    total = step_size * total
    if upper:
        out_ref[0:16] = total[0:16]
        out_ref[16:32] = total[16:32] + base_ref[...]
        out_ref[32:40] = total[32:40]
    else:
        out_ref[...] = total + base_ref[...]


def fold_kernel(mine_ref, chip_ref, core_ref, out_ref):
    lane = lax.broadcasted_iota(jnp.int32, (40, 128), 1)
    spot = lax.rem(lane, 20)
    live = lane < 120
    odd = (lax.axis_index("gz") & 1) == 1
    chip, core = chip_ref[...], core_ref[...]
    low = pltpu.roll(jnp.where(odd, core, chip), 112, 1)
    high = pltpu.roll(jnp.where(odd, chip, core), 16, 1)
    total = mine_ref[...]
    total = total + jnp.where(live & (spot < 3), low, 0.0)
    out_ref[...] = total + jnp.where(live & (spot >= 16), high, 0.0)


def across_kernel(own_ref, far_ref, one_ref, two_ref, out_ref, mine_ref):
    odd = (lax.axis_index("gx") & 1) == 1
    tiles = lambda ref: [ref[8 * p : 8 * p + 8] for p in range(5)]
    own, one, two, far = tiles(own_ref), tiles(one_ref), tiles(two_ref), tiles(far_ref)
    below = [jnp.where(odd, a, b) for a, b in zip(one, two)]
    above = [jnp.where(odd, b, a) for a, b in zip(one, two)]
    window = [
        own[0] + below[2] + far[4],
        own[1] + below[3],
        own[2] + below[4] + above[0],
        own[3] + above[1],
        own[4] + above[2] + far[0],
        above[3] + far[1],
    ]
    for w in range(6):
        mine_ref[8 * w : 8 * w + 8] = window[w]
    low_half = lax.broadcasted_iota(jnp.int32, (8, 128), 0) < 4
    upper, lower = [], []
    for w in (0, 4):
        upper.append(jnp.where(low_half, pltpu.roll(window[w], 4, 0), window[w + 1]))
        lower.append(jnp.where(low_half, window[w], pltpu.roll(window[w + 1], 4, 0)))
    following = lax.rem(lax.axis_index("gy") + 1, 8)
    for n in range(8):
        out_ref[n, 0:8] = window[2]
        out_ref[n, 8:16] = window[3]
        for m in range(2):
            out_ref[n, 16 + 8 * m : 24 + 8 * m] = jnp.where(following == n, upper[m], lower[m])


def field_kernel(g_ref, mine_ref, wxy_ref, wz_ref, nv_ref, field_ref, rows_ref, buf_ref, own_ref, sems):
    me_i, me_j, me_k = coords()
    ni, nj, nk = (lax.axis_size(a) for a in AXES)
    row8 = lax.broadcasted_iota(jnp.int32, (8, 128), 0)

    window = []
    before, after = lax.rem(me_j + 7, 8), lax.rem(me_j + 1, 8)
    for w in range(6):
        at = 8 * (w - 2) if 2 <= w <= 3 else 16 + 8 * (w // 4)
        lows, highs = g_ref[before, at : at + 8], g_ref[after, at : at + 8]
        if w not in (0, 4):
            lows = pltpu.roll(lows, 4, 0)
        if w not in (1, 5):
            highs = pltpu.roll(highs, 4, 0)
        window.append(mine_ref[8 * w : 8 * w + 8] + jnp.where(row8 < 4, lows, highs))
    coefs = jnp.concatenate(window, axis=0)
    row = lax.broadcasted_iota(jnp.int32, (48, 128), 0)
    lane = lax.broadcasted_iota(jnp.int32, (48, 128), 1)
    at_x = 2 * me_i - 2 + lax.shift_right_logical(row, 3)
    at_y = 4 * me_j - 2 + (row & 7)
    at_z = 16 * me_k - 2 + lax.rem(lane, 20)
    real = (at_x >= 0) & (at_x < 2 * ni) & (at_y >= 0) & (at_y < 4 * nj)
    real = real & (at_z >= 0) & (at_z < 16 * nk) & (lane < 120)
    part = lax.div(lane, 20)
    coefs = jnp.where(real, coefs, 0.0)
    hi, lo = split2(jnp.concatenate([jnp.where(part == c, coefs, 0.0) for c in range(6)], axis=0))
    along = dot(jnp.concatenate([hi, lo], axis=0), wz_ref[...])
    along = (along[0:288, 0:128] + along[0:288, 128:256]) + along[288:576, 0:128]
    ch, cl = split2(along)
    copies = []
    for pair in range(3):
        rhs = []
        for c in (2 * pair, 2 * pair + 1):
            rows = slice(48 * c, 48 * c + 48)
            rhs.append(jnp.concatenate([ch[rows], cl[rows], ch[rows]], axis=0))
        both = dot(wxy_ref[...], jnp.concatenate(rhs, axis=1)).astype(bf16)
        for n in range(2):
            buf_ref[2 * pair + n] = both[:, 128 * n : 128 * n + 128]
        there = pl.ds(2 * pair, 2)
        copy = pltpu.make_async_copy(buf_ref.at[there], field_ref.at[there], sems.at[pair])
        copy.start()
        copies.append(copy)

    for side in range(2):
        cols = [g_ref[j, 8 * side : 8 * side + 8] for j in range(8)]
        turned = [pltpu.roll(c, 4, 0) for c in cols]
        tiles = []
        zero = jnp.zeros((8, 128), f32)
        for n in range(5):
            even = cols[2 * n] if n < 4 else zero
            high = turned[2 * n + 1] if n < 4 else zero
            low = turned[2 * n - 1] if n > 0 else zero
            tiles.append(even + jnp.where(row8 < 4, low, high))
        tiles[4] = tiles[4] + tiles[0]
        for n in range(5):
            rows_ref[side, 8 * n : 8 * n + 8] = tiles[n]
        block = jnp.transpose(rows_ref[side, 2:34])
        for c in range(6):
            own_ref[c, side] = block[20 * c + 2 : 20 * c + 18]
    copy = pltpu.make_async_copy(own_ref, nv_ref, sems.at[3])
    copy.start()
    copies.append(copy)
    for copy in copies:
        copy.wait()


VMEM = pl.BlockSpec(memory_space=pltpu.VMEM)


HBM = pl.BlockSpec(memory_space=pltpu.HBM)


def call(body, out_shape, in_specs, scratch=(), out_specs=None, flops=0, bytes_accessed=0):
    return pl.pallas_call(
        body,
        out_shape=[jax.ShapeDtypeStruct(shape, dtype) for shape, dtype in out_shape],
        in_specs=in_specs,
        out_specs=out_specs or [VMEM] * len(out_shape),
        scratch_shapes=list(scratch),
        compiler_params=pltpu.CompilerParams(vmem_limit_bytes=48 << 20),
        cost_estimate=pl.CostEstimate(flops=flops, bytes_accessed=bytes_accessed, transcendentals=0),
    )


def pairs(mesh_sizes, di, dj, dk):
    ni, nj, nk = mesh_sizes
    out = []
    for i in range(ni):
        for j in range(nj):
            for k in range(nk):
                to = (((i + di) % ni) * nj + (j + dj) % nj) * nk + (k + dk) % nk
                out.append(((i * nj + j) * nk + k, to))
    return out


def fixed_tables():
    weight = lambda n, points: spline((np.arange(n)[None, :] - 8.0 * (np.arange(points) - 2)[:, None] - 3.5) / 8.0)
    ex, ey, ez = (weight(n, points) for n, points in ((16, 6), (32, 8), (128, 20)))
    hi, lo = split_two(np.einsum("px,qy->xypq", ex, ey).reshape(512, 48))
    exy = np.concatenate([hi, hi, lo], axis=1)
    padded = lambda part: np.concatenate([np.tile(part, (6, 1)), np.zeros((8, 128), part.dtype)])
    return exy, np.concatenate([padded(part) for part in split_two(ez)], axis=1)


def shards(images, velocity):
    sizes = tuple(lax.axis_size(a) for a in AXES)
    nk = sizes[2]
    exy, ezs = fixed_tables()

    def send(v, di, dj, dk):
        return lax.ppermute(v, AXES, pairs(sizes, di, dj, dk))

    (pack,) = call(pack_kernel, [((2, 32, 128), f32)], [VMEM], bytes_accessed=6 * 10**5)(images)
    to_x, to_y, to_xy = call(
        slab_kernel,
        [((2, 8, 32, 128), f32), ((2, 16, 8, 128), f32), ((2, 9, 8, 128), f32)],
        [pl.BlockSpec(memory_space=pl.ANY), VMEM],
        bytes_accessed=10**6,
    )(pack, images)
    zr = lax.ppermute(pack, "gz", [(n, (n + 1) % nk) for n in range(nk)])
    yr = send(to_y, 0, 1, 0)
    xr = send(to_x, 1, 0, 0)

    velocity = jnp.swapaxes(velocity, 3, 4).reshape(6, 2, 16, 32)
    vel, wxy, wzs, xsum, zsum = call(
        prep_kernel,
        [((16, 128), f32), ((80, 512), bf16), ((128, 256), bf16), ((256, 128), bf16), ((256, 128), f32)],
        [VMEM],
        [pltpu.VMEM((128, 32), f32)],
        bytes_accessed=10**6,
    )(velocity)
    zr, vel = lax.optimization_barrier((zr, vel))
    top = zr[:, 24:]
    yzr = send(zr, 0, 1, 0)
    xyr = send(to_xy.at[:, 8].set(top), 1, 1, 0)
    xzr = send(zr, 1, 0, 0)

    def forces(upper, more, *arrays):
        return call(
            functools.partial(force_kernel, upper),
            [((40, 128), f32)] + [(shape, f32) for shape in more],
            [VMEM] * (len(arrays) + 4),
            [
                pltpu.VMEM((2, 16, 40, 128), f32),
                pltpu.VMEM((2, 2, 40, 128), f32),
                pltpu.VMEM((2, 10, 40, 128), f32),
                pltpu.VMEM((2, 8, 40, 128), f32),
                pltpu.VMEM((5, 8, 40, 128), f32),
                pltpu.VMEM((5, 3, 32, 128), bf16),
                pltpu.VMEM((6, 256, 128), bf16),
                pltpu.VMEM((6, 256, 128), bf16),
            ],
            flops=5 * 10**8,
            bytes_accessed=10**6,
        )(*arrays, wxy, wzs, xsum, zsum)

    shared = [(2, 5, 40, 128), (2, 4, 40, 128), (5, 8, 40, 128), (5, 32, 128)]
    part, *own_parts = forces(True, shared, images, zr, yr, yzr, vel)
    (part,) = forces(False, (), images, zr, yr, yzr, xr, xyr, xzr, part, *own_parts)

    swap = lambda v, axis, couples: lax.ppermute(v, axis, couples + [(b, a) for a, b in couples])
    chip = swap(part, "gz", [(1, 2), (3, 0)])
    core = swap(part, "gz", [(0, 1), (2, 3)])
    (own,) = call(fold_kernel, [((40, 128), f32)], [VMEM] * 3)(part, chip, core)
    far = swap(own, "gx", [(0, 2), (1, 3)])
    one = swap(own, "gx", [(0, 1), (2, 3)])
    two = swap(own, "gx", [(1, 2), (3, 0)])
    copies, mine = call(across_kernel, [((8, 32, 128), f32), ((48, 128), f32)], [VMEM] * 4)(own, far, one, two)
    everything = lax.all_to_all(copies, "gy", 0, 0, tiled=True)

    nv, field = call(
        field_kernel,
        [((6, 2, 16, 32), f32), ((6, 512, 128), bf16)],
        [VMEM] * 4,
        [pltpu.VMEM((2, 40, 128), f32), pltpu.VMEM((6, 512, 128), bf16), pltpu.VMEM((6, 2, 16, 32), f32), pltpu.SemaphoreType.DMA((4,))],
        out_specs=[HBM, HBM],
        flops=10**8,
        bytes_accessed=10**6,
    )(everything, mine, exy, ezs)
    nv = jnp.swapaxes(nv.reshape(2, 3, 2, 16, 32), 3, 4)
    return nv, field.reshape(2, 3, 16, 32, 128)


def solution(mesh):
    placed = (P(None, "gx", "gy", "gz"), P(None, None, "gx", None, "gz"))
    return jax.shard_map(
        shards,
        mesh=mesh,
        in_specs=placed,
        out_specs=(P(None, None, "gx", None, "gz"), P(None, None, "gx", "gy", "gz")),
        check_vma=False,
    )
```

```python
import functools

import jax
import jax.numpy as jnp
import numpy as np
from jax import lax
from jax.experimental import pallas as pl
from jax.experimental.pallas import tpu as pltpu
from jax.sharding import PartitionSpec as P

epsilon_value = 1e-05
step_size = 0.5
AXES = ("gx", "gy", "gz")
f32 = jnp.float32
bf16 = jnp.bfloat16


def spline(t):
    m = np.abs(t)
    inside = 2.0 / 3.0 - m * m + 0.5 * m * m * m
    out = np.maximum(2.0 - m, 0.0)
    return np.where(m < 1.0, inside, out * out * out / 6.0)


def split_two(w):
    hi = w.astype(np.float32).astype(jnp.bfloat16)
    lo = (w - hi.astype(np.float64)).astype(np.float32).astype(jnp.bfloat16)
    return hi, lo


def pack_kernel(img_ref, out_ref):
    lane = lax.broadcasted_iota(jnp.int32, (32, 128), 1)
    for h in range(2):
        packed = jnp.zeros((32, 128), f32)
        for t in range(16):
            moved = pltpu.roll(img_ref[h, t], (8 * t + 8) % 128, 1)
            packed = jnp.where((lane >= 8 * t) & (lane < 8 * t + 8), moved, packed)
        out_ref[h] = packed


def slab_kernel(after_ref, img_ref, x_ref, y_ref, xy_ref):
    for h in range(2):
        for t in range(16):
            y_ref[h, t] = img_ref[h, t, 24:32]
            if t >= 8:
                x_ref[h, t - 8] = img_ref[h, t]
                xy_ref[h, t - 8] = img_ref[h, t, 24:32]
        xy_ref[h, 8] = jnp.zeros((8, 128), f32)


def spline_at(t):
    m = jnp.abs(t)
    inside = 2.0 / 3.0 - m * m + 0.5 * m * m * m
    out = jnp.maximum(2.0 - m, 0.0)
    return jnp.where(m < 1.0, inside, out * out * out / 6.0)


def weights(voxel, point):
    return spline_at((voxel.astype(f32) - 8.0 * point.astype(f32) - 3.5) * 0.125)


def prep_kernel(vel_ref, vel_out, wxy_out, wz_out, xsum_out, zsum_out, rows_ref):
    i, j, k = coords()
    ni, nj, nk = (lax.axis_size(a) for a in AXES)
    ex = jnp.where(i == 0, 0.0, 1.0)
    ez = jnp.where(k == 0, 0.0, 1.0)
    row = lax.broadcasted_iota(jnp.int32, (40, 512), 0)
    col = lax.broadcasted_iota(jnp.int32, (40, 512), 1)
    p = lax.shift_right_logical(row, 3)
    q = row & 7
    o = lax.shift_right_logical(col, 5)
    r = col & 31
    ok = ((p < 2) == (o < 4)) | (i != 0)
    ok = ok & (((q < 2) == (r < 4)) | (j != 0)) & (q < 7)
    ok = ok & ((p < 4) | (i != ni - 1)) & ((q < 6) | (j != nj - 1))
    table = jnp.where(ok, weights(o - 4, p - 2) * weights(r - 4, q - 2), 0.0)
    hi, lo = split2(table)
    wxy_out[...] = jnp.concatenate([hi.astype(f32), lo.astype(f32)], axis=0).astype(bf16)
    lane = lax.broadcasted_iota(jnp.int32, (128, 128), 1)
    sub = lax.broadcasted_iota(jnp.int32, (128, 128), 0)
    spot = lax.rem(lane, 20)
    ok = ((spot < 2) == (sub >= 124)) | (k != 0)
    ok = ok & (spot < 19) & ((spot < 18) | (k != nk - 1))
    voxel = jnp.where(sub >= 124, sub - 128, sub)
    hi, lo = split2(jnp.where(ok, weights(voxel, spot - 2), 0.0))
    wz_out[...] = jnp.concatenate([hi, lo], axis=1)

    src = lax.broadcasted_iota(jnp.int32, (256, 128), 0)
    dst = lax.broadcasted_iota(jnp.int32, (256, 128), 1)
    plane = jnp.where(src < 128, lax.shift_right_logical(src, 3) + 8, lax.shift_right_logical(src - 128, 3) - 8)
    goal = lax.shift_right_logical(dst, 3)
    near = (plane >= goal) & (plane <= goal + 8) & ((src & 7) == (dst & 7)) & (plane >= 0)
    across = (plane < 8) != (goal < 4)
    xsum_out[...] = jnp.where(near, jnp.where(across, ex, 1.0), 0.0).astype(bf16)
    centre = jnp.where(dst < 124, dst, dst - 128)
    below = src >= 128
    place = jnp.where(below, (src & 7) - 8, src)
    gap = place - centre
    inside = (gap <= 4) & (gap >= -4)
    crossing = below != (dst >= 124)
    zsum_out[...] = jnp.where(inside, jnp.where(crossing, ez, 1.0), 0.0)

    pick_q = lax.broadcasted_iota(jnp.int32, (8, 32), 0)
    pick_y = lax.broadcasted_iota(jnp.int32, (8, 32), 1)
    pick = ((pick_y == 4 * j + pick_q - 2) & (pick_q >= 2) & (pick_q < 6)).astype(f32).astype(bf16)
    for side in range(2):
        rows_ref[...] = jnp.zeros((128, 32), f32)
        for c in range(6):
            rows_ref[20 * c + 2 : 20 * c + 18] = vel_ref[c, side]
        turned = jnp.transpose(rows_ref[...])
        total = jnp.zeros((8, 128), f32)
        for piece in split3(turned):
            total = total + dot(pick, piece)
        vel_out[8 * side : 8 * side + 8] = total


def coords():
    return tuple(lax.axis_index(a) for a in AXES)


def split3(v):
    hi = v.astype(bf16)
    r = v - hi.astype(f32)
    mid = r.astype(bf16)
    lo = (r - mid.astype(f32)).astype(bf16)
    return hi, mid, lo


def split2(v):
    hi = v.astype(bf16)
    return hi, (v - hi.astype(f32)).astype(bf16)


def dot(a, b):
    return jnp.dot(a, b, preferred_element_type=f32)


def up_by(v, n, row):
    size = v.shape[0]
    return jnp.where(row < size - n, pltpu.roll(v, size - n, 0), 0.0)


def rows_window(v, head, tail, row8):
    first = v[0:8]
    own = jnp.concatenate([jnp.zeros((8, 128), f32), v[8:40]], axis=0)
    s = first + up_by(first, 1, row8)
    s = s + up_by(s, 2, row8)
    s = s + up_by(s, 4, row8)
    w = own + pltpu.roll(own, 39, 0)
    w = w + pltpu.roll(w, 38, 0)
    w = w + pltpu.roll(w, 36, 0)
    w = w[0:32] + own[8:40]
    top = head * s + tail * w[0:8]
    return jnp.concatenate([top, w[8:32]], axis=0)


def force_kernel(upper, own_ref, zr_ref, yr_ref, yzr_ref, *refs):
    if upper:
        base_ref, *refs = refs
        wxy_ref, wz_ref, xsum_ref, zsum_ref, out_ref, vown_ref, dzown_ref, xown_ref, hown_ref, *refs = refs
    else:
        xr_ref, xyr_ref, xzr_ref, base_ref, vown_ref, dzown_ref, xown_ref, hown_ref, *refs = refs
        wxy_ref, wz_ref, xsum_ref, zsum_ref, out_ref, *refs = refs
    a_ref, h_ref, v_ref, dz_ref, xs_ref, hs_ref, fh_ref, fl_ref = refs
    first = 8 if upper else 0
    ex, ey, ez = (jnp.where(at == 0, 0.0, 1.0) for at in coords())
    row8 = lax.broadcasted_iota(jnp.int32, (8, 128), 0)
    row32 = lax.broadcasted_iota(jnp.int32, (32, 128), 0)
    lane40 = lax.broadcasted_iota(jnp.int32, (40, 128), 1)
    head = jnp.where(row8 < 4, 1.0, ey)
    tail = jnp.where(row8 < 4, ey, 1.0)

    for h in range(2):
        for n in range(16 if upper else 8):
            a_ref[h, n, 8:40] = own_ref[h, n] if upper else xr_ref[h, n]
            a_ref[h, n, 0:8] = yr_ref[h, n] if upper else xyr_ref[h, n]
        if upper:
            h_ref[h, 0, 8:40] = zr_ref[h]
            h_ref[h, 0, 0:8] = yzr_ref[h, 24:32]
        else:
            h_ref[h, 1, 8:40] = xzr_ref[h]
            h_ref[h, 1, 0:8] = xyr_ref[h, 8]

    plus_z = jnp.where(lane40 == 127, ez, 1.0)
    minus_z = jnp.where(lane40 == 0, ez, 1.0)
    def centre(h, n):
        if upper:
            return v_ref.at[h, n - 3]
        return v_ref.at[h, n - 3] if n < 8 else vown_ref.at[h, n - 8]

    def slope(h, n):
        if upper:
            return dz_ref.at[h, n - 4] if n >= 4 else dzown_ref.at[h, n]
        return dz_ref.at[h, n - 4] if n < 8 else dzown_ref.at[h, n - 8]

    planes = range(0, 13) if upper else range(3, 8)
    sloped = range(0, 12) if upper else range(4, 8)
    for h in range(2):
        for n in planes:
            if upper:
                halo = pltpu.roll(h_ref[h, 0], (120 - 8 * n) % 128, 1)
            else:
                halo = pltpu.roll(h_ref[h, 1], (120 - 8 * (n + 8)) % 128, 1)
            value = jnp.where(lane40 >= 124, halo, a_ref[h, n])
            if upper and n < 5:
                vown_ref[h, n] = value
            if not upper or n >= 3:
                v_ref[h, n - 3] = value
            if n in sloped:
                slope(h, n)[...] = halo
    for h in range(2):
        for n in sloped:
            a = a_ref[h, n]
            halo = slope(h, n)[...]
            up = pltpu.roll(jnp.where(lane40 >= 125, halo, a), 127, 1)
            down = pltpu.roll(jnp.where(lane40 >= 123, halo, a), 1, 1)
            slope(h, n)[...] = plus_z * up - minus_z * down

    def x_step(tile, carry):
        rows = pl.ds(pl.multiple_of(tile * 8, 8), 8)
        for q in range(5):
            p = []
            for n in range(16 if upper else 8):
                if q == 4:
                    p.append(a_ref[0, n, rows] * a_ref[1, n, rows])
                else:
                    value = a_ref[q % 2, n, rows]
                    p.append(value if q < 2 else value * value)
            if upper:
                b = [p[n] + p[n + 1] for n in range(15)]
                b = [b[n] + b[n + 2] for n in range(13)]
                b = [b[n] + b[n + 4] for n in range(9)]
                right = p[0]
                for o in range(8):
                    xs_ref[q, o, rows] = b[o] + p[o + 8]
                    if o > 0:
                        right = right + p[o]
                    xown_ref[q, o, rows] = right
                continue
            left = [None] * 8
            left[7] = p[7]
            for o in range(6, -1, -1):
                left[o] = left[o + 1] + p[o]
            for o in range(8):
                right = xown_ref[q, o, rows]
                xs_ref[q, o, rows] = left[o] + ex * right if o < 4 else ex * left[o] + right
        return carry

    lax.fori_loop(0, 5, x_step, 0)

    side = 0 if upper else 1
    x_sum = xsum_ref[128 * side : 128 * side + 128]
    for q in range(5):
        f = h_ref[0, side]
        m = h_ref[1, side]
        value = (f, m, f * f, m * m, f * m)[q]
        total = jnp.zeros((32, 128), f32) if upper else hown_ref[q]
        for piece in split3(rows_window(value, head, tail, row8)):
            total = total + dot(piece, x_sum)
        if upper:
            hown_ref[q] = total
        for n, piece in enumerate(split3(total)):
            hs_ref[q, n] = piece

    from_row = lax.broadcasted_iota(jnp.int32, (256, 128), 0)
    plus_y = jnp.where(row32 == 3, ey, 1.0)
    minus_y = jnp.where(row32 == 4, ey, 1.0)

    for o in range(8):
        mine = (from_row < 128) | (lax.shift_right_logical(from_row - 128, 3) == o + first)
        z_sum = jnp.where(mine, zsum_ref[...], 0.0).astype(bf16)
        pieces = [[], [], []]
        for q in range(5):
            y = rows_window(xs_ref[q, o], head, tail, row8)
            for n, piece in enumerate(split3(y)):
                pieces[n].append(jnp.concatenate([piece, hs_ref[q, n]], axis=1))
        big = dot(jnp.concatenate(pieces[0] + pieces[1] + pieces[2], axis=0), z_sum)
        sums = (big[0:160] + big[160:320]) + big[320:480]
        sums = sums * (1.0 / 729.0)
        mean_f = sums[0:32]
        mean_m = sums[32:64]
        var_f = sums[64:96] - mean_f * mean_f + epsilon_value
        var_m = sums[96:128] - mean_m * mean_m + epsilon_value
        cov = sums[128:160] - mean_f * mean_m
        off_f = centre(0, o + 4)[4:36] - mean_f
        off_m = centre(1, o + 4)[4:36] - mean_m
        inv = 1.0 / (var_f * var_m)
        factor = cov * inv
        pulls = (
            factor * (off_m - factor * var_m * off_f),
            factor * (off_f - factor * var_f * off_m),
        )
        plus_x = ex if o + first == 3 else 1.0
        minus_x = ex if o + first == 4 else 1.0
        where_to = slice(32 * o, 32 * o + 32)
        for h in range(2):
            dx = plus_x * centre(h, o + 5)[4:36] - minus_x * centre(h, o + 3)[4:36]
            dy = plus_y * centre(h, o + 4)[5:37] - minus_y * centre(h, o + 4)[3:35]
            dz = slope(h, o + 4)[4:36]
            for c, d in enumerate((dx, dy, dz)):
                hi, lo = split2(pulls[h] * d)
                fh_ref[3 * h + c, where_to] = hi
                fl_ref[3 * h + c, where_to] = lo

    cols = slice(32 * first, 32 * first + 256)
    wxy = wxy_ref[:, cols]
    wxy_hi = wxy_ref[0:40, cols]
    lattice = []
    for c in range(6):
        one = dot(wxy, fh_ref[c])
        lattice.append(one[0:40] + one[40:80] + dot(wxy_hi, fl_ref[c]))
    hi, lo = split2(jnp.concatenate(lattice, axis=0))
    along = dot(jnp.concatenate([hi, lo], axis=0), wz_ref[...])
    along = (along[0:240, 0:128] + along[0:240, 128:256]) + along[240:480, 0:128]
    which = lax.div(lax.broadcasted_iota(jnp.int32, (40, 128), 1), 20)
    total = jnp.zeros((40, 128), f32)
    for c in range(6):
        total = total + jnp.where(which == c, along[40 * c : 40 * c + 40], 0.0)
    total = step_size * total
    if upper:
        out_ref[0:16] = total[0:16]
        out_ref[16:32] = total[16:32] + base_ref[...]
        out_ref[32:40] = total[32:40]
    else:
        out_ref[...] = total + base_ref[...]


def fold_kernel(mine_ref, core_ref, chip_ref, out_ref):
    lane = lax.broadcasted_iota(jnp.int32, (40, 128), 1)
    spot = lax.rem(lane, 20)
    live = lane < 120
    odd = (lax.axis_index("gz") & 1) == 1
    chip, core = chip_ref[...], core_ref[...]
    low = pltpu.roll(jnp.where(odd, core, chip), 112, 1)
    high = pltpu.roll(jnp.where(odd, chip, core), 16, 1)
    total = mine_ref[...]
    total = total + jnp.where(live & (spot < 3), low, 0.0)
    out_ref[...] = total + jnp.where(live & (spot >= 16), high, 0.0)


def across_kernel(own_ref, one_ref, two_ref, far_ref, out_ref, mine_ref):
    odd = (lax.axis_index("gx") & 1) == 1
    tiles = lambda ref: [ref[8 * p : 8 * p + 8] for p in range(5)]
    own, one, two, far = tiles(own_ref), tiles(one_ref), tiles(two_ref), tiles(far_ref)
    below = [jnp.where(odd, a, b) for a, b in zip(one, two)]
    above = [jnp.where(odd, b, a) for a, b in zip(one, two)]
    window = [
        own[0] + below[2] + far[4],
        own[1] + below[3],
        own[2] + below[4] + above[0],
        own[3] + above[1],
        own[4] + above[2] + far[0],
        above[3] + far[1],
    ]
    for w in range(6):
        mine_ref[8 * w : 8 * w + 8] = window[w]
    low_half = lax.broadcasted_iota(jnp.int32, (8, 128), 0) < 4
    upper, lower = [], []
    for w in (0, 4):
        upper.append(jnp.where(low_half, pltpu.roll(window[w], 4, 0), window[w + 1]))
        lower.append(jnp.where(low_half, window[w], pltpu.roll(window[w + 1], 4, 0)))
    following = lax.rem(lax.axis_index("gy") + 1, 8)
    for n in range(8):
        out_ref[n, 0:8] = window[2]
        out_ref[n, 8:16] = window[3]
        for m in range(2):
            out_ref[n, 16 + 8 * m : 24 + 8 * m] = jnp.where(following == n, upper[m], lower[m])


def field_kernel(g_ref, mine_ref, wxy_ref, wz_ref, nv_ref, field_ref, rows_ref, buf_ref, own_ref, sems):
    me_i, me_j, me_k = coords()
    ni, nj, nk = (lax.axis_size(a) for a in AXES)
    row8 = lax.broadcasted_iota(jnp.int32, (8, 128), 0)

    window = []
    before, after = lax.rem(me_j + 7, 8), lax.rem(me_j + 1, 8)
    for w in range(6):
        at = 8 * (w - 2) if 2 <= w <= 3 else 16 + 8 * (w // 4)
        lows, highs = g_ref[before, at : at + 8], g_ref[after, at : at + 8]
        if w not in (0, 4):
            lows = pltpu.roll(lows, 4, 0)
        if w not in (1, 5):
            highs = pltpu.roll(highs, 4, 0)
        window.append(mine_ref[8 * w : 8 * w + 8] + jnp.where(row8 < 4, lows, highs))
    coefs = jnp.concatenate(window, axis=0)
    row = lax.broadcasted_iota(jnp.int32, (48, 128), 0)
    lane = lax.broadcasted_iota(jnp.int32, (48, 128), 1)
    at_x = 2 * me_i - 2 + lax.shift_right_logical(row, 3)
    at_y = 4 * me_j - 2 + (row & 7)
    at_z = 16 * me_k - 2 + lax.rem(lane, 20)
    real = (at_x >= 0) & (at_x < 2 * ni) & (at_y >= 0) & (at_y < 4 * nj)
    real = real & (at_z >= 0) & (at_z < 16 * nk) & (lane < 120)
    part = lax.div(lane, 20)
    coefs = jnp.where(real, coefs, 0.0)
    hi, lo = split2(jnp.concatenate([jnp.where(part == c, coefs, 0.0) for c in range(6)], axis=0))
    along = dot(jnp.concatenate([hi, lo], axis=0), wz_ref[...])
    along = (along[0:288, 0:128] + along[0:288, 128:256]) + along[288:576, 0:128]
    ch, cl = split2(along)
    copies = []
    for pair in range(3):
        rhs = []
        for c in (2 * pair, 2 * pair + 1):
            rows = slice(48 * c, 48 * c + 48)
            rhs.append(jnp.concatenate([ch[rows], cl[rows], ch[rows]], axis=0))
        both = dot(wxy_ref[...], jnp.concatenate(rhs, axis=1)).astype(bf16)
        for n in range(2):
            buf_ref[2 * pair + n] = both[:, 128 * n : 128 * n + 128]
        there = pl.ds(2 * pair, 2)
        copy = pltpu.make_async_copy(buf_ref.at[there], field_ref.at[there], sems.at[pair])
        copy.start()
        copies.append(copy)

    for side in range(2):
        cols = [g_ref[j, 8 * side : 8 * side + 8] for j in range(8)]
        turned = [pltpu.roll(c, 4, 0) for c in cols]
        tiles = []
        zero = jnp.zeros((8, 128), f32)
        for n in range(5):
            even = cols[2 * n] if n < 4 else zero
            high = turned[2 * n + 1] if n < 4 else zero
            low = turned[2 * n - 1] if n > 0 else zero
            tiles.append(even + jnp.where(row8 < 4, low, high))
        tiles[4] = tiles[4] + tiles[0]
        for n in range(5):
            rows_ref[side, 8 * n : 8 * n + 8] = tiles[n]
        block = jnp.transpose(rows_ref[side, 2:34])
        for c in range(6):
            own_ref[c, side] = block[20 * c + 2 : 20 * c + 18]
    copy = pltpu.make_async_copy(own_ref, nv_ref, sems.at[3])
    copy.start()
    copies.append(copy)
    for copy in copies:
        copy.wait()


VMEM = pl.BlockSpec(memory_space=pltpu.VMEM)


HBM = pl.BlockSpec(memory_space=pltpu.HBM)


def call(body, out_shape, in_specs, scratch=(), out_specs=None, flops=0, bytes_accessed=0):
    return pl.pallas_call(
        body,
        out_shape=[jax.ShapeDtypeStruct(shape, dtype) for shape, dtype in out_shape],
        in_specs=in_specs,
        out_specs=out_specs or [VMEM] * len(out_shape),
        scratch_shapes=list(scratch),
        compiler_params=pltpu.CompilerParams(vmem_limit_bytes=48 << 20),
        cost_estimate=pl.CostEstimate(flops=flops, bytes_accessed=bytes_accessed, transcendentals=0),
    )


def pairs(mesh_sizes, di, dj, dk):
    ni, nj, nk = mesh_sizes
    out = []
    for i in range(ni):
        for j in range(nj):
            for k in range(nk):
                to = (((i + di) % ni) * nj + (j + dj) % nj) * nk + (k + dk) % nk
                out.append(((i * nj + j) * nk + k, to))
    return out


def fixed_tables():
    weight = lambda n, points: spline((np.arange(n)[None, :] - 8.0 * (np.arange(points) - 2)[:, None] - 3.5) / 8.0)
    ex, ey, ez = (weight(n, points) for n, points in ((16, 6), (32, 8), (128, 20)))
    hi, lo = split_two(np.einsum("px,qy->xypq", ex, ey).reshape(512, 48))
    exy = np.concatenate([hi, hi, lo], axis=1)
    padded = lambda part: np.concatenate([np.tile(part, (6, 1)), np.zeros((8, 128), part.dtype)])
    return exy, np.concatenate([padded(part) for part in split_two(ez)], axis=1)


def shards(images, velocity):
    sizes = tuple(lax.axis_size(a) for a in AXES)
    nk = sizes[2]
    exy, ezs = fixed_tables()

    def send(v, di, dj, dk):
        return lax.ppermute(v, AXES, pairs(sizes, di, dj, dk))

    (pack,) = call(pack_kernel, [((2, 32, 128), f32)], [VMEM], bytes_accessed=6 * 10**5)(images)
    to_x, to_y, to_xy = call(
        slab_kernel,
        [((2, 8, 32, 128), f32), ((2, 16, 8, 128), f32), ((2, 9, 8, 128), f32)],
        [pl.BlockSpec(memory_space=pl.ANY), VMEM],
        bytes_accessed=10**6,
    )(pack, images)
    zr = lax.ppermute(pack, "gz", [(n, (n + 1) % nk) for n in range(nk)])
    yr = send(to_y, 0, 1, 0)
    xr = send(to_x, 1, 0, 0)

    velocity = jnp.swapaxes(velocity, 3, 4).reshape(6, 2, 16, 32)
    vel, wxy, wzs, xsum, zsum = call(
        prep_kernel,
        [((16, 128), f32), ((80, 512), bf16), ((128, 256), bf16), ((256, 128), bf16), ((256, 128), f32)],
        [VMEM],
        [pltpu.VMEM((128, 32), f32)],
        bytes_accessed=10**6,
    )(velocity)
    zr, vel = lax.optimization_barrier((zr, vel))
    top = zr[:, 24:]
    yzr = send(zr, 0, 1, 0)
    xyr = send(to_xy.at[:, 8].set(top), 1, 1, 0)
    xzr = send(zr, 1, 0, 0)

    def forces(upper, more, *arrays):
        return call(
            functools.partial(force_kernel, upper),
            [((40, 128), f32)] + [(shape, f32) for shape in more],
            [VMEM] * (len(arrays) + 4),
            [
                pltpu.VMEM((2, 16, 40, 128), f32),
                pltpu.VMEM((2, 2, 40, 128), f32),
                pltpu.VMEM((2, 10, 40, 128), f32),
                pltpu.VMEM((2, 8, 40, 128), f32),
                pltpu.VMEM((5, 8, 40, 128), f32),
                pltpu.VMEM((5, 3, 32, 128), bf16),
                pltpu.VMEM((6, 256, 128), bf16),
                pltpu.VMEM((6, 256, 128), bf16),
            ],
            flops=5 * 10**8,
            bytes_accessed=10**6,
        )(*arrays, wxy, wzs, xsum, zsum)

    shared = [(2, 5, 40, 128), (2, 4, 40, 128), (5, 8, 40, 128), (5, 32, 128)]
    part, *own_parts = forces(True, shared, images, zr, yr, yzr, vel)
    (part,) = forces(False, (), images, zr, yr, yzr, xr, xyr, xzr, part, *own_parts)

    swap = lambda v, axis, couples: lax.ppermute(v, axis, couples + [(b, a) for a, b in couples])
    chip = swap(part, "gz", [(1, 2), (3, 0)])
    core = swap(part, "gz", [(0, 1), (2, 3)])
    (own,) = call(fold_kernel, [((40, 128), f32)], [VMEM] * 3)(part, core, chip)
    far = swap(own, "gx", [(0, 2), (1, 3)])
    one = swap(own, "gx", [(0, 1), (2, 3)])
    two = swap(own, "gx", [(1, 2), (3, 0)])
    copies, mine = call(across_kernel, [((8, 32, 128), f32), ((48, 128), f32)], [VMEM] * 4)(own, one, two, far)
    everything = lax.all_to_all(copies, "gy", 0, 0, tiled=True)

    nv, field = call(
        field_kernel,
        [((6, 2, 16, 32), f32), ((6, 512, 128), bf16)],
        [VMEM] * 4,
        [pltpu.VMEM((2, 40, 128), f32), pltpu.VMEM((6, 512, 128), bf16), pltpu.VMEM((6, 2, 16, 32), f32), pltpu.SemaphoreType.DMA((4,))],
        out_specs=[HBM, HBM],
        flops=10**8,
        bytes_accessed=10**6,
    )(everything, mine, exy, ezs)
    nv = jnp.swapaxes(nv.reshape(2, 3, 2, 16, 32), 3, 4)
    return nv, field.reshape(2, 3, 16, 32, 128)


def solution(mesh):
    placed = (P(None, "gx", "gy", "gz"), P(None, None, "gx", None, "gz"))
    return jax.shard_map(
        shards,
        mesh=mesh,
        in_specs=placed,
        out_specs=(P(None, None, "gx", None, "gz"), P(None, None, "gx", "gy", "gz")),
        check_vma=False,
    )
```

```python
import functools

import jax
import jax.numpy as jnp
import numpy as np
from jax import lax
from jax.experimental import pallas as pl
from jax.experimental.pallas import tpu as pltpu
from jax.sharding import PartitionSpec as P

epsilon_value = 1e-05
step_size = 0.5
AXES = ("gx", "gy", "gz")
f32 = jnp.float32
bf16 = jnp.bfloat16


def spline(t):
    m = np.abs(t)
    inside = 2.0 / 3.0 - m * m + 0.5 * m * m * m
    out = np.maximum(2.0 - m, 0.0)
    return np.where(m < 1.0, inside, out * out * out / 6.0)


def split_two(w):
    hi = w.astype(np.float32).astype(jnp.bfloat16)
    lo = (w - hi.astype(np.float64)).astype(np.float32).astype(jnp.bfloat16)
    return hi, lo


def pack_kernel(img_ref, out_ref):
    lane = lax.broadcasted_iota(jnp.int32, (32, 128), 1)
    for h in range(2):
        packed = jnp.zeros((32, 128), f32)
        for t in range(16):
            moved = pltpu.roll(img_ref[h, t], (8 * t + 8) % 128, 1)
            packed = jnp.where((lane >= 8 * t) & (lane < 8 * t + 8), moved, packed)
        out_ref[h] = packed


def slab_kernel(after_ref, img_ref, x_ref, y_ref, xy_ref):
    for h in range(2):
        for t in range(16):
            y_ref[h, t] = img_ref[h, t, 24:32]
            if t >= 8:
                x_ref[h, t - 8] = img_ref[h, t]
                xy_ref[h, t - 8] = img_ref[h, t, 24:32]
        xy_ref[h, 8] = jnp.zeros((8, 128), f32)


def spline_at(t):
    m = jnp.abs(t)
    inside = 2.0 / 3.0 - m * m + 0.5 * m * m * m
    out = jnp.maximum(2.0 - m, 0.0)
    return jnp.where(m < 1.0, inside, out * out * out / 6.0)


def weights(voxel, point):
    return spline_at((voxel.astype(f32) - 8.0 * point.astype(f32) - 3.5) * 0.125)


def prep_kernel(vel_ref, vel_out, wxy_out, wz_out, xsum_out, zsum_out, rows_ref):
    i, j, k = coords()
    ni, nj, nk = (lax.axis_size(a) for a in AXES)
    ex = jnp.where(i == 0, 0.0, 1.0)
    ez = jnp.where(k == 0, 0.0, 1.0)
    row = lax.broadcasted_iota(jnp.int32, (40, 512), 0)
    col = lax.broadcasted_iota(jnp.int32, (40, 512), 1)
    p = lax.shift_right_logical(row, 3)
    q = row & 7
    o = lax.shift_right_logical(col, 5)
    r = col & 31
    ok = ((p < 2) == (o < 4)) | (i != 0)
    ok = ok & (((q < 2) == (r < 4)) | (j != 0)) & (q < 7)
    ok = ok & ((p < 4) | (i != ni - 1)) & ((q < 6) | (j != nj - 1))
    table = jnp.where(ok, weights(o - 4, p - 2) * weights(r - 4, q - 2), 0.0)
    hi, lo = split2(table)
    wxy_out[...] = jnp.concatenate([hi.astype(f32), lo.astype(f32)], axis=0).astype(bf16)
    lane = lax.broadcasted_iota(jnp.int32, (128, 128), 1)
    sub = lax.broadcasted_iota(jnp.int32, (128, 128), 0)
    spot = lax.rem(lane, 20)
    ok = ((spot < 2) == (sub >= 124)) | (k != 0)
    ok = ok & (spot < 19) & ((spot < 18) | (k != nk - 1))
    voxel = jnp.where(sub >= 124, sub - 128, sub)
    hi, lo = split2(jnp.where(ok, weights(voxel, spot - 2), 0.0))
    wz_out[...] = jnp.concatenate([hi, lo], axis=1)

    src = lax.broadcasted_iota(jnp.int32, (256, 128), 0)
    dst = lax.broadcasted_iota(jnp.int32, (256, 128), 1)
    plane = jnp.where(src < 128, lax.shift_right_logical(src, 3) + 8, lax.shift_right_logical(src - 128, 3) - 8)
    goal = lax.shift_right_logical(dst, 3)
    near = (plane >= goal) & (plane <= goal + 8) & ((src & 7) == (dst & 7)) & (plane >= 0)
    across = (plane < 8) != (goal < 4)
    xsum_out[...] = jnp.where(near, jnp.where(across, ex, 1.0), 0.0).astype(bf16)
    centre = jnp.where(dst < 124, dst, dst - 128)
    below = src >= 128
    place = jnp.where(below, (src & 7) - 8, src)
    gap = place - centre
    inside = (gap <= 4) & (gap >= -4)
    crossing = below != (dst >= 124)
    zsum_out[...] = jnp.where(inside, jnp.where(crossing, ez, 1.0), 0.0)

    pick_q = lax.broadcasted_iota(jnp.int32, (8, 32), 0)
    pick_y = lax.broadcasted_iota(jnp.int32, (8, 32), 1)
    pick = ((pick_y == 4 * j + pick_q - 2) & (pick_q >= 2) & (pick_q < 6)).astype(f32).astype(bf16)
    for side in range(2):
        rows_ref[...] = jnp.zeros((128, 32), f32)
        for c in range(6):
            rows_ref[20 * c + 2 : 20 * c + 18] = vel_ref[c, side]
        turned = jnp.transpose(rows_ref[...])
        total = jnp.zeros((8, 128), f32)
        for piece in split3(turned):
            total = total + dot(pick, piece)
        vel_out[8 * side : 8 * side + 8] = total


def coords():
    return tuple(lax.axis_index(a) for a in AXES)


def split3(v):
    hi = v.astype(bf16)
    r = v - hi.astype(f32)
    mid = r.astype(bf16)
    lo = (r - mid.astype(f32)).astype(bf16)
    return hi, mid, lo


def split2(v):
    hi = v.astype(bf16)
    return hi, (v - hi.astype(f32)).astype(bf16)


def dot(a, b):
    return jnp.dot(a, b, preferred_element_type=f32)


def up_by(v, n, row):
    size = v.shape[0]
    return jnp.where(row < size - n, pltpu.roll(v, size - n, 0), 0.0)


def rows_window(v, head, tail, row8):
    first = v[0:8]
    own = jnp.concatenate([jnp.zeros((8, 128), f32), v[8:40]], axis=0)
    s = first + up_by(first, 1, row8)
    s = s + up_by(s, 2, row8)
    s = s + up_by(s, 4, row8)
    w = own + pltpu.roll(own, 39, 0)
    w = w + pltpu.roll(w, 38, 0)
    w = w + pltpu.roll(w, 36, 0)
    w = w[0:32] + own[8:40]
    top = head * s + tail * w[0:8]
    return jnp.concatenate([top, w[8:32]], axis=0)


def force_kernel(upper, own_ref, zr_ref, yr_ref, yzr_ref, *refs):
    if upper:
        base_ref, *refs = refs
        wxy_ref, wz_ref, xsum_ref, zsum_ref, out_ref, vown_ref, dzown_ref, xown_ref, hown_ref, *refs = refs
    else:
        xr_ref, xyr_ref, xzr_ref, base_ref, vown_ref, dzown_ref, xown_ref, hown_ref, *refs = refs
        wxy_ref, wz_ref, xsum_ref, zsum_ref, out_ref, *refs = refs
    a_ref, h_ref, v_ref, dz_ref, xs_ref, hs_ref, fh_ref, fl_ref = refs
    first = 8 if upper else 0
    ex, ey, ez = (jnp.where(at == 0, 0.0, 1.0) for at in coords())
    row8 = lax.broadcasted_iota(jnp.int32, (8, 128), 0)
    row32 = lax.broadcasted_iota(jnp.int32, (32, 128), 0)
    lane40 = lax.broadcasted_iota(jnp.int32, (40, 128), 1)
    head = jnp.where(row8 < 4, 1.0, ey)
    tail = jnp.where(row8 < 4, ey, 1.0)

    for h in range(2):
        for n in range(16 if upper else 8):
            a_ref[h, n, 8:40] = own_ref[h, n] if upper else xr_ref[h, n]
            a_ref[h, n, 0:8] = yr_ref[h, n] if upper else xyr_ref[h, n]
        if upper:
            h_ref[h, 0, 8:40] = zr_ref[h]
            h_ref[h, 0, 0:8] = yzr_ref[h, 24:32]
        else:
            h_ref[h, 1, 8:40] = xzr_ref[h]
            h_ref[h, 1, 0:8] = xyr_ref[h, 8]

    plus_z = jnp.where(lane40 == 127, ez, 1.0)
    minus_z = jnp.where(lane40 == 0, ez, 1.0)
    def centre(h, n):
        if upper:
            return v_ref.at[h, n - 3]
        return v_ref.at[h, n - 3] if n < 8 else vown_ref.at[h, n - 8]

    def slope(h, n):
        if upper:
            return dz_ref.at[h, n - 4] if n >= 4 else dzown_ref.at[h, n]
        return dz_ref.at[h, n - 4] if n < 8 else dzown_ref.at[h, n - 8]

    planes = range(0, 13) if upper else range(3, 8)
    sloped = range(0, 12) if upper else range(4, 8)
    for h in range(2):
        for n in planes:
            if upper:
                halo = pltpu.roll(h_ref[h, 0], (120 - 8 * n) % 128, 1)
            else:
                halo = pltpu.roll(h_ref[h, 1], (120 - 8 * (n + 8)) % 128, 1)
            value = jnp.where(lane40 >= 124, halo, a_ref[h, n])
            if upper and n < 5:
                vown_ref[h, n] = value
            if not upper or n >= 3:
                v_ref[h, n - 3] = value
            if n in sloped:
                slope(h, n)[...] = halo
    for h in range(2):
        for n in sloped:
            a = a_ref[h, n]
            halo = slope(h, n)[...]
            up = pltpu.roll(jnp.where(lane40 >= 125, halo, a), 127, 1)
            down = pltpu.roll(jnp.where(lane40 >= 123, halo, a), 1, 1)
            slope(h, n)[...] = plus_z * up - minus_z * down

    for tile in range(5):
        rows = slice(8 * tile, 8 * tile + 8)
        for q in range(5):
            p = []
            for n in range(16 if upper else 8):
                if q == 4:
                    p.append(a_ref[0, n, rows] * a_ref[1, n, rows])
                else:
                    value = a_ref[q % 2, n, rows]
                    p.append(value if q < 2 else value * value)
            if upper:
                b = [p[n] + p[n + 1] for n in range(15)]
                b = [b[n] + b[n + 2] for n in range(13)]
                b = [b[n] + b[n + 4] for n in range(9)]
                right = p[0]
                for o in range(8):
                    xs_ref[q, o, rows] = b[o] + p[o + 8]
                    if o > 0:
                        right = right + p[o]
                    xown_ref[q, o, rows] = right
                continue
            left = [None] * 8
            left[7] = p[7]
            for o in range(6, -1, -1):
                left[o] = left[o + 1] + p[o]
            for o in range(8):
                right = xown_ref[q, o, rows]
                xs_ref[q, o, rows] = left[o] + ex * right if o < 4 else ex * left[o] + right

    side = 0 if upper else 1
    x_sum = xsum_ref[128 * side : 128 * side + 128]
    for q in range(5):
        f = h_ref[0, side]
        m = h_ref[1, side]
        value = (f, m, f * f, m * m, f * m)[q]
        total = jnp.zeros((32, 128), f32) if upper else hown_ref[q]
        for piece in split3(rows_window(value, head, tail, row8)):
            total = total + dot(piece, x_sum)
        if upper:
            hown_ref[q] = total
        for n, piece in enumerate(split3(total)):
            hs_ref[q, n] = piece

    group = lax.shift_right_logical(lax.broadcasted_iota(jnp.int32, (128, 128), 0), 3)
    z_own = zsum_ref[0:128].astype(bf16)
    z_halo = zsum_ref[128:256]
    plus_y = jnp.where(row32 == 3, ey, 1.0)
    minus_y = jnp.where(row32 == 4, ey, 1.0)

    for o in range(8):
        z_sum = jnp.concatenate([z_own, jnp.where(group == o + first, z_halo, 0.0).astype(bf16)], axis=0)
        pieces = [[], [], []]
        for q in range(5):
            y = rows_window(xs_ref[q, o], head, tail, row8)
            for n, piece in enumerate(split3(y)):
                pieces[n].append(jnp.concatenate([piece, hs_ref[q, n]], axis=1))
        big = dot(jnp.concatenate(pieces[0] + pieces[1] + pieces[2], axis=0), z_sum)
        sums = (big[0:160] + big[160:320]) + big[320:480]
        sums = sums * (1.0 / 729.0)
        mean_f = sums[0:32]
        mean_m = sums[32:64]
        var_f = sums[64:96] - mean_f * mean_f + epsilon_value
        var_m = sums[96:128] - mean_m * mean_m + epsilon_value
        cov = sums[128:160] - mean_f * mean_m
        off_f = centre(0, o + 4)[4:36] - mean_f
        off_m = centre(1, o + 4)[4:36] - mean_m
        inv = 1.0 / (var_f * var_m)
        factor = cov * inv
        pulls = (
            factor * (off_m - factor * var_m * off_f),
            factor * (off_f - factor * var_f * off_m),
        )
        plus_x = ex if o + first == 3 else 1.0
        minus_x = ex if o + first == 4 else 1.0
        where_to = slice(32 * o, 32 * o + 32)
        for h in range(2):
            dx = plus_x * centre(h, o + 5)[4:36] - minus_x * centre(h, o + 3)[4:36]
            dy = plus_y * centre(h, o + 4)[5:37] - minus_y * centre(h, o + 4)[3:35]
            dz = slope(h, o + 4)[4:36]
            for c, d in enumerate((dx, dy, dz)):
                hi, lo = split2(pulls[h] * d)
                fh_ref[3 * h + c, where_to] = hi
                fl_ref[3 * h + c, where_to] = lo

    cols = slice(32 * first, 32 * first + 256)
    wxy = wxy_ref[:, cols]
    wxy_hi = wxy_ref[0:40, cols]
    lattice = []
    for c in range(6):
        one = dot(wxy, fh_ref[c])
        lattice.append(one[0:40] + one[40:80] + dot(wxy_hi, fl_ref[c]))
    hi, lo = split2(jnp.concatenate(lattice, axis=0))
    along = dot(jnp.concatenate([hi, lo], axis=0), wz_ref[...])
    along = (along[0:240, 0:128] + along[0:240, 128:256]) + along[240:480, 0:128]
    which = lax.div(lax.broadcasted_iota(jnp.int32, (40, 128), 1), 20)
    total = jnp.zeros((40, 128), f32)
    for c in range(6):
        total = total + jnp.where(which == c, along[40 * c : 40 * c + 40], 0.0)
    total = step_size * total
    if upper:
        out_ref[0:16] = total[0:16]
        out_ref[16:32] = total[16:32] + base_ref[...]
        out_ref[32:40] = total[32:40]
    else:
        out_ref[...] = total + base_ref[...]


def fold_kernel(mine_ref, core_ref, chip_ref, out_ref):
    lane = lax.broadcasted_iota(jnp.int32, (40, 128), 1)
    spot = lax.rem(lane, 20)
    live = lane < 120
    odd = (lax.axis_index("gz") & 1) == 1
    chip, core = chip_ref[...], core_ref[...]
    low = pltpu.roll(jnp.where(odd, core, chip), 112, 1)
    high = pltpu.roll(jnp.where(odd, chip, core), 16, 1)
    total = mine_ref[...]
    total = total + jnp.where(live & (spot < 3), low, 0.0)
    out_ref[...] = total + jnp.where(live & (spot >= 16), high, 0.0)


def across_kernel(own_ref, one_ref, two_ref, far_ref, out_ref, mine_ref):
    odd = (lax.axis_index("gx") & 1) == 1
    tiles = lambda ref: [ref[8 * p : 8 * p + 8] for p in range(5)]
    own, one, two, far = tiles(own_ref), tiles(one_ref), tiles(two_ref), tiles(far_ref)
    below = [jnp.where(odd, a, b) for a, b in zip(one, two)]
    above = [jnp.where(odd, b, a) for a, b in zip(one, two)]
    window = [
        own[0] + below[2] + far[4],
        own[1] + below[3],
        own[2] + below[4] + above[0],
        own[3] + above[1],
        own[4] + above[2] + far[0],
        above[3] + far[1],
    ]
    for w in range(6):
        mine_ref[8 * w : 8 * w + 8] = window[w]
    low_half = lax.broadcasted_iota(jnp.int32, (8, 128), 0) < 4
    upper, lower = [], []
    for w in (0, 4):
        upper.append(jnp.where(low_half, pltpu.roll(window[w], 4, 0), window[w + 1]))
        lower.append(jnp.where(low_half, window[w], pltpu.roll(window[w + 1], 4, 0)))
    following = lax.rem(lax.axis_index("gy") + 1, 8)
    for n in range(8):
        out_ref[n, 0:8] = window[2]
        out_ref[n, 8:16] = window[3]
        for m in range(2):
            out_ref[n, 16 + 8 * m : 24 + 8 * m] = jnp.where(following == n, upper[m], lower[m])


def field_kernel(g_ref, mine_ref, wxy_ref, wz_ref, nv_ref, field_ref, rows_ref, buf_ref, own_ref, sems):
    me_i, me_j, me_k = coords()
    ni, nj, nk = (lax.axis_size(a) for a in AXES)
    row8 = lax.broadcasted_iota(jnp.int32, (8, 128), 0)

    window = []
    before, after = lax.rem(me_j + 7, 8), lax.rem(me_j + 1, 8)
    for w in range(6):
        at = 8 * (w - 2) if 2 <= w <= 3 else 16 + 8 * (w // 4)
        lows, highs = g_ref[before, at : at + 8], g_ref[after, at : at + 8]
        if w not in (0, 4):
            lows = pltpu.roll(lows, 4, 0)
        if w not in (1, 5):
            highs = pltpu.roll(highs, 4, 0)
        window.append(mine_ref[8 * w : 8 * w + 8] + jnp.where(row8 < 4, lows, highs))
    coefs = jnp.concatenate(window, axis=0)
    row = lax.broadcasted_iota(jnp.int32, (48, 128), 0)
    lane = lax.broadcasted_iota(jnp.int32, (48, 128), 1)
    at_x = 2 * me_i - 2 + lax.shift_right_logical(row, 3)
    at_y = 4 * me_j - 2 + (row & 7)
    at_z = 16 * me_k - 2 + lax.rem(lane, 20)
    real = (at_x >= 0) & (at_x < 2 * ni) & (at_y >= 0) & (at_y < 4 * nj)
    real = real & (at_z >= 0) & (at_z < 16 * nk) & (lane < 120)
    part = lax.div(lane, 20)
    coefs = jnp.where(real, coefs, 0.0)
    hi, lo = split2(jnp.concatenate([jnp.where(part == c, coefs, 0.0) for c in range(6)], axis=0))
    along = dot(jnp.concatenate([hi, lo], axis=0), wz_ref[...])
    along = (along[0:288, 0:128] + along[0:288, 128:256]) + along[288:576, 0:128]
    ch, cl = split2(along)
    copies = []
    for pair in range(3):
        rhs = []
        for c in (2 * pair, 2 * pair + 1):
            rows = slice(48 * c, 48 * c + 48)
            rhs.append(jnp.concatenate([ch[rows], cl[rows], ch[rows]], axis=0))
        both = dot(wxy_ref[...], jnp.concatenate(rhs, axis=1)).astype(bf16)
        for n in range(2):
            buf_ref[2 * pair + n] = both[:, 128 * n : 128 * n + 128]
        there = pl.ds(2 * pair, 2)
        copy = pltpu.make_async_copy(buf_ref.at[there], field_ref.at[there], sems.at[pair])
        copy.start()
        copies.append(copy)

    for side in range(2):
        cols = [g_ref[j, 8 * side : 8 * side + 8] for j in range(8)]
        turned = [pltpu.roll(c, 4, 0) for c in cols]
        tiles = []
        zero = jnp.zeros((8, 128), f32)
        for n in range(5):
            even = cols[2 * n] if n < 4 else zero
            high = turned[2 * n + 1] if n < 4 else zero
            low = turned[2 * n - 1] if n > 0 else zero
            tiles.append(even + jnp.where(row8 < 4, low, high))
        tiles[4] = tiles[4] + tiles[0]
        for n in range(5):
            rows_ref[side, 8 * n : 8 * n + 8] = tiles[n]
        block = jnp.transpose(rows_ref[side, 2:34])
        for c in range(6):
            own_ref[c, side] = block[20 * c + 2 : 20 * c + 18]
    copy = pltpu.make_async_copy(own_ref, nv_ref, sems.at[3])
    copy.start()
    copies.append(copy)
    for copy in copies:
        copy.wait()


VMEM = pl.BlockSpec(memory_space=pltpu.VMEM)


HBM = pl.BlockSpec(memory_space=pltpu.HBM)


def call(body, out_shape, in_specs, scratch=(), out_specs=None, flops=0, bytes_accessed=0):
    return pl.pallas_call(
        body,
        out_shape=[jax.ShapeDtypeStruct(shape, dtype) for shape, dtype in out_shape],
        in_specs=in_specs,
        out_specs=out_specs or [VMEM] * len(out_shape),
        scratch_shapes=list(scratch),
        compiler_params=pltpu.CompilerParams(vmem_limit_bytes=48 << 20),
        cost_estimate=pl.CostEstimate(flops=flops, bytes_accessed=bytes_accessed, transcendentals=0),
    )


def pairs(mesh_sizes, di, dj, dk):
    ni, nj, nk = mesh_sizes
    out = []
    for i in range(ni):
        for j in range(nj):
            for k in range(nk):
                to = (((i + di) % ni) * nj + (j + dj) % nj) * nk + (k + dk) % nk
                out.append(((i * nj + j) * nk + k, to))
    return out


def fixed_tables():
    weight = lambda n, points: spline((np.arange(n)[None, :] - 8.0 * (np.arange(points) - 2)[:, None] - 3.5) / 8.0)
    ex, ey, ez = (weight(n, points) for n, points in ((16, 6), (32, 8), (128, 20)))
    hi, lo = split_two(np.einsum("px,qy->xypq", ex, ey).reshape(512, 48))
    exy = np.concatenate([hi, hi, lo], axis=1)
    padded = lambda part: np.concatenate([np.tile(part, (6, 1)), np.zeros((8, 128), part.dtype)])
    return exy, np.concatenate([padded(part) for part in split_two(ez)], axis=1)


def shards(images, velocity):
    sizes = tuple(lax.axis_size(a) for a in AXES)
    nk = sizes[2]
    exy, ezs = fixed_tables()

    def send(v, di, dj, dk):
        return lax.ppermute(v, AXES, pairs(sizes, di, dj, dk))

    (pack,) = call(pack_kernel, [((2, 32, 128), f32)], [VMEM], bytes_accessed=6 * 10**5)(images)
    to_x, to_y, to_xy = call(
        slab_kernel,
        [((2, 8, 32, 128), f32), ((2, 16, 8, 128), f32), ((2, 9, 8, 128), f32)],
        [pl.BlockSpec(memory_space=pl.ANY), VMEM],
        bytes_accessed=10**6,
    )(pack, images)
    zr = lax.ppermute(pack, "gz", [(n, (n + 1) % nk) for n in range(nk)])
    yr = send(to_y, 0, 1, 0)
    xr = send(to_x, 1, 0, 0)

    velocity = jnp.swapaxes(velocity, 3, 4).reshape(6, 2, 16, 32)
    vel, wxy, wzs, xsum, zsum = call(
        prep_kernel,
        [((16, 128), f32), ((80, 512), bf16), ((128, 256), bf16), ((256, 128), bf16), ((256, 128), f32)],
        [VMEM],
        [pltpu.VMEM((128, 32), f32)],
        bytes_accessed=10**6,
    )(velocity)
    zr, vel = lax.optimization_barrier((zr, vel))
    top = zr[:, 24:]
    yzr = send(zr, 0, 1, 0)
    xyr = send(to_xy.at[:, 8].set(top), 1, 1, 0)
    xzr = send(zr, 1, 0, 0)

    def forces(upper, more, *arrays):
        return call(
            functools.partial(force_kernel, upper),
            [((40, 128), f32)] + [(shape, f32) for shape in more],
            [VMEM] * (len(arrays) + 4),
            [
                pltpu.VMEM((2, 16, 40, 128), f32),
                pltpu.VMEM((2, 2, 40, 128), f32),
                pltpu.VMEM((2, 10, 40, 128), f32),
                pltpu.VMEM((2, 8, 40, 128), f32),
                pltpu.VMEM((5, 8, 40, 128), f32),
                pltpu.VMEM((5, 3, 32, 128), bf16),
                pltpu.VMEM((6, 256, 128), bf16),
                pltpu.VMEM((6, 256, 128), bf16),
            ],
            flops=5 * 10**8,
            bytes_accessed=10**6,
        )(*arrays, wxy, wzs, xsum, zsum)

    shared = [(2, 5, 40, 128), (2, 4, 40, 128), (5, 8, 40, 128), (5, 32, 128)]
    part, *own_parts = forces(True, shared, images, zr, yr, yzr, vel)
    (part,) = forces(False, (), images, zr, yr, yzr, xr, xyr, xzr, part, *own_parts)

    swap = lambda v, axis, couples: lax.ppermute(v, axis, couples + [(b, a) for a, b in couples])
    chip = swap(part, "gz", [(1, 2), (3, 0)])
    core = swap(part, "gz", [(0, 1), (2, 3)])
    (own,) = call(fold_kernel, [((40, 128), f32)], [VMEM] * 3)(part, core, chip)
    far = swap(own, "gx", [(0, 2), (1, 3)])
    one = swap(own, "gx", [(0, 1), (2, 3)])
    two = swap(own, "gx", [(1, 2), (3, 0)])
    copies, mine = call(across_kernel, [((8, 32, 128), f32), ((48, 128), f32)], [VMEM] * 4)(own, one, two, far)
    everything = lax.all_to_all(copies, "gy", 0, 0, tiled=True)

    nv, field = call(
        field_kernel,
        [((6, 2, 16, 32), f32), ((6, 512, 128), bf16)],
        [VMEM] * 4,
        [pltpu.VMEM((2, 40, 128), f32), pltpu.VMEM((6, 512, 128), bf16), pltpu.VMEM((6, 2, 16, 32), f32), pltpu.SemaphoreType.DMA((4,))],
        out_specs=[HBM, HBM],
        flops=10**8,
        bytes_accessed=10**6,
    )(everything, mine, exy, ezs)
    nv = jnp.swapaxes(nv.reshape(2, 3, 2, 16, 32), 3, 4)
    return nv, field.reshape(2, 3, 16, 32, 128)


def solution(mesh):
    placed = (P(None, "gx", "gy", "gz"), P(None, None, "gx", None, "gz"))
    return jax.shard_map(
        shards,
        mesh=mesh,
        in_specs=placed,
        out_specs=(P(None, None, "gx", None, "gz"), P(None, None, "gx", "gy", "gz")),
        check_vma=False,
    )
```

```python
import functools

import jax
import jax.numpy as jnp
import numpy as np
from jax import lax
from jax.experimental import pallas as pl
from jax.experimental.pallas import tpu as pltpu
from jax.sharding import PartitionSpec as P

epsilon_value = 1e-05
step_size = 0.5
AXES = ("gx", "gy", "gz")
f32 = jnp.float32
bf16 = jnp.bfloat16


def spline(t):
    m = np.abs(t)
    inside = 2.0 / 3.0 - m * m + 0.5 * m * m * m
    out = np.maximum(2.0 - m, 0.0)
    return np.where(m < 1.0, inside, out * out * out / 6.0)


def split_two(w):
    hi = w.astype(np.float32).astype(jnp.bfloat16)
    lo = (w - hi.astype(np.float64)).astype(np.float32).astype(jnp.bfloat16)
    return hi, lo


def pack_kernel(img_ref, out_ref):
    lane = lax.broadcasted_iota(jnp.int32, (32, 128), 1)
    for h in range(2):
        packed = jnp.zeros((32, 128), f32)
        for t in range(16):
            moved = pltpu.roll(img_ref[h, t], (8 * t + 8) % 128, 1)
            packed = jnp.where((lane >= 8 * t) & (lane < 8 * t + 8), moved, packed)
        out_ref[h] = packed


def slab_kernel(after_ref, img_ref, x_ref, y_ref, xy_ref):
    for h in range(2):
        for t in range(16):
            y_ref[h, t] = img_ref[h, t, 24:32]
            if t >= 8:
                x_ref[h, t - 8] = img_ref[h, t]
                xy_ref[h, t - 8] = img_ref[h, t, 24:32]
        xy_ref[h, 8] = jnp.zeros((8, 128), f32)


def spline_at(t):
    m = jnp.abs(t)
    inside = 2.0 / 3.0 - m * m + 0.5 * m * m * m
    out = jnp.maximum(2.0 - m, 0.0)
    return jnp.where(m < 1.0, inside, out * out * out / 6.0)


def weights(voxel, point):
    return spline_at((voxel.astype(f32) - 8.0 * point.astype(f32) - 3.5) * 0.125)


def prep_kernel(vel_ref, vel_out, wxy_out, wz_out, xsum_out, zsum_out, rows_ref):
    i, j, k = coords()
    ni, nj, nk = (lax.axis_size(a) for a in AXES)
    ex = jnp.where(i == 0, 0.0, 1.0)
    ez = jnp.where(k == 0, 0.0, 1.0)
    row = lax.broadcasted_iota(jnp.int32, (40, 512), 0)
    col = lax.broadcasted_iota(jnp.int32, (40, 512), 1)
    p = lax.shift_right_logical(row, 3)
    q = row & 7
    o = lax.shift_right_logical(col, 5)
    r = col & 31
    ok = ((p < 2) == (o < 4)) | (i != 0)
    ok = ok & (((q < 2) == (r < 4)) | (j != 0)) & (q < 7)
    ok = ok & ((p < 4) | (i != ni - 1)) & ((q < 6) | (j != nj - 1))
    table = jnp.where(ok, weights(o - 4, p - 2) * weights(r - 4, q - 2), 0.0)
    hi, lo = split2(table)
    wxy_out[...] = jnp.concatenate([hi.astype(f32), lo.astype(f32)], axis=0).astype(bf16)
    lane = lax.broadcasted_iota(jnp.int32, (128, 128), 1)
    sub = lax.broadcasted_iota(jnp.int32, (128, 128), 0)
    spot = lax.rem(lane, 20)
    ok = ((spot < 2) == (sub >= 124)) | (k != 0)
    ok = ok & (spot < 19) & ((spot < 18) | (k != nk - 1))
    voxel = jnp.where(sub >= 124, sub - 128, sub)
    hi, lo = split2(jnp.where(ok, weights(voxel, spot - 2), 0.0))
    wz_out[...] = jnp.concatenate([hi, lo], axis=1)

    src = lax.broadcasted_iota(jnp.int32, (256, 128), 0)
    dst = lax.broadcasted_iota(jnp.int32, (256, 128), 1)
    plane = jnp.where(src < 128, lax.shift_right_logical(src, 3) + 8, lax.shift_right_logical(src - 128, 3) - 8)
    goal = lax.shift_right_logical(dst, 3)
    near = (plane >= goal) & (plane <= goal + 8) & ((src & 7) == (dst & 7)) & (plane >= 0)
    across = (plane < 8) != (goal < 4)
    xsum_out[...] = jnp.where(near, jnp.where(across, ex, 1.0), 0.0).astype(bf16)
    centre = jnp.where(dst < 124, dst, dst - 128)
    below = src >= 128
    place = jnp.where(below, (src & 7) - 8, src)
    gap = place - centre
    inside = (gap <= 4) & (gap >= -4)
    crossing = below != (dst >= 124)
    zsum_out[...] = jnp.where(inside, jnp.where(crossing, ez, 1.0), 0.0)

    pick_q = lax.broadcasted_iota(jnp.int32, (8, 32), 0)
    pick_y = lax.broadcasted_iota(jnp.int32, (8, 32), 1)
    pick = ((pick_y == 4 * j + pick_q - 2) & (pick_q >= 2) & (pick_q < 6)).astype(f32).astype(bf16)
    for side in range(2):
        rows_ref[...] = jnp.zeros((128, 32), f32)
        for c in range(6):
            rows_ref[20 * c + 2 : 20 * c + 18] = vel_ref[c, side]
        turned = jnp.transpose(rows_ref[...])
        total = jnp.zeros((8, 128), f32)
        for piece in split3(turned):
            total = total + dot(pick, piece)
        vel_out[8 * side : 8 * side + 8] = total


def coords():
    return tuple(lax.axis_index(a) for a in AXES)


def split3(v):
    hi = v.astype(bf16)
    r = v - hi.astype(f32)
    mid = r.astype(bf16)
    lo = (r - mid.astype(f32)).astype(bf16)
    return hi, mid, lo


def split2(v):
    hi = v.astype(bf16)
    return hi, (v - hi.astype(f32)).astype(bf16)


def dot(a, b):
    return jnp.dot(a, b, preferred_element_type=f32)


def up_by(v, n, row):
    size = v.shape[0]
    return jnp.where(row < size - n, pltpu.roll(v, size - n, 0), 0.0)


def rows_window(v, head, tail, row8):
    first = v[0:8]
    own = jnp.concatenate([jnp.zeros((8, 128), f32), v[8:40]], axis=0)
    s = first + up_by(first, 1, row8)
    s = s + up_by(s, 2, row8)
    s = s + up_by(s, 4, row8)
    w = own + pltpu.roll(own, 39, 0)
    w = w + pltpu.roll(w, 38, 0)
    w = w + pltpu.roll(w, 36, 0)
    w = w[0:32] + own[8:40]
    top = head * s + tail * w[0:8]
    return jnp.concatenate([top, w[8:32]], axis=0)


def force_kernel(upper, own_ref, zr_ref, yr_ref, yzr_ref, *refs):
    if upper:
        base_ref, *refs = refs
        wxy_ref, wz_ref, xsum_ref, zsum_ref, out_ref, vown_ref, dzown_ref, xown_ref, hown_ref, *refs = refs
    else:
        xr_ref, xyr_ref, xzr_ref, base_ref, vown_ref, dzown_ref, xown_ref, hown_ref, *refs = refs
        wxy_ref, wz_ref, xsum_ref, zsum_ref, out_ref, *refs = refs
    a_ref, h_ref, v_ref, dz_ref, xs_ref, hs_ref, fh_ref, fl_ref = refs
    first = 8 if upper else 0
    ex, ey, ez = (jnp.where(at == 0, 0.0, 1.0) for at in coords())
    row8 = lax.broadcasted_iota(jnp.int32, (8, 128), 0)
    row32 = lax.broadcasted_iota(jnp.int32, (32, 128), 0)
    lane40 = lax.broadcasted_iota(jnp.int32, (40, 128), 1)
    head = jnp.where(row8 < 4, 1.0, ey)
    tail = jnp.where(row8 < 4, ey, 1.0)

    for h in range(2):
        for n in range(16 if upper else 8):
            a_ref[h, n, 8:40] = own_ref[h, n] if upper else xr_ref[h, n]
            a_ref[h, n, 0:8] = yr_ref[h, n] if upper else xyr_ref[h, n]
        if upper:
            h_ref[h, 0, 8:40] = zr_ref[h]
            h_ref[h, 0, 0:8] = yzr_ref[h, 24:32]
        else:
            h_ref[h, 1, 8:40] = xzr_ref[h]
            h_ref[h, 1, 0:8] = xyr_ref[h, 8]

    plus_z = jnp.where(lane40 == 127, ez, 1.0)
    minus_z = jnp.where(lane40 == 0, ez, 1.0)
    def centre(h, n):
        if upper:
            return v_ref.at[h, n - 3]
        return v_ref.at[h, n - 3] if n < 8 else vown_ref.at[h, n - 8]

    def slope(h, n):
        if upper:
            return dz_ref.at[h, n - 4] if n >= 4 else dzown_ref.at[h, n]
        return dz_ref.at[h, n - 4] if n < 8 else dzown_ref.at[h, n - 8]

    planes = range(0, 13) if upper else range(3, 8)
    sloped = range(0, 12) if upper else range(4, 8)
    for h in range(2):
        for n in planes:
            if upper:
                halo = pltpu.roll(h_ref[h, 0], (120 - 8 * n) % 128, 1)
            else:
                halo = pltpu.roll(h_ref[h, 1], (120 - 8 * (n + 8)) % 128, 1)
            value = jnp.where(lane40 >= 124, halo, a_ref[h, n])
            if upper and n < 5:
                vown_ref[h, n] = value
            if not upper or n >= 3:
                v_ref[h, n - 3] = value
            if n in sloped:
                slope(h, n)[...] = halo
    for h in range(2):
        for n in sloped:
            a = a_ref[h, n]
            halo = slope(h, n)[...]
            up = pltpu.roll(jnp.where(lane40 >= 125, halo, a), 127, 1)
            down = pltpu.roll(jnp.where(lane40 >= 123, halo, a), 1, 1)
            slope(h, n)[...] = plus_z * up - minus_z * down

    for tile in range(5):
        rows = slice(8 * tile, 8 * tile + 8)
        for q in range(5):
            p = []
            for n in range(16 if upper else 8):
                if q == 4:
                    p.append(a_ref[0, n, rows] * a_ref[1, n, rows])
                else:
                    value = a_ref[q % 2, n, rows]
                    p.append(value if q < 2 else value * value)
            if upper:
                b = [p[n] + p[n + 1] for n in range(15)]
                b = [b[n] + b[n + 2] for n in range(13)]
                b = [b[n] + b[n + 4] for n in range(9)]
                right = p[0]
                for o in range(8):
                    xs_ref[q, o, rows] = b[o] + p[o + 8]
                    if o > 0:
                        right = right + p[o]
                    xown_ref[q, o, rows] = right
                continue
            left = [None] * 8
            left[7] = p[7]
            for o in range(6, -1, -1):
                left[o] = left[o + 1] + p[o]
            for o in range(8):
                right = xown_ref[q, o, rows]
                xs_ref[q, o, rows] = left[o] + ex * right if o < 4 else ex * left[o] + right

    side = 0 if upper else 1
    x_sum = xsum_ref[128 * side : 128 * side + 128]
    for q in range(5):
        f = h_ref[0, side]
        m = h_ref[1, side]
        value = (f, m, f * f, m * m, f * m)[q]
        total = jnp.zeros((32, 128), f32) if upper else hown_ref[q]
        for piece in split3(rows_window(value, head, tail, row8)):
            total = total + dot(piece, x_sum)
        if upper:
            hown_ref[q] = total
        for n, piece in enumerate(split3(total)):
            hs_ref[q, n] = piece

    group = lax.shift_right_logical(lax.broadcasted_iota(jnp.int32, (128, 128), 0), 3)
    z_own = zsum_ref[0:128].astype(bf16)
    z_halo = zsum_ref[128:256]
    plus_y = jnp.where(row32 == 3, ey, 1.0)
    minus_y = jnp.where(row32 == 4, ey, 1.0)

    for o in range(8):
        z_sum = jnp.concatenate([z_own, jnp.where(group == o + first, z_halo, 0.0).astype(bf16)], axis=0)
        pieces = [[], [], []]
        for q in range(5):
            y = rows_window(xs_ref[q, o], head, tail, row8)
            for n, piece in enumerate(split3(y)):
                pieces[n].append(jnp.concatenate([piece, hs_ref[q, n]], axis=1))
        big = dot(jnp.concatenate(pieces[0] + pieces[1] + pieces[2], axis=0), z_sum)
        sums = (big[0:160] + big[160:320]) + big[320:480]
        sums = sums * (1.0 / 729.0)
        mean_f = sums[0:32]
        mean_m = sums[32:64]
        var_f = sums[64:96] - mean_f * mean_f + epsilon_value
        var_m = sums[96:128] - mean_m * mean_m + epsilon_value
        cov = sums[128:160] - mean_f * mean_m
        off_f = centre(0, o + 4)[4:36] - mean_f
        off_m = centre(1, o + 4)[4:36] - mean_m
        inv = 1.0 / (var_f * var_m)
        factor = cov * inv
        pulls = (
            factor * (off_m - factor * var_m * off_f),
            factor * (off_f - factor * var_f * off_m),
        )
        plus_x = ex if o + first == 3 else 1.0
        minus_x = ex if o + first == 4 else 1.0
        where_to = slice(32 * o, 32 * o + 32)
        for h in range(2):
            dx = plus_x * centre(h, o + 5)[4:36] - minus_x * centre(h, o + 3)[4:36]
            dy = plus_y * centre(h, o + 4)[5:37] - minus_y * centre(h, o + 4)[3:35]
            dz = slope(h, o + 4)[4:36]
            for c, d in enumerate((dx, dy, dz)):
                hi, lo = split2(pulls[h] * d)
                pair, lanes = divmod(3 * h + c, 2)
                fh_ref[pair, where_to, 128 * lanes : 128 * lanes + 128] = hi
                fl_ref[pair, where_to, 128 * lanes : 128 * lanes + 128] = lo

    cols = slice(32 * first, 32 * first + 256)
    wxy = wxy_ref[:, cols]
    wxy_hi = wxy_ref[0:40, cols]
    lattice = []
    for pair in range(3):
        one = dot(wxy, fh_ref[pair])
        both = one[0:40] + one[40:80] + dot(wxy_hi, fl_ref[pair])
        lattice += [both[:, 0:128], both[:, 128:256]]
    hi, lo = split2(jnp.concatenate(lattice, axis=0))
    along = dot(jnp.concatenate([hi, lo], axis=0), wz_ref[...])
    along = (along[0:240, 0:128] + along[0:240, 128:256]) + along[240:480, 0:128]
    which = lax.div(lax.broadcasted_iota(jnp.int32, (40, 128), 1), 20)
    total = jnp.zeros((40, 128), f32)
    for c in range(6):
        total = total + jnp.where(which == c, along[40 * c : 40 * c + 40], 0.0)
    total = step_size * total
    if upper:
        out_ref[0:16] = total[0:16]
        out_ref[16:32] = total[16:32] + base_ref[...]
        out_ref[32:40] = total[32:40]
    else:
        out_ref[...] = total + base_ref[...]


def fold_kernel(mine_ref, core_ref, chip_ref, out_ref):
    lane = lax.broadcasted_iota(jnp.int32, (40, 128), 1)
    spot = lax.rem(lane, 20)
    live = lane < 120
    odd = (lax.axis_index("gz") & 1) == 1
    chip, core = chip_ref[...], core_ref[...]
    low = pltpu.roll(jnp.where(odd, core, chip), 112, 1)
    high = pltpu.roll(jnp.where(odd, chip, core), 16, 1)
    total = mine_ref[...]
    total = total + jnp.where(live & (spot < 3), low, 0.0)
    out_ref[...] = total + jnp.where(live & (spot >= 16), high, 0.0)


def across_kernel(own_ref, one_ref, two_ref, far_ref, out_ref, mine_ref):
    odd = (lax.axis_index("gx") & 1) == 1
    tiles = lambda ref: [ref[8 * p : 8 * p + 8] for p in range(5)]
    own, one, two, far = tiles(own_ref), tiles(one_ref), tiles(two_ref), tiles(far_ref)
    below = [jnp.where(odd, a, b) for a, b in zip(one, two)]
    above = [jnp.where(odd, b, a) for a, b in zip(one, two)]
    window = [
        own[0] + below[2] + far[4],
        own[1] + below[3],
        own[2] + below[4] + above[0],
        own[3] + above[1],
        own[4] + above[2] + far[0],
        above[3] + far[1],
    ]
    for w in range(6):
        mine_ref[8 * w : 8 * w + 8] = window[w]
    low_half = lax.broadcasted_iota(jnp.int32, (8, 128), 0) < 4
    upper, lower = [], []
    for w in (0, 4):
        upper.append(jnp.where(low_half, pltpu.roll(window[w], 4, 0), window[w + 1]))
        lower.append(jnp.where(low_half, window[w], pltpu.roll(window[w + 1], 4, 0)))
    following = lax.rem(lax.axis_index("gy") + 1, 8)
    for n in range(8):
        out_ref[n, 0:8] = window[2]
        out_ref[n, 8:16] = window[3]
        for m in range(2):
            out_ref[n, 16 + 8 * m : 24 + 8 * m] = jnp.where(following == n, upper[m], lower[m])


def field_kernel(g_ref, mine_ref, wxy_ref, wz_ref, nv_ref, field_ref, rows_ref, buf_ref, own_ref, sems):
    me_i, me_j, me_k = coords()
    ni, nj, nk = (lax.axis_size(a) for a in AXES)
    row8 = lax.broadcasted_iota(jnp.int32, (8, 128), 0)

    window = []
    before, after = lax.rem(me_j + 7, 8), lax.rem(me_j + 1, 8)
    for w in range(6):
        at = 8 * (w - 2) if 2 <= w <= 3 else 16 + 8 * (w // 4)
        lows, highs = g_ref[before, at : at + 8], g_ref[after, at : at + 8]
        if w not in (0, 4):
            lows = pltpu.roll(lows, 4, 0)
        if w not in (1, 5):
            highs = pltpu.roll(highs, 4, 0)
        window.append(mine_ref[8 * w : 8 * w + 8] + jnp.where(row8 < 4, lows, highs))
    coefs = jnp.concatenate(window, axis=0)
    row = lax.broadcasted_iota(jnp.int32, (48, 128), 0)
    lane = lax.broadcasted_iota(jnp.int32, (48, 128), 1)
    at_x = 2 * me_i - 2 + lax.shift_right_logical(row, 3)
    at_y = 4 * me_j - 2 + (row & 7)
    at_z = 16 * me_k - 2 + lax.rem(lane, 20)
    real = (at_x >= 0) & (at_x < 2 * ni) & (at_y >= 0) & (at_y < 4 * nj)
    real = real & (at_z >= 0) & (at_z < 16 * nk) & (lane < 120)
    part = lax.div(lane, 20)
    coefs = jnp.where(real, coefs, 0.0)
    hi, lo = split2(jnp.concatenate([jnp.where(part == c, coefs, 0.0) for c in range(6)], axis=0))
    along = dot(jnp.concatenate([hi, lo], axis=0), wz_ref[...])
    along = (along[0:288, 0:128] + along[0:288, 128:256]) + along[288:576, 0:128]
    ch, cl = split2(along)
    copies = []
    for pair in range(3):
        rhs = []
        for c in (2 * pair, 2 * pair + 1):
            rows = slice(48 * c, 48 * c + 48)
            rhs.append(jnp.concatenate([ch[rows], cl[rows], ch[rows]], axis=0))
        rhs = jnp.concatenate(rhs, axis=1)
        for half in range(2):
            rows = pl.ds(256 * half, 256)
            both = dot(wxy_ref[rows], rhs).astype(bf16)
            for n in range(2):
                buf_ref[2 * pair + n, rows] = both[:, 128 * n : 128 * n + 128]
            there = pl.ds(2 * pair, 2)
            copy = pltpu.make_async_copy(buf_ref.at[there, rows], field_ref.at[there, rows], sems.at[2 * pair + half])
            copy.start()
            copies.append(copy)

    for side in range(2):
        cols = [g_ref[j, 8 * side : 8 * side + 8] for j in range(8)]
        turned = [pltpu.roll(c, 4, 0) for c in cols]
        tiles = []
        zero = jnp.zeros((8, 128), f32)
        for n in range(5):
            even = cols[2 * n] if n < 4 else zero
            high = turned[2 * n + 1] if n < 4 else zero
            low = turned[2 * n - 1] if n > 0 else zero
            tiles.append(even + jnp.where(row8 < 4, low, high))
        tiles[4] = tiles[4] + tiles[0]
        for n in range(5):
            rows_ref[side, 8 * n : 8 * n + 8] = tiles[n]
        block = jnp.transpose(rows_ref[side, 2:34])
        for c in range(6):
            own_ref[c, side] = block[20 * c + 2 : 20 * c + 18]
    copy = pltpu.make_async_copy(own_ref, nv_ref, sems.at[6])
    copy.start()
    copies.append(copy)
    for copy in copies:
        copy.wait()


VMEM = pl.BlockSpec(memory_space=pltpu.VMEM)


HBM = pl.BlockSpec(memory_space=pltpu.HBM)


def call(body, out_shape, in_specs, scratch=(), out_specs=None, flops=0, bytes_accessed=0):
    return pl.pallas_call(
        body,
        out_shape=[jax.ShapeDtypeStruct(shape, dtype) for shape, dtype in out_shape],
        in_specs=in_specs,
        out_specs=out_specs or [VMEM] * len(out_shape),
        scratch_shapes=list(scratch),
        compiler_params=pltpu.CompilerParams(vmem_limit_bytes=48 << 20),
        cost_estimate=pl.CostEstimate(flops=flops, bytes_accessed=bytes_accessed, transcendentals=0),
    )


def pairs(mesh_sizes, di, dj, dk):
    ni, nj, nk = mesh_sizes
    out = []
    for i in range(ni):
        for j in range(nj):
            for k in range(nk):
                to = (((i + di) % ni) * nj + (j + dj) % nj) * nk + (k + dk) % nk
                out.append(((i * nj + j) * nk + k, to))
    return out


def fixed_tables():
    weight = lambda n, points: spline((np.arange(n)[None, :] - 8.0 * (np.arange(points) - 2)[:, None] - 3.5) / 8.0)
    ex, ey, ez = (weight(n, points) for n, points in ((16, 6), (32, 8), (128, 20)))
    hi, lo = split_two(np.einsum("px,qy->xypq", ex, ey).reshape(512, 48))
    exy = np.concatenate([hi, hi, lo], axis=1)
    padded = lambda part: np.concatenate([np.tile(part, (6, 1)), np.zeros((8, 128), part.dtype)])
    return exy, np.concatenate([padded(part) for part in split_two(ez)], axis=1)


def shards(images, velocity):
    sizes = tuple(lax.axis_size(a) for a in AXES)
    nk = sizes[2]
    exy, ezs = fixed_tables()

    def send(v, di, dj, dk):
        return lax.ppermute(v, AXES, pairs(sizes, di, dj, dk))

    (pack,) = call(pack_kernel, [((2, 32, 128), f32)], [VMEM], bytes_accessed=6 * 10**5)(images)
    to_x, to_y, to_xy = call(
        slab_kernel,
        [((2, 8, 32, 128), f32), ((2, 16, 8, 128), f32), ((2, 9, 8, 128), f32)],
        [pl.BlockSpec(memory_space=pl.ANY), VMEM],
        bytes_accessed=10**6,
    )(pack, images)
    zr = lax.ppermute(pack, "gz", [(n, (n + 1) % nk) for n in range(nk)])
    yr = send(to_y, 0, 1, 0)
    xr = send(to_x, 1, 0, 0)

    velocity = jnp.swapaxes(velocity, 3, 4).reshape(6, 2, 16, 32)
    vel, wxy, wzs, xsum, zsum = call(
        prep_kernel,
        [((16, 128), f32), ((80, 512), bf16), ((128, 256), bf16), ((256, 128), bf16), ((256, 128), f32)],
        [VMEM],
        [pltpu.VMEM((128, 32), f32)],
        bytes_accessed=10**6,
    )(velocity)
    zr, vel = lax.optimization_barrier((zr, vel))
    top = zr[:, 24:]
    yzr = send(zr, 0, 1, 0)
    xyr = send(to_xy.at[:, 8].set(top), 1, 1, 0)
    xzr = send(zr, 1, 0, 0)

    def forces(upper, more, *arrays):
        return call(
            functools.partial(force_kernel, upper),
            [((40, 128), f32)] + [(shape, f32) for shape in more],
            [VMEM] * (len(arrays) + 4),
            [
                pltpu.VMEM((2, 16, 40, 128), f32),
                pltpu.VMEM((2, 2, 40, 128), f32),
                pltpu.VMEM((2, 10, 40, 128), f32),
                pltpu.VMEM((2, 8, 40, 128), f32),
                pltpu.VMEM((5, 8, 40, 128), f32),
                pltpu.VMEM((5, 3, 32, 128), bf16),
                pltpu.VMEM((3, 256, 256), bf16),
                pltpu.VMEM((3, 256, 256), bf16),
            ],
            flops=5 * 10**8,
            bytes_accessed=10**6,
        )(*arrays, wxy, wzs, xsum, zsum)

    shared = [(2, 5, 40, 128), (2, 4, 40, 128), (5, 8, 40, 128), (5, 32, 128)]
    part, *own_parts = forces(True, shared, images, zr, yr, yzr, vel)
    (part,) = forces(False, (), images, zr, yr, yzr, xr, xyr, xzr, part, *own_parts)

    swap = lambda v, axis, couples: lax.ppermute(v, axis, couples + [(b, a) for a, b in couples])
    chip = swap(part, "gz", [(1, 2), (3, 0)])
    core = swap(part, "gz", [(0, 1), (2, 3)])
    (own,) = call(fold_kernel, [((40, 128), f32)], [VMEM] * 3)(part, core, chip)
    far = swap(own, "gx", [(0, 2), (1, 3)])
    one = swap(own, "gx", [(0, 1), (2, 3)])
    two = swap(own, "gx", [(1, 2), (3, 0)])
    copies, mine = call(across_kernel, [((8, 32, 128), f32), ((48, 128), f32)], [VMEM] * 4)(own, one, two, far)
    everything = lax.all_to_all(copies, "gy", 0, 0, tiled=True)

    nv, field = call(
        field_kernel,
        [((6, 2, 16, 32), f32), ((6, 512, 128), bf16)],
        [VMEM] * 4,
        [pltpu.VMEM((2, 40, 128), f32), pltpu.VMEM((6, 512, 128), bf16), pltpu.VMEM((6, 2, 16, 32), f32), pltpu.SemaphoreType.DMA((7,))],
        out_specs=[HBM, HBM],
        flops=10**8,
        bytes_accessed=10**6,
    )(everything, mine, exy, ezs)
    nv = jnp.swapaxes(nv.reshape(2, 3, 2, 16, 32), 3, 4)
    return nv, field.reshape(2, 3, 16, 32, 128)


def solution(mesh):
    placed = (P(None, "gx", "gy", "gz"), P(None, None, "gx", None, "gz"))
    return jax.shard_map(
        shards,
        mesh=mesh,
        in_specs=placed,
        out_specs=(P(None, None, "gx", None, "gz"), P(None, None, "gx", "gy", "gz")),
        check_vma=False,
    )
```

```python
import functools

import jax
import jax.numpy as jnp
import numpy as np
from jax import lax
from jax.experimental import pallas as pl
from jax.experimental.pallas import tpu as pltpu
from jax.sharding import PartitionSpec as P

epsilon_value = 1e-05
step_size = 0.5
AXES = ("gx", "gy", "gz")
f32 = jnp.float32
bf16 = jnp.bfloat16


def spline(t):
    m = np.abs(t)
    inside = 2.0 / 3.0 - m * m + 0.5 * m * m * m
    out = np.maximum(2.0 - m, 0.0)
    return np.where(m < 1.0, inside, out * out * out / 6.0)


def split_two(w):
    hi = w.astype(np.float32).astype(jnp.bfloat16)
    lo = (w - hi.astype(np.float64)).astype(np.float32).astype(jnp.bfloat16)
    return hi, lo


def pack_kernel(img_ref, out_ref):
    lane = lax.broadcasted_iota(jnp.int32, (32, 128), 1)
    for h in range(2):
        packed = jnp.zeros((32, 128), f32)
        for t in range(16):
            moved = pltpu.roll(img_ref[h, t], (8 * t + 8) % 128, 1)
            packed = jnp.where((lane >= 8 * t) & (lane < 8 * t + 8), moved, packed)
        out_ref[h] = packed


def slab_kernel(after_ref, img_ref, x_ref, y_ref, xy_ref):
    for h in range(2):
        for t in range(16):
            y_ref[h, t] = img_ref[h, t, 24:32]
            if t >= 8:
                x_ref[h, t - 8] = img_ref[h, t]
                xy_ref[h, t - 8] = img_ref[h, t, 24:32]
        xy_ref[h, 8] = jnp.zeros((8, 128), f32)


def spline_at(t):
    m = jnp.abs(t)
    inside = 2.0 / 3.0 - m * m + 0.5 * m * m * m
    out = jnp.maximum(2.0 - m, 0.0)
    return jnp.where(m < 1.0, inside, out * out * out / 6.0)


def weights(voxel, point):
    return spline_at((voxel.astype(f32) - 8.0 * point.astype(f32) - 3.5) * 0.125)


def prep_kernel(vel_ref, vel_out, wxy_out, wz_out, xsum_out, zsum_out, rows_ref):
    i, j, k = coords()
    ni, nj, nk = (lax.axis_size(a) for a in AXES)
    ex = jnp.where(i == 0, 0.0, 1.0)
    ez = jnp.where(k == 0, 0.0, 1.0)
    row = lax.broadcasted_iota(jnp.int32, (40, 512), 0)
    col = lax.broadcasted_iota(jnp.int32, (40, 512), 1)
    p = lax.shift_right_logical(row, 3)
    q = row & 7
    o = lax.shift_right_logical(col, 5)
    r = col & 31
    ok = ((p < 2) == (o < 4)) | (i != 0)
    ok = ok & (((q < 2) == (r < 4)) | (j != 0)) & (q < 7)
    ok = ok & ((p < 4) | (i != ni - 1)) & ((q < 6) | (j != nj - 1))
    table = jnp.where(ok, weights(o - 4, p - 2) * weights(r - 4, q - 2), 0.0)
    hi, lo = split2(table)
    wxy_out[...] = jnp.concatenate([hi.astype(f32), lo.astype(f32)], axis=0).astype(bf16)
    lane = lax.broadcasted_iota(jnp.int32, (128, 128), 1)
    sub = lax.broadcasted_iota(jnp.int32, (128, 128), 0)
    spot = lax.rem(lane, 20)
    ok = ((spot < 2) == (sub >= 124)) | (k != 0)
    ok = ok & (spot < 19) & ((spot < 18) | (k != nk - 1))
    voxel = jnp.where(sub >= 124, sub - 128, sub)
    hi, lo = split2(jnp.where(ok, weights(voxel, spot - 2), 0.0))
    wz_out[...] = jnp.concatenate([hi, lo], axis=1)

    src = lax.broadcasted_iota(jnp.int32, (256, 128), 0)
    dst = lax.broadcasted_iota(jnp.int32, (256, 128), 1)
    plane = jnp.where(src < 128, lax.shift_right_logical(src, 3) + 8, lax.shift_right_logical(src - 128, 3) - 8)
    goal = lax.shift_right_logical(dst, 3)
    near = (plane >= goal) & (plane <= goal + 8) & ((src & 7) == (dst & 7)) & (plane >= 0)
    across = (plane < 8) != (goal < 4)
    xsum_out[...] = jnp.where(near, jnp.where(across, ex, 1.0), 0.0).astype(bf16)
    centre = jnp.where(dst < 124, dst, dst - 128)
    below = src >= 128
    place = jnp.where(below, (src & 7) - 8, src)
    gap = place - centre
    inside = (gap <= 4) & (gap >= -4)
    crossing = below != (dst >= 124)
    zsum_out[...] = jnp.where(inside, jnp.where(crossing, ez, 1.0), 0.0)

    pick_q = lax.broadcasted_iota(jnp.int32, (8, 32), 0)
    pick_y = lax.broadcasted_iota(jnp.int32, (8, 32), 1)
    pick = ((pick_y == 4 * j + pick_q - 2) & (pick_q >= 2) & (pick_q < 6)).astype(f32).astype(bf16)
    for side in range(2):
        rows_ref[...] = jnp.zeros((128, 32), f32)
        for c in range(6):
            rows_ref[20 * c + 2 : 20 * c + 18] = vel_ref[c, side]
        turned = jnp.transpose(rows_ref[...])
        total = jnp.zeros((8, 128), f32)
        for piece in split3(turned):
            total = total + dot(pick, piece)
        vel_out[8 * side : 8 * side + 8] = total


def coords():
    return tuple(lax.axis_index(a) for a in AXES)


def split3(v):
    hi = v.astype(bf16)
    r = v - hi.astype(f32)
    mid = r.astype(bf16)
    lo = (r - mid.astype(f32)).astype(bf16)
    return hi, mid, lo


def split2(v):
    hi = v.astype(bf16)
    return hi, (v - hi.astype(f32)).astype(bf16)


def dot(a, b):
    return jnp.dot(a, b, preferred_element_type=f32)


def up_by(v, n, row):
    size = v.shape[0]
    return jnp.where(row < size - n, pltpu.roll(v, size - n, 0), 0.0)


def rows_window(v, head, tail, row8):
    first = v[0:8]
    own = jnp.concatenate([jnp.zeros((8, 128), f32), v[8:40]], axis=0)
    s = first + up_by(first, 1, row8)
    s = s + up_by(s, 2, row8)
    s = s + up_by(s, 4, row8)
    w = own + pltpu.roll(own, 39, 0)
    w = w + pltpu.roll(w, 38, 0)
    w = w + pltpu.roll(w, 36, 0)
    w = w[0:32] + own[8:40]
    top = head * s + tail * w[0:8]
    return jnp.concatenate([top, w[8:32]], axis=0)


def force_kernel(upper, own_ref, zr_ref, yr_ref, yzr_ref, *refs):
    if upper:
        base_ref, *refs = refs
        wxy_ref, wz_ref, xsum_ref, zsum_ref, out_ref, vown_ref, dzown_ref, xown_ref, hown_ref, *refs = refs
    else:
        xr_ref, xyr_ref, xzr_ref, base_ref, vown_ref, dzown_ref, xown_ref, hown_ref, *refs = refs
        wxy_ref, wz_ref, xsum_ref, zsum_ref, out_ref, *refs = refs
    a_ref, h_ref, v_ref, dz_ref, xs_ref, hs_ref, fh_ref, fl_ref = refs
    first = 8 if upper else 0
    ex, ey, ez = (jnp.where(at == 0, 0.0, 1.0) for at in coords())
    row8 = lax.broadcasted_iota(jnp.int32, (8, 128), 0)
    row32 = lax.broadcasted_iota(jnp.int32, (32, 128), 0)
    lane40 = lax.broadcasted_iota(jnp.int32, (40, 128), 1)
    head = jnp.where(row8 < 4, 1.0, ey)
    tail = jnp.where(row8 < 4, ey, 1.0)

    for h in range(2):
        for n in range(16 if upper else 8):
            a_ref[h, n, 8:40] = own_ref[h, n] if upper else xr_ref[h, n]
            a_ref[h, n, 0:8] = yr_ref[h, n] if upper else xyr_ref[h, n]
        if upper:
            h_ref[h, 0, 8:40] = zr_ref[h]
            h_ref[h, 0, 0:8] = yzr_ref[h, 24:32]
        else:
            h_ref[h, 1, 8:40] = xzr_ref[h]
            h_ref[h, 1, 0:8] = xyr_ref[h, 8]

    plus_z = jnp.where(lane40 == 127, ez, 1.0)
    minus_z = jnp.where(lane40 == 0, ez, 1.0)
    def centre(h, n):
        if upper:
            return v_ref.at[h, n - 3]
        return v_ref.at[h, n - 3] if n < 8 else vown_ref.at[h, n - 8]

    def slope(h, n):
        if upper:
            return dz_ref.at[h, n - 4] if n >= 4 else dzown_ref.at[h, n]
        return dz_ref.at[h, n - 4] if n < 8 else dzown_ref.at[h, n - 8]

    planes = range(0, 13) if upper else range(3, 8)
    sloped = range(0, 12) if upper else range(4, 8)
    for h in range(2):
        for n in planes:
            if upper:
                halo = pltpu.roll(h_ref[h, 0], (120 - 8 * n) % 128, 1)
            else:
                halo = pltpu.roll(h_ref[h, 1], (120 - 8 * (n + 8)) % 128, 1)
            value = jnp.where(lane40 >= 124, halo, a_ref[h, n])
            if upper and n < 5:
                vown_ref[h, n] = value
            if not upper or n >= 3:
                v_ref[h, n - 3] = value
            if n in sloped:
                slope(h, n)[...] = halo
    for h in range(2):
        for n in sloped:
            a = a_ref[h, n]
            halo = slope(h, n)[...]
            up = pltpu.roll(jnp.where(lane40 >= 125, halo, a), 127, 1)
            down = pltpu.roll(jnp.where(lane40 >= 123, halo, a), 1, 1)
            slope(h, n)[...] = plus_z * up - minus_z * down

    for tile in range(5):
        rows = slice(8 * tile, 8 * tile + 8)
        for q in range(5):
            p = []
            for n in range(16 if upper else 8):
                if q == 4:
                    p.append(a_ref[0, n, rows] * a_ref[1, n, rows])
                else:
                    value = a_ref[q % 2, n, rows]
                    p.append(value if q < 2 else value * value)
            if upper:
                b = [p[n] + p[n + 1] for n in range(15)]
                b = [b[n] + b[n + 2] for n in range(13)]
                b = [b[n] + b[n + 4] for n in range(9)]
                right = p[0]
                for o in range(8):
                    xs_ref[q, o, rows] = b[o] + p[o + 8]
                    if o > 0:
                        right = right + p[o]
                    xown_ref[q, o, rows] = right
                continue
            left = [None] * 8
            left[7] = p[7]
            for o in range(6, -1, -1):
                left[o] = left[o + 1] + p[o]
            for o in range(8):
                right = xown_ref[q, o, rows]
                xs_ref[q, o, rows] = left[o] + ex * right if o < 4 else ex * left[o] + right

    side = 0 if upper else 1
    x_sum = xsum_ref[128 * side : 128 * side + 128]
    for q in range(5):
        f = h_ref[0, side]
        m = h_ref[1, side]
        value = (f, m, f * f, m * m, f * m)[q]
        total = jnp.zeros((32, 128), f32) if upper else hown_ref[q]
        for piece in split3(rows_window(value, head, tail, row8)):
            total = total + dot(piece, x_sum)
        if upper:
            hown_ref[q] = total
        for n, piece in enumerate(split3(total)):
            hs_ref[q, n] = piece

    group = lax.shift_right_logical(lax.broadcasted_iota(jnp.int32, (128, 128), 0), 3)
    z_own = zsum_ref[0:128].astype(bf16)
    z_halo = zsum_ref[128:256]
    plus_y = jnp.where(row32 == 3, ey, 1.0)
    minus_y = jnp.where(row32 == 4, ey, 1.0)

    for o in range(8):
        z_sum = jnp.concatenate([z_own, jnp.where(group == o + first, z_halo, 0.0).astype(bf16)], axis=0)
        pieces = [[], [], []]
        for q in range(5):
            y = rows_window(xs_ref[q, o], head, tail, row8)
            for n, piece in enumerate(split3(y)):
                pieces[n].append(jnp.concatenate([piece, hs_ref[q, n]], axis=1))
        big = dot(jnp.concatenate(pieces[0] + pieces[1] + pieces[2], axis=0), z_sum)
        sums = (big[0:160] + big[160:320]) + big[320:480]
        sums = sums * (1.0 / 729.0)
        mean_f = sums[0:32]
        mean_m = sums[32:64]
        var_f = sums[64:96] - mean_f * mean_f + epsilon_value
        var_m = sums[96:128] - mean_m * mean_m + epsilon_value
        cov = sums[128:160] - mean_f * mean_m
        off_f = centre(0, o + 4)[4:36] - mean_f
        off_m = centre(1, o + 4)[4:36] - mean_m
        inv = 1.0 / (var_f * var_m)
        factor = cov * inv
        pulls = (
            factor * (off_m - factor * var_m * off_f),
            factor * (off_f - factor * var_f * off_m),
        )
        plus_x = ex if o + first == 3 else 1.0
        minus_x = ex if o + first == 4 else 1.0
        where_to = slice(32 * o, 32 * o + 32)
        for h in range(2):
            dx = plus_x * centre(h, o + 5)[4:36] - minus_x * centre(h, o + 3)[4:36]
            dy = plus_y * centre(h, o + 4)[5:37] - minus_y * centre(h, o + 4)[3:35]
            dz = slope(h, o + 4)[4:36]
            for c, d in enumerate((dx, dy, dz)):
                hi, lo = split2(pulls[h] * d)
                fh_ref[3 * h + c, where_to] = hi
                fl_ref[3 * h + c, where_to] = lo

    cols = slice(32 * first, 32 * first + 256)
    wxy = wxy_ref[:, cols]
    wxy_hi = wxy_ref[0:40, cols]
    lattice = []
    for c in range(6):
        one = dot(wxy, fh_ref[c])
        lattice.append(one[0:40] + one[40:80] + dot(wxy_hi, fl_ref[c]))
    hi, lo = split2(jnp.concatenate(lattice, axis=0))
    along = dot(jnp.concatenate([hi, lo], axis=0), wz_ref[...])
    along = (along[0:240, 0:128] + along[0:240, 128:256]) + along[240:480, 0:128]
    which = lax.div(lax.broadcasted_iota(jnp.int32, (40, 128), 1), 20)
    total = jnp.zeros((40, 128), f32)
    for c in range(6):
        total = total + jnp.where(which == c, along[40 * c : 40 * c + 40], 0.0)
    total = step_size * total
    if upper:
        out_ref[0:16] = total[0:16]
        out_ref[16:32] = total[16:32] + base_ref[...]
        out_ref[32:40] = total[32:40]
    else:
        out_ref[...] = total + base_ref[...]


def fold_kernel(mine_ref, core_ref, chip_ref, out_ref, one_ref, two_ref):
    lane = lax.broadcasted_iota(jnp.int32, (40, 128), 1)
    spot = lax.rem(lane, 20)
    live = lane < 120
    odd = (lax.axis_index("gz") & 1) == 1
    chip, core = chip_ref[...], core_ref[...]
    low = pltpu.roll(jnp.where(odd, core, chip), 112, 1)
    high = pltpu.roll(jnp.where(odd, chip, core), 16, 1)
    total = mine_ref[...]
    total = total + jnp.where(live & (spot < 3), low, 0.0)
    total = total + jnp.where(live & (spot >= 16), high, 0.0)
    out_ref[...] = total
    before, after = total[0:32], total[8:40]
    odd_x = (lax.axis_index("gx") & 1) == 1
    one_ref[...] = jnp.where(odd_x, before, after)
    two_ref[...] = jnp.where(odd_x, after, before)


def across_kernel(own_ref, one_ref, two_ref, far_ref, out_ref, mine_ref):
    odd = (lax.axis_index("gx") & 1) == 1
    tiles = lambda ref: [ref[8 * p : 8 * p + 8] for p in range(ref.shape[0] // 8)]
    own, one, two, far = tiles(own_ref), tiles(one_ref), tiles(two_ref), tiles(far_ref)
    below = [None] + [jnp.where(odd, a, b) for a, b in zip(one, two)]
    above = [jnp.where(odd, b, a) for a, b in zip(one, two)]
    window = [
        own[0] + below[2] + far[4],
        own[1] + below[3],
        own[2] + below[4] + above[0],
        own[3] + above[1],
        own[4] + above[2] + far[0],
        above[3] + far[1],
    ]
    for w in range(6):
        mine_ref[8 * w : 8 * w + 8] = window[w]
    low_half = lax.broadcasted_iota(jnp.int32, (8, 128), 0) < 4
    upper, lower = [], []
    for w in (0, 4):
        upper.append(jnp.where(low_half, pltpu.roll(window[w], 4, 0), window[w + 1]))
        lower.append(jnp.where(low_half, window[w], pltpu.roll(window[w + 1], 4, 0)))
    following = lax.rem(lax.axis_index("gy") + 1, 8)
    for n in range(8):
        out_ref[n, 0:8] = window[2]
        out_ref[n, 8:16] = window[3]
        for m in range(2):
            out_ref[n, 16 + 8 * m : 24 + 8 * m] = jnp.where(following == n, upper[m], lower[m])


def field_kernel(g_ref, mine_ref, wxy_ref, wz_ref, nv_ref, field_ref, rows_ref, buf_ref, own_ref, sems):
    me_i, me_j, me_k = coords()
    ni, nj, nk = (lax.axis_size(a) for a in AXES)
    row8 = lax.broadcasted_iota(jnp.int32, (8, 128), 0)

    window = []
    before, after = lax.rem(me_j + 7, 8), lax.rem(me_j + 1, 8)
    for w in range(6):
        at = 8 * (w - 2) if 2 <= w <= 3 else 16 + 8 * (w // 4)
        lows, highs = g_ref[before, at : at + 8], g_ref[after, at : at + 8]
        if w not in (0, 4):
            lows = pltpu.roll(lows, 4, 0)
        if w not in (1, 5):
            highs = pltpu.roll(highs, 4, 0)
        window.append(mine_ref[8 * w : 8 * w + 8] + jnp.where(row8 < 4, lows, highs))
    coefs = jnp.concatenate(window, axis=0)
    row = lax.broadcasted_iota(jnp.int32, (48, 128), 0)
    lane = lax.broadcasted_iota(jnp.int32, (48, 128), 1)
    at_x = 2 * me_i - 2 + lax.shift_right_logical(row, 3)
    at_y = 4 * me_j - 2 + (row & 7)
    at_z = 16 * me_k - 2 + lax.rem(lane, 20)
    real = (at_x >= 0) & (at_x < 2 * ni) & (at_y >= 0) & (at_y < 4 * nj)
    real = real & (at_z >= 0) & (at_z < 16 * nk) & (lane < 120)
    part = lax.div(lane, 20)
    coefs = jnp.where(real, coefs, 0.0)
    hi, lo = split2(jnp.concatenate([jnp.where(part == c, coefs, 0.0) for c in range(6)], axis=0))
    along = dot(jnp.concatenate([hi, lo], axis=0), wz_ref[...])
    along = (along[0:288, 0:128] + along[0:288, 128:256]) + along[288:576, 0:128]
    ch, cl = split2(along)
    copies = []
    for pair in range(3):
        rhs = []
        for c in (2 * pair, 2 * pair + 1):
            rows = slice(48 * c, 48 * c + 48)
            rhs.append(jnp.concatenate([ch[rows], cl[rows], ch[rows]], axis=0))
        both = dot(wxy_ref[...], jnp.concatenate(rhs, axis=1)).astype(bf16)
        for n in range(2):
            buf_ref[2 * pair + n] = both[:, 128 * n : 128 * n + 128]
        there = pl.ds(2 * pair, 2)
        copy = pltpu.make_async_copy(buf_ref.at[there], field_ref.at[there], sems.at[pair])
        copy.start()
        copies.append(copy)

    for side in range(2):
        cols = [g_ref[j, 8 * side : 8 * side + 8] for j in range(8)]
        turned = [pltpu.roll(c, 4, 0) for c in cols]
        tiles = []
        zero = jnp.zeros((8, 128), f32)
        for n in range(5):
            even = cols[2 * n] if n < 4 else zero
            high = turned[2 * n + 1] if n < 4 else zero
            low = turned[2 * n - 1] if n > 0 else zero
            tiles.append(even + jnp.where(row8 < 4, low, high))
        tiles[4] = tiles[4] + tiles[0]
        for n in range(5):
            rows_ref[side, 8 * n : 8 * n + 8] = tiles[n]
        block = jnp.transpose(rows_ref[side, 2:34])
        for c in range(6):
            own_ref[c, side] = block[20 * c + 2 : 20 * c + 18]
    copy = pltpu.make_async_copy(own_ref, nv_ref, sems.at[3])
    copy.start()
    copies.append(copy)
    for copy in copies:
        copy.wait()


VMEM = pl.BlockSpec(memory_space=pltpu.VMEM)


HBM = pl.BlockSpec(memory_space=pltpu.HBM)


def call(body, out_shape, in_specs, scratch=(), out_specs=None, flops=0, bytes_accessed=0):
    return pl.pallas_call(
        body,
        out_shape=[jax.ShapeDtypeStruct(shape, dtype) for shape, dtype in out_shape],
        in_specs=in_specs,
        out_specs=out_specs or [VMEM] * len(out_shape),
        scratch_shapes=list(scratch),
        compiler_params=pltpu.CompilerParams(vmem_limit_bytes=48 << 20),
        cost_estimate=pl.CostEstimate(flops=flops, bytes_accessed=bytes_accessed, transcendentals=0),
    )


def pairs(mesh_sizes, di, dj, dk):
    ni, nj, nk = mesh_sizes
    out = []
    for i in range(ni):
        for j in range(nj):
            for k in range(nk):
                to = (((i + di) % ni) * nj + (j + dj) % nj) * nk + (k + dk) % nk
                out.append(((i * nj + j) * nk + k, to))
    return out


def fixed_tables():
    weight = lambda n, points: spline((np.arange(n)[None, :] - 8.0 * (np.arange(points) - 2)[:, None] - 3.5) / 8.0)
    ex, ey, ez = (weight(n, points) for n, points in ((16, 6), (32, 8), (128, 20)))
    hi, lo = split_two(np.einsum("px,qy->xypq", ex, ey).reshape(512, 48))
    exy = np.concatenate([hi, hi, lo], axis=1)
    padded = lambda part: np.concatenate([np.tile(part, (6, 1)), np.zeros((8, 128), part.dtype)])
    return exy, np.concatenate([padded(part) for part in split_two(ez)], axis=1)


def shards(images, velocity):
    sizes = tuple(lax.axis_size(a) for a in AXES)
    nk = sizes[2]
    exy, ezs = fixed_tables()

    def send(v, di, dj, dk):
        return lax.ppermute(v, AXES, pairs(sizes, di, dj, dk))

    (pack,) = call(pack_kernel, [((2, 32, 128), f32)], [VMEM], bytes_accessed=6 * 10**5)(images)
    to_x, to_y, to_xy = call(
        slab_kernel,
        [((2, 8, 32, 128), f32), ((2, 16, 8, 128), f32), ((2, 9, 8, 128), f32)],
        [pl.BlockSpec(memory_space=pl.ANY), VMEM],
        bytes_accessed=10**6,
    )(pack, images)
    zr = lax.ppermute(pack, "gz", [(n, (n + 1) % nk) for n in range(nk)])
    yr = send(to_y, 0, 1, 0)
    xr = send(to_x, 1, 0, 0)

    velocity = jnp.swapaxes(velocity, 3, 4).reshape(6, 2, 16, 32)
    vel, wxy, wzs, xsum, zsum = call(
        prep_kernel,
        [((16, 128), f32), ((80, 512), bf16), ((128, 256), bf16), ((256, 128), bf16), ((256, 128), f32)],
        [VMEM],
        [pltpu.VMEM((128, 32), f32)],
        bytes_accessed=10**6,
    )(velocity)
    zr, vel = lax.optimization_barrier((zr, vel))
    top = zr[:, 24:]
    yzr = send(zr, 0, 1, 0)
    xyr = send(to_xy.at[:, 8].set(top), 1, 1, 0)
    xzr = send(zr, 1, 0, 0)

    def forces(upper, more, *arrays):
        return call(
            functools.partial(force_kernel, upper),
            [((40, 128), f32)] + [(shape, f32) for shape in more],
            [VMEM] * (len(arrays) + 4),
            [
                pltpu.VMEM((2, 16, 40, 128), f32),
                pltpu.VMEM((2, 2, 40, 128), f32),
                pltpu.VMEM((2, 10, 40, 128), f32),
                pltpu.VMEM((2, 8, 40, 128), f32),
                pltpu.VMEM((5, 8, 40, 128), f32),
                pltpu.VMEM((5, 3, 32, 128), bf16),
                pltpu.VMEM((6, 256, 128), bf16),
                pltpu.VMEM((6, 256, 128), bf16),
            ],
            flops=5 * 10**8,
            bytes_accessed=10**6,
        )(*arrays, wxy, wzs, xsum, zsum)

    shared = [(2, 5, 40, 128), (2, 4, 40, 128), (5, 8, 40, 128), (5, 32, 128)]
    part, *own_parts = forces(True, shared, images, zr, yr, yzr, vel)
    (part,) = forces(False, (), images, zr, yr, yzr, xr, xyr, xzr, part, *own_parts)

    swap = lambda v, axis, couples: lax.ppermute(v, axis, couples + [(b, a) for a, b in couples])
    chip = swap(part, "gz", [(1, 2), (3, 0)])
    core = swap(part, "gz", [(0, 1), (2, 3)])
    own, to_one, to_two = call(fold_kernel, [((40, 128), f32), ((32, 128), f32), ((32, 128), f32)], [VMEM] * 3)(part, core, chip)
    far = swap(own, "gx", [(0, 2), (1, 3)])
    one = swap(to_one, "gx", [(0, 1), (2, 3)])
    two = swap(to_two, "gx", [(1, 2), (3, 0)])
    copies, mine = call(across_kernel, [((8, 32, 128), f32), ((48, 128), f32)], [VMEM] * 4)(own, one, two, far)
    everything = lax.all_to_all(copies, "gy", 0, 0, tiled=True)

    nv, field = call(
        field_kernel,
        [((6, 2, 16, 32), f32), ((6, 512, 128), bf16)],
        [VMEM] * 4,
        [pltpu.VMEM((2, 40, 128), f32), pltpu.VMEM((6, 512, 128), bf16), pltpu.VMEM((6, 2, 16, 32), f32), pltpu.SemaphoreType.DMA((4,))],
        out_specs=[HBM, HBM],
        flops=10**8,
        bytes_accessed=10**6,
    )(everything, mine, exy, ezs)
    nv = jnp.swapaxes(nv.reshape(2, 3, 2, 16, 32), 3, 4)
    return nv, field.reshape(2, 3, 16, 32, 128)


def solution(mesh):
    placed = (P(None, "gx", "gy", "gz"), P(None, None, "gx", None, "gz"))
    return jax.shard_map(
        shards,
        mesh=mesh,
        in_specs=placed,
        out_specs=(P(None, None, "gx", None, "gz"), P(None, None, "gx", "gy", "gz")),
        check_vma=False,
    )
```
